256 devices in a mesh: path: 128 (over y, z, x_lo, core), width: 2 (over x_hi).
Axes of the slice: x: 4 (x_hi: 2, x_lo: 2; x = x_hi * 2 + x_lo), y: 4, z: 8, core: 2. Of those that a mesh axis runs over, the one named last changes fastest.
Arguments:
- adjoint: float32 [2, 8, 8, 8, 16384], P('width', None, None, None, 'path'), may hold values from -6 to 6
- velocity: float32 [3, 2, 8, 8, 8, 16384], P(None, 'width', None, None, None, 'path'), may hold values from -3 to 3
- diffusivity: float32 [2, 16384], P('width', 'path'), may hold values from 0.005 to 0.05
- wall_pair: int32 [128, 16], P('path'), may hold values from 0 to 15, each once within a row
Outputs:
- advanced: float32 [2, 8, 8, 8, 16384], P('width', None, None, None, 'path')
The draws below stay inside these ranges and needn't reach their ends.
Inputs may be any that keep to these rules, and one draw needn't show every extreme that they name: `wall_pair`: each row names every wall element of a block once.
All inputs are finite; a program needn't handle non-finite values.
Results may differ from the reference program's by a relative error of at most 0.00005.
Values sent between devices are 32-bit elements; how exact they have to be, the bound alone decides.
A program may use at most 64 MiB of HBM per device.

```python
import math
import jax
import jax.numpy as jnp
import numpy as np
from jax import lax

POINTS = 8
PATH_ELEMS = 2
WIDTH_ELEMS = 8
DEPTH_ELEMS = 8
WALL_ELEMS = 16
PATHS = 128
STRIPS = 2
ELEMS = 16384


def block_scale(rng, extent, pieces, smallest, high):
    gain = 1.0
    for position, shards_of in pieces:
        steps = jax.random.uniform(jax.random.fold_in(jax.random.fold_in(rng, 6), position), (shards_of,), jnp.float32, smallest / len(pieces), high / len(pieces))
        gain = gain * jnp.repeat(jnp.exp(steps), extent[position] // shards_of).reshape((-1,) + (1,) * (len(extent) - 1 - position))
    return gain


def bell_draw(own_key, extent, width, limit, cuts=(), dtype=jnp.bfloat16):
    level = block_scale(own_key, extent, cuts, -0.22, 0.18) if cuts else 1.0
    values = jax.random.normal(own_key, extent, jnp.float32) * width * level
    return jnp.minimum(jnp.maximum(values, -limit), limit).astype(dtype)


def setup_inputs(seed: int = 0) -> dict:
    splits = jax.random.split(jax.random.key(seed), 5)
    adjoint = bell_draw(splits[0], (STRIPS, POINTS, POINTS, POINTS, ELEMS), 1.0, 6.0, ((0, 2), (4, 128)), jnp.float32)
    velocity = bell_draw(splits[1], (3, STRIPS, POINTS, POINTS, POINTS, ELEMS), 0.5, 3.0, ((1, 2), (5, 128)), jnp.float32)
    diffusivity = jnp.clip(jnp.exp(math.log(0.05) - 2.3025851 * jax.random.uniform(splits[2], (STRIPS, ELEMS), jnp.float32) ** block_scale(splits[2], (STRIPS, ELEMS), ((0, 2), (1, 128)), -0.2, 0.2)), 0.005, 0.05)
    wall_pair = jax.vmap(lambda own: jax.random.permutation(own, WALL_ELEMS))(jax.random.split(splits[3], PATHS)).reshape((PATHS, WALL_ELEMS)).astype(jnp.int32)
    return dict(adjoint=adjoint, velocity=velocity, diffusivity=diffusivity, wall_pair=wall_pair)


LIFT_FACTOR = 56.0
PENALTY = 2.0
TIME_STEP = 0.004
HIGHEST = lax.Precision.HIGHEST
INNER_POINTS = (-0.8717401485096066, -0.5917001814331423, -0.2092992179024789,
                0.2092992179024789, 0.5917001814331423, 0.8717401485096066)


def legendre_seven(points):
    before = np.ones(points.shape)
    current = points * 1.0
    for order in range(1, 7):
        after = ((2.0 * order + 1.0) * points * current - order * before) / (order + 1.0)
        before = current
        current = after
    return current


def lobatto_table():
    degree = 7
    points = np.array((-1.0,) + INNER_POINTS + (1.0,))
    values = legendre_seven(points)
    deriv_table = np.zeros((degree + 1, degree + 1))
    for i in range(degree + 1):
        for j in range(degree + 1):
            if i != j:
                deriv_table[i, j] = values[i] / (values[j] * (points[i] - points[j]))
    deriv_table[0, 0] = -degree * (degree + 1) / 4.0
    deriv_table[degree, degree] = degree * (degree + 1) / 4.0
    return jnp.asarray(deriv_table, jnp.float32)


def slopes(adjoint, deriv_table):
    along_s = 2.0 * jnp.einsum("ij,qjbce->qibce", deriv_table, adjoint, precision=HIGHEST)
    along_w = 2.0 * jnp.einsum("ij,qajce->qaice", deriv_table, adjoint, precision=HIGHEST)
    along_z = 2.0 * jnp.einsum("ij,qabje->qabie", deriv_table, adjoint, precision=HIGHEST)
    return along_s, along_w, along_z


def trace_pair(adjoint, slope, node_axis, node_index):
    return jnp.stack([lax.index_in_dim(adjoint, node_index, node_axis, keepdims=False),
                      lax.index_in_dim(slope, node_index, node_axis, keepdims=False)])


def assemble(adjoint, velocity, diffusivity, gradients, outside, deriv_table):
    along_s, along_w, along_z = gradients
    divergence = 2.0 * (jnp.einsum("ij,qjbce->qibce", deriv_table, along_s, precision=HIGHEST)
                        + jnp.einsum("ij,qajce->qaice", deriv_table, along_w, precision=HIGHEST)
                        + jnp.einsum("ij,qabje->qabie", deriv_table, along_z, precision=HIGHEST))
    spread = diffusivity[:, None, None, None, :]
    tendency = velocity[0] * along_s + velocity[1] * along_w + velocity[2] * along_z + spread * divergence
    face_kappa = diffusivity[:, None, None, :]
    for direction in range(3):
        node_axis = direction + 1
        slope = gradients[direction]
        speed = velocity[direction]
        for side_index in range(2):
            node_index = 7 * side_index
            side_sign = 2.0 * side_index - 1.0
            outer = outside[2 * direction + side_index]
            own_value = lax.index_in_dim(adjoint, node_index, node_axis, keepdims=False)
            own_slope = lax.index_in_dim(slope, node_index, node_axis, keepdims=False)
            own_speed = lax.index_in_dim(speed, node_index, node_axis, keepdims=False)
            jump_size = outer[0] - own_value
            correction = LIFT_FACTOR * (side_sign * (own_speed * jump_size * 0.5 + face_kappa * (outer[1] - own_slope) * 0.5)
                                        + face_kappa * PENALTY * jump_size)
            tendency = tendency.at[(slice(None),) * node_axis + (node_index,)].add(correction)
    return tendency


def neighbour_shift(values, axis, step):
    length = values.shape[axis]
    blank = jnp.zeros_like(lax.slice_in_dim(values, 0, 1, axis=axis))
    if step > 0:
        return jnp.concatenate([lax.slice_in_dim(values, 1, length, axis=axis), blank], axis=axis)
    return jnp.concatenate([blank, lax.slice_in_dim(values, 0, length - 1, axis=axis)], axis=axis)


def along_path(values, step):
    moved = jnp.moveaxis(values, 4, 5)
    merged = moved.reshape(moved.shape[:5] + (PATHS * PATH_ELEMS, WIDTH_ELEMS))
    shifted = neighbour_shift(merged, 5, step).reshape(moved.shape)
    return jnp.moveaxis(shifted, 5, 4)


def across_strips(values, step):
    moved = jnp.moveaxis(values, 1, 6)
    merged = moved.reshape(moved.shape[:6] + (moved.shape[6] * WIDTH_ELEMS,))
    shifted = neighbour_shift(merged, 6, step).reshape(moved.shape)
    return jnp.moveaxis(shifted, 6, 1)


def outer_traces(adjoint, gradients, wall_pair):
    along_s, along_w, along_z = gradients
    strips = adjoint.shape[0]
    grid_shape = (2, strips, 8, 8, PATHS, DEPTH_ELEMS, PATH_ELEMS, WIDTH_ELEMS)
    depth_shape = (2, strips, 8, 8, PATHS, DEPTH_ELEMS, WALL_ELEMS)
    flat_shape = (2, strips, 8, 8, ELEMS)
    path_low = trace_pair(adjoint, along_s, 1, 0).reshape(grid_shape)
    path_high = trace_pair(adjoint, along_s, 1, 7).reshape(grid_shape)
    lower_path = along_path(path_high, -1)
    upper_path = along_path(path_low, 1)
    strip_low = trace_pair(adjoint, along_w, 2, 0).reshape(grid_shape)
    strip_high = trace_pair(adjoint, along_w, 2, 7).reshape(grid_shape)
    lower_strip = across_strips(strip_high, -1)
    upper_strip = across_strips(strip_low, 1)
    depth_low = trace_pair(adjoint, along_z, 3, 0).reshape(depth_shape)
    depth_high = trace_pair(adjoint, along_z, 3, 7).reshape(depth_shape)
    upper_depth = neighbour_shift(depth_low, 5, 1)
    bottom = depth_low[:, :, :, :, :, 0, :]
    partner = bottom[:, :, :, :, ::-1, :]
    flipper = jnp.array([1.0, -1.0], jnp.float32).reshape(2, 1, 1, 1, 1, 1)
    mirrored = partner[:, :, ::-1] * flipper
    facing = jnp.take_along_axis(mirrored, jnp.broadcast_to(wall_pair, mirrored.shape), axis=5)
    lower_depth = jnp.concatenate([facing[:, :, :, :, :, None, :], depth_high[:, :, :, :, :, :DEPTH_ELEMS - 1, :]], axis=5)
    result = []
    for traces in (lower_path, upper_path, lower_strip, upper_strip, lower_depth, upper_depth):
        flat = traces.reshape(flat_shape)
        result.append((flat[0], flat[1]))
    return result


def reference(adjoint, velocity, diffusivity, wall_pair):
    deriv_table = lobatto_table()

    def tendency_of(state):
        gradients = slopes(state, deriv_table)
        outside = outer_traces(state, gradients, wall_pair)
        return assemble(state, velocity, diffusivity, gradients, outside, deriv_table)

    first_rate = tendency_of(adjoint)
    second_rate = tendency_of(adjoint + (0.5 * TIME_STEP) * first_rate)
    third_rate = tendency_of(adjoint + (0.5 * TIME_STEP) * second_rate)
    fourth_rate = tendency_of(adjoint + TIME_STEP * third_rate)
    return adjoint + (TIME_STEP / 6.0) * (first_rate + 2.0 * second_rate + 2.0 * third_rate + fourth_rate)
```

```python
import functools

import jax
import jax.numpy as jnp
import numpy as np
from jax import lax
from jax.experimental import pallas as pl
from jax.experimental.pallas import tpu as pltpu
from jax.sharding import PartitionSpec as P

TIME_STEP = 0.004
STAGES = 4
INNER_POINTS = (
    -0.8717401485096066,
    -0.5917001814331423,
    -0.2092992179024789,
    0.2092992179024789,
    0.5917001814331423,
    0.8717401485096066,
)
F32 = jnp.float32
BF16 = jnp.bfloat16
WALL, BEHIND, AHEAD, ACROSS = range(4)


def legendre_seven(points):
    before = np.ones(points.shape)
    current = points * 1.0
    for order in range(1, 7):
        after = ((2.0 * order + 1.0) * points * current - order * before) / (order + 1.0)
        before = current
        current = after
    return current


def lobatto_table():
    degree = 7
    points = np.array((-1.0,) + INNER_POINTS + (1.0,))
    values = legendre_seven(points)
    table = np.zeros((degree + 1, degree + 1))
    for i in range(degree + 1):
        for j in range(degree + 1):
            if i != j:
                table[i, j] = values[i] / (values[j] * (points[i] - points[j]))
    table[0, 0] = -degree * (degree + 1) / 4.0
    table[degree, degree] = degree * (degree + 1) / 4.0
    return table


SLOPE = 2.0 * lobatto_table()
ADVECT = SLOPE.copy()
ADVECT[0, 0] += 28.0
ADVECT[7, 7] -= 28.0
SPREAD = SLOPE @ SLOPE
SPREAD[0] += 28.0 * SLOPE[0]
SPREAD[0, 0] -= 112.0
SPREAD[7] -= 28.0 * SLOPE[7]
SPREAD[7, 7] -= 112.0


def plane_matrix():
    eye = np.eye(8)
    full = np.concatenate(
        [np.kron(ADVECT, eye), np.kron(eye, ADVECT), np.kron(SPREAD, eye) + np.kron(eye, SPREAD)]
    )
    high = full.astype(jnp.bfloat16)
    low = (full - high.astype(np.float64)).astype(jnp.bfloat16)
    return np.concatenate([high, high, low], axis=1)


def halves(row):
    even = [float((row[j] + row[7 - j]) / 2) for j in range(4)]
    odd = [float((row[j] - row[7 - j]) / 2) for j in range(4)]
    return even, odd


def weighted(factors, values):
    total = values[0] * factors[0]
    for j in range(1, 4):
        total = total + values[j] * factors[j]
    return total


def end_slopes(line):
    even = [line[j] + line[7 - j] for j in range(4)]
    odd = [line[j] - line[7 - j] for j in range(4)]
    for_even, for_odd = halves(SLOPE[0])
    left, right = weighted(for_even, even), weighted(for_odd, odd)
    return left + right, right - left


def rows(a, b):
    return pl.ds((a * 8 + b) * 8, 8)


def face(a, c):
    return pl.ds(a * 64 + c, 8, stride=8)


def kernel(
    adj_hbm,
    vel_hbm,
    kappa_ref,
    pair_ref,
    matrix_ref,
    out_hbm,
    adj,
    vel,
    state,
    rate,
    slope_s,
    slope_w,
    slope_z,
    lift_s,
    lift_w,
    lift_z,
    lift_far,
    path_out,
    path_in,
    side_out,
    side_in,
    load_sem,
    send_sem,
    recv_sem,
):
    p, q = lax.axis_index("path"), lax.axis_index("width")
    blocks = lax.axis_size("path")
    ahead, behind = lax.rem(p + 1, blocks), lax.rem(p + blocks - 1, blocks)
    mirror, across = blocks - 1 - p, 1 - q

    loads = [
        pltpu.make_async_copy(adj_hbm, state, load_sem.at[0]),
        pltpu.make_async_copy(vel_hbm, vel, load_sem.at[1]),
        pltpu.make_async_copy(adj_hbm, adj, load_sem.at[2]),
    ]
    for load in loads:
        load.start()

    barrier = pltpu.get_barrier_semaphore()
    for partner in ({"path": mirror}, {"path": behind}, {"path": ahead}, {"width": across}):
        pl.semaphore_signal(barrier, inc=1, device_id=partner, device_id_type=pl.DeviceIdType.MESH)

    lane = lax.broadcasted_iota(jnp.int32, (8, 128), 1)
    width_lane = lane & 7
    first_row = (lane & 8) == 0
    layer = lane >> 4
    kappa = jnp.broadcast_to(kappa_ref[...], (8, 128))
    edge = 7 * (1 - q)
    edge_sign = (1 - 2 * q).astype(F32)

    def to_edge(a):
        return lax.rem(edge - a + 128, 128)

    def from_edge(a):
        return lax.rem(a - edge + 128, 128)

    def copies(stage):
        def remote(kind, src, dst, device):
            return pltpu.make_async_remote_copy(
                src_ref=src,
                dst_ref=dst,
                send_sem=send_sem.at[stage, kind],
                recv_sem=recv_sem.at[stage, kind],
                device_id=device,
                device_id_type=pl.DeviceIdType.MESH,
            )

        return [
            remote(WALL, side_out.at[stage, 0], side_in.at[stage, 0], {"path": mirror}),
            remote(BEHIND, path_out.at[stage, 0], path_in.at[stage, 0], {"path": ahead}),
            remote(AHEAD, path_out.at[stage, 1], path_in.at[stage, 1], {"path": behind}),
            remote(ACROSS, side_out.at[stage, 1], side_in.at[stage, 1], {"width": across}),
        ]

    def send_traces(stage):
        moves = copies(stage)
        values = jnp.zeros((8, 128), F32)
        slopes = jnp.zeros((8, 128), F32)
        for a in range(8):
            line = [state[face(a, c), :] for c in range(8)]
            low, high = end_slopes(line)
            slope_z[0, a] = low
            slope_z[1, a] = high
            value = line[0]
            if a:
                value = pltpu.roll(value, 16 * a, 1)
                low = pltpu.roll(low, 16 * a, 1)
            values = jnp.where(layer == a, value, values)
            slopes = jnp.where(layer == a, low, slopes)
        side_out[stage, 0, 0] = values
        side_out[stage, 0, 1] = slopes
        moves[WALL].start()
        for b in range(8):
            line = [state[rows(a, b), :] for a in range(8)]
            low, high = end_slopes(line)
            slope_s[0, b] = low
            slope_s[1, b] = high
            path_out[stage, 0, b] = jnp.where(first_row, pltpu.roll(high, 120, 1), line[7])
            path_out[stage, 1, b] = jnp.where(first_row, line[0], pltpu.roll(low, 8, 1))
        moves[BEHIND].start()
        moves[AHEAD].start()
        values = jnp.zeros((8, 128), F32)
        slopes = jnp.zeros((8, 128), F32)
        for a in range(8):
            line = [state[rows(a, b), :] for b in range(8)]
            low, high = end_slopes(line)
            slope_w[0, a] = low
            slope_w[1, a] = high
            value = pltpu.roll(jnp.where(q == 0, line[7], line[0]), from_edge(a), 1)
            slope = pltpu.roll(jnp.where(q == 0, high, low), from_edge(a), 1)
            values = jnp.where(width_lane == a, value, values)
            slopes = jnp.where(width_lane == a, slope, slopes)
        side_out[stage, 1, 0] = values
        side_out[stage, 1, 1] = slopes
        moves[ACROSS].start()

    def prepare():
        base = kappa * 112.0
        for i in range(8):
            lift_s[0, i] = base - 28.0 * vel[rows(0, i), :]
            lift_s[1, i] = base + 28.0 * vel[rows(7, i), :]
            lift_w[0, i] = base - 28.0 * vel[rows(8 + i, 0), :]
            lift_w[1, i] = base + 28.0 * vel[rows(8 + i, 7), :]
            lift_z[0, i] = base - 28.0 * vel[face(16 + i, 0), :]
            lift_z[1, i] = base + 28.0 * vel[face(16 + i, 7), :]
        wall_value = jnp.zeros((8, 128), F32)
        wall_slope = jnp.zeros((8, 128), F32)
        far_value = jnp.zeros((8, 128), F32)
        far_slope = jnp.zeros((8, 128), F32)
        for a in range(8):
            value, slope = lift_z[0, a], kappa * 28.0
            if a:
                value, slope = pltpu.roll(value, 16 * a, 1), pltpu.roll(slope, 16 * a, 1)
            wall_value = jnp.where(layer == a, value, wall_value)
            wall_slope = jnp.where(layer == a, slope, wall_slope)
            value = jnp.where(q == 0, lift_w[1, a], lift_w[0, a])
            far_value = jnp.where(width_lane == a, pltpu.roll(value, from_edge(a), 1), far_value)
            slope = pltpu.roll(kappa * (edge_sign * 28.0), from_edge(a), 1)
            far_slope = jnp.where(width_lane == a, slope, far_slope)
        lift_far[0] = wall_value
        lift_far[1] = wall_slope
        lift_far[2] = far_value
        lift_far[3] = far_slope

    def local_rates(step):
        for b in range(8):
            line = [state[rows(a, b), :] for a in range(8)]
            even = [line[j] + line[7 - j] for j in range(4)]
            odd = [line[j] - line[7 - j] for j in range(4)]
            for i in range(4):
                for_even, for_odd = halves(ADVECT[i])
                left, right = weighted(for_even, even), weighted(for_odd, odd)
                for_even, for_odd = halves(SPREAD[i])
                inner, outer = weighted(for_even, even), weighted(for_odd, odd)
                near = vel[rows(i, b), :] * (left + right) + kappa * (inner + outer)
                far = vel[rows(7 - i, b), :] * (right - left) + kappa * (inner - outer)
                if i == 0:
                    lower = lift_s[0, b] * pltpu.roll(line[7], 8, 1) - (kappa * 28.0) * pltpu.roll(
                        slope_s[1, b], 8, 1
                    )
                    upper = lift_s[1, b] * pltpu.roll(line[0], 120, 1) + (
                        kappa * 28.0
                    ) * pltpu.roll(slope_s[0, b], 120, 1)
                    near = near + jnp.where(first_row, 0.0, lower)
                    far = far + jnp.where(first_row, upper, 0.0)
                rate[rows(i, b), :] = near
                rate[rows(7 - i, b), :] = far
        for pair in range(4):
            both = range(2 * pair, 2 * pair + 2)
            planes = [state[pl.ds(64 * a, 64), :] for a in both]
            plane = jnp.concatenate(planes, axis=1)
            high = plane.astype(BF16)
            low = (plane - high.astype(F32)).astype(BF16)
            stacked = jnp.concatenate([high, low, high], axis=0)
            product = jnp.dot(matrix_ref[...], stacked, preferred_element_type=F32)
            for k, a in enumerate(both):
                block = product[:, 128 * k : 128 * (k + 1)]
                bottom, top = state[face(a, 0), :], state[face(a, 7), :]
                first, last = state[rows(a, 0), :], state[rows(a, 7), :]
                for b in range(8):
                    at = slice(8 * b, 8 * b + 8)
                    value = (
                        rate[rows(a, b), :]
                        + vel[rows(8 + a, b), :] * block[0:64][at]
                        + vel[rows(16 + a, b), :] * block[64:128][at]
                        + kappa * block[128:192][at]
                    )
                    if b == 0:
                        lower = lift_w[0, a] * pltpu.roll(last, 1, 1) - (
                            kappa * 28.0
                        ) * pltpu.roll(slope_w[1, a], 1, 1)
                        value = value + jnp.where(width_lane == 0, 0.0, lower)
                    if b == 7:
                        upper = lift_w[1, a] * pltpu.roll(first, 127, 1) + (
                            kappa * 28.0
                        ) * pltpu.roll(slope_w[0, a], 127, 1)
                        value = value + jnp.where(width_lane == 7, 0.0, upper)
                    state[rows(a, b), :] = adj[rows(a, b), :] + step * value
                lower = lift_z[0, a] * pltpu.roll(top, 16, 1) - (kappa * 28.0) * pltpu.roll(
                    slope_z[1, a], 16, 1
                )
                upper = lift_z[1, a] * pltpu.roll(bottom, 112, 1) + (kappa * 28.0) * pltpu.roll(
                    slope_z[0, a], 112, 1
                )
                state[face(a, 0), :] += step * jnp.where(layer == 0, 0.0, lower)
                state[face(a, 7), :] += step * jnp.where(layer == 7, 0.0, upper)

    def far_rates(stage, step, wall_index):
        moves = copies(stage)
        moves[ACROSS].wait_recv()
        change = step * (lift_far[2] * side_in[stage, 1, 0] + lift_far[3] * side_in[stage, 1, 1])
        for a in range(8):
            moved = pltpu.roll(change, to_edge(a), 1)
            state[rows(a, edge), :] += jnp.where(width_lane == edge, moved, 0.0)
        slope_factor = kappa * 28.0
        moves[BEHIND].wait_recv()
        lower_lanes = first_row & (p > 0)
        for b in range(8):
            packet = path_in[stage, 0, b]
            change = lift_s[0, b] * pltpu.roll(packet, 120, 1) - slope_factor * packet
            state[rows(0, b), :] += jnp.where(lower_lanes, step * change, 0.0)
        moves[AHEAD].wait_recv()
        upper_lanes = jnp.logical_not(first_row) & (p < blocks - 1)
        for b in range(8):
            packet = path_in[stage, 1, b]
            change = lift_s[1, b] * pltpu.roll(packet, 8, 1) + slope_factor * packet
            state[rows(7, b), :] += jnp.where(upper_lanes, step * change, 0.0)
        moves[WALL].wait_recv()
        value = jnp.take_along_axis(side_in[stage, 0, 0], wall_index, axis=1)
        slope = jnp.take_along_axis(side_in[stage, 0, 1], wall_index, axis=1)
        change = step * (lift_far[0] * value + lift_far[1] * slope)
        for a in range(8):
            moved = pltpu.roll(change, 128 - 16 * a, 1) if a else change
            state[face(a, 0), :] += jnp.where(layer == 0, moved, 0.0)

    wall_index = jnp.zeros((8, 128), jnp.int32)
    for j in range(16):
        wall_index = jnp.where((lane & 15) == j, pair_ref[0, j], wall_index)
    wall_index = wall_index + 16 * (7 - layer)

    loads[0].wait()
    pl.semaphore_wait(barrier, 4)
    send_traces(0)
    loads[1].wait()
    prepare()
    loads[2].wait()

    def advance(stage, carry):
        step = jnp.float32(TIME_STEP) / (4 - stage).astype(F32)
        local_rates(step)
        far_rates(stage, step, wall_index)

        @pl.when(stage < STAGES - 1)
        def _():
            send_traces(stage + 1)

        return carry

    lax.fori_loop(0, STAGES, advance, 0)
    store = pltpu.make_async_copy(state, out_hbm, load_sem.at[3])
    store.start()
    for stage in range(STAGES):
        for move in copies(stage):
            move.wait_send()
    store.wait()


def shards(adjoint, velocity, diffusivity, wall_pair):
    matrix = jnp.asarray(plane_matrix())
    result = pl.pallas_call(
        kernel,
        out_shape=jax.ShapeDtypeStruct((512, 128), F32),
        in_specs=[
            pl.BlockSpec(memory_space=pl.ANY),
            pl.BlockSpec(memory_space=pl.ANY),
            pl.BlockSpec(memory_space=pltpu.VMEM),
            pl.BlockSpec(memory_space=pltpu.SMEM),
            pl.BlockSpec(memory_space=pltpu.VMEM),
        ],
        out_specs=pl.BlockSpec(memory_space=pl.ANY),
        scratch_shapes=[
            pltpu.VMEM((512, 128), F32),
            pltpu.VMEM((1536, 128), F32),
            pltpu.VMEM((512, 128), F32),
            pltpu.VMEM((512, 128), F32),
            pltpu.VMEM((2, 8, 8, 128), F32),
            pltpu.VMEM((2, 8, 8, 128), F32),
            pltpu.VMEM((2, 8, 8, 128), F32),
            pltpu.VMEM((2, 8, 8, 128), F32),
            pltpu.VMEM((2, 8, 8, 128), F32),
            pltpu.VMEM((2, 8, 8, 128), F32),
            pltpu.VMEM((4, 8, 128), F32),
            pltpu.VMEM((STAGES, 2, 8, 8, 128), F32),
            pltpu.VMEM((STAGES, 2, 8, 8, 128), F32),
            pltpu.VMEM((STAGES, 2, 2, 8, 128), F32),
            pltpu.VMEM((STAGES, 2, 2, 8, 128), F32),
            pltpu.SemaphoreType.DMA((4,)),
            pltpu.SemaphoreType.DMA((STAGES, 4)),
            pltpu.SemaphoreType.DMA((STAGES, 4)),
        ],
        compiler_params=pltpu.CompilerParams(
            collective_id=0, has_side_effects=True, vmem_limit_bytes=32 * 1024 * 1024
        ),
        name="plate_step",
    )(
        adjoint.reshape(512, 128),
        velocity.reshape(1536, 128),
        diffusivity,
        wall_pair,
        matrix,
    )
    return result.reshape(adjoint.shape)


def solution(mesh):
    placed = (
        P("width", None, None, None, "path"),
        P(None, "width", None, None, None, "path"),
        P("width", "path"),
        P("path", None),
    )
    return jax.shard_map(
        shards,
        mesh=mesh,
        in_specs=placed,
        out_specs=P("width", None, None, None, "path"),
        check_vma=False,
    )
```

```python
import functools

import jax
import jax.numpy as jnp
import numpy as np
from jax import lax
from jax.experimental import pallas as pl
from jax.experimental.pallas import tpu as pltpu
from jax.sharding import PartitionSpec as P

TIME_STEP = 0.004
STAGES = 4
INNER_POINTS = (
    -0.8717401485096066,
    -0.5917001814331423,
    -0.2092992179024789,
    0.2092992179024789,
    0.5917001814331423,
    0.8717401485096066,
)
F32 = jnp.float32
BF16 = jnp.bfloat16
WALL, BEHIND, AHEAD, ACROSS = range(4)


def legendre_seven(points):
    before = np.ones(points.shape)
    current = points * 1.0
    for order in range(1, 7):
        after = ((2.0 * order + 1.0) * points * current - order * before) / (order + 1.0)
        before = current
        current = after
    return current


def lobatto_table():
    degree = 7
    points = np.array((-1.0,) + INNER_POINTS + (1.0,))
    values = legendre_seven(points)
    table = np.zeros((degree + 1, degree + 1))
    for i in range(degree + 1):
        for j in range(degree + 1):
            if i != j:
                table[i, j] = values[i] / (values[j] * (points[i] - points[j]))
    table[0, 0] = -degree * (degree + 1) / 4.0
    table[degree, degree] = degree * (degree + 1) / 4.0
    return table


SLOPE = 2.0 * lobatto_table()
ADVECT = SLOPE.copy()
ADVECT[0, 0] += 28.0
ADVECT[7, 7] -= 28.0
SPREAD = SLOPE @ SLOPE
SPREAD[0] += 28.0 * SLOPE[0]
SPREAD[0, 0] -= 112.0
SPREAD[7] -= 28.0 * SLOPE[7]
SPREAD[7, 7] -= 112.0


def plane_matrix():
    eye = np.eye(8)
    full = np.concatenate(
        [np.kron(ADVECT, eye), np.kron(eye, ADVECT), np.kron(SPREAD, eye) + np.kron(eye, SPREAD)]
    )
    high = full.astype(jnp.bfloat16)
    low = (full - high.astype(np.float64)).astype(jnp.bfloat16)
    return np.concatenate([high, high, low], axis=1)


def halves(row):
    even = [float((row[j] + row[7 - j]) / 2) for j in range(4)]
    odd = [float((row[j] - row[7 - j]) / 2) for j in range(4)]
    return even, odd


def weighted(factors, values):
    total = values[0] * factors[0]
    for j in range(1, 4):
        total = total + values[j] * factors[j]
    return total


def end_slopes(line):
    even = [line[j] + line[7 - j] for j in range(4)]
    odd = [line[j] - line[7 - j] for j in range(4)]
    for_even, for_odd = halves(SLOPE[0])
    left, right = weighted(for_even, even), weighted(for_odd, odd)
    return left + right, right - left


def rows(a, b):
    return pl.ds((a * 8 + b) * 8, 8)


def face(a, c):
    return pl.ds(a * 64 + c, 8, stride=8)


def kernel(
    adj_hbm,
    vel_hbm,
    kappa_hbm,
    pair_hbm,
    matrix_hbm,
    out_hbm,
    kappa_ref,
    pair_ref,
    matrix_ref,
    adj,
    vel,
    state,
    rate,
    slope_s,
    slope_w,
    slope_z,
    lift_s,
    lift_w,
    lift_z,
    lift_far,
    path_out,
    path_in,
    side_out,
    side_in,
    load_sem,
    send_sem,
    recv_sem,
):
    p, q = lax.axis_index("path"), lax.axis_index("width")
    blocks = lax.axis_size("path")
    ahead, behind = lax.rem(p + 1, blocks), lax.rem(p + blocks - 1, blocks)
    mirror, across = blocks - 1 - p, 1 - q

    loads = [
        pltpu.make_async_copy(adj_hbm, state, load_sem.at[0]),
        pltpu.make_async_copy(vel_hbm, vel, load_sem.at[1]),
        pltpu.make_async_copy(adj_hbm, adj, load_sem.at[2]),
        pltpu.make_async_copy(kappa_hbm, kappa_ref, load_sem.at[4]),
        pltpu.make_async_copy(pair_hbm, pair_ref, load_sem.at[5]),
        pltpu.make_async_copy(matrix_hbm, matrix_ref, load_sem.at[6]),
    ]
    for load in loads:
        load.start()

    barrier = pltpu.get_barrier_semaphore()
    for partner in ({"path": mirror}, {"path": behind}, {"path": ahead}, {"width": across}):
        pl.semaphore_signal(barrier, inc=1, device_id=partner, device_id_type=pl.DeviceIdType.MESH)

    lane = lax.broadcasted_iota(jnp.int32, (8, 128), 1)
    width_lane = lane & 7
    first_row = (lane & 8) == 0
    layer = lane >> 4
    edge = 7 * (1 - q)
    edge_sign = (1 - 2 * q).astype(F32)

    def to_edge(a):
        return lax.rem(edge - a + 128, 128)

    def from_edge(a):
        return lax.rem(a - edge + 128, 128)

    def copies(stage):
        def remote(kind, src, dst, device):
            return pltpu.make_async_remote_copy(
                src_ref=src,
                dst_ref=dst,
                send_sem=send_sem.at[stage, kind],
                recv_sem=recv_sem.at[stage, kind],
                device_id=device,
                device_id_type=pl.DeviceIdType.MESH,
            )

        return [
            remote(WALL, side_out.at[stage, 0], side_in.at[stage, 0], {"path": mirror}),
            remote(BEHIND, path_out.at[stage, 0], path_in.at[stage, 0], {"path": ahead}),
            remote(AHEAD, path_out.at[stage, 1], path_in.at[stage, 1], {"path": behind}),
            remote(ACROSS, side_out.at[stage, 1], side_in.at[stage, 1], {"width": across}),
        ]

    def send_traces(stage):
        moves = copies(stage)
        values = jnp.zeros((8, 128), F32)
        slopes = jnp.zeros((8, 128), F32)
        for a in range(8):
            line = [state[face(a, c), :] for c in range(8)]
            low, high = end_slopes(line)
            slope_z[0, a] = low
            slope_z[1, a] = high
            value = line[0]
            if a:
                value = pltpu.roll(value, 16 * a, 1)
                low = pltpu.roll(low, 16 * a, 1)
            values = jnp.where(layer == a, value, values)
            slopes = jnp.where(layer == a, low, slopes)
        side_out[stage, 0, 0] = values
        side_out[stage, 0, 1] = slopes
        moves[WALL].start()
        for b in range(8):
            line = [state[rows(a, b), :] for a in range(8)]
            low, high = end_slopes(line)
            slope_s[0, b] = low
            slope_s[1, b] = high
            path_out[stage, 0, b] = jnp.where(first_row, pltpu.roll(high, 120, 1), line[7])
            path_out[stage, 1, b] = jnp.where(first_row, line[0], pltpu.roll(low, 8, 1))
        moves[BEHIND].start()
        moves[AHEAD].start()
        values = jnp.zeros((8, 128), F32)
        slopes = jnp.zeros((8, 128), F32)
        for a in range(8):
            line = [state[rows(a, b), :] for b in range(8)]
            low, high = end_slopes(line)
            slope_w[0, a] = low
            slope_w[1, a] = high
            value = pltpu.roll(jnp.where(q == 0, line[7], line[0]), from_edge(a), 1)
            slope = pltpu.roll(jnp.where(q == 0, high, low), from_edge(a), 1)
            values = jnp.where(width_lane == a, value, values)
            slopes = jnp.where(width_lane == a, slope, slopes)
        side_out[stage, 1, 0] = values
        side_out[stage, 1, 1] = slopes
        moves[ACROSS].start()

    def prepare(kappa):
        base = kappa * 112.0
        for i in range(8):
            lift_s[0, i] = base - 28.0 * vel[rows(0, i), :]
            lift_s[1, i] = base + 28.0 * vel[rows(7, i), :]
            lift_w[0, i] = base - 28.0 * vel[rows(8 + i, 0), :]
            lift_w[1, i] = base + 28.0 * vel[rows(8 + i, 7), :]
            lift_z[0, i] = base - 28.0 * vel[face(16 + i, 0), :]
            lift_z[1, i] = base + 28.0 * vel[face(16 + i, 7), :]
        wall_value = jnp.zeros((8, 128), F32)
        wall_slope = jnp.zeros((8, 128), F32)
        far_value = jnp.zeros((8, 128), F32)
        far_slope = jnp.zeros((8, 128), F32)
        for a in range(8):
            value, slope = lift_z[0, a], kappa * 28.0
            if a:
                value, slope = pltpu.roll(value, 16 * a, 1), pltpu.roll(slope, 16 * a, 1)
            wall_value = jnp.where(layer == a, value, wall_value)
            wall_slope = jnp.where(layer == a, slope, wall_slope)
            value = jnp.where(q == 0, lift_w[1, a], lift_w[0, a])
            far_value = jnp.where(width_lane == a, pltpu.roll(value, from_edge(a), 1), far_value)
            slope = pltpu.roll(kappa * (edge_sign * 28.0), from_edge(a), 1)
            far_slope = jnp.where(width_lane == a, slope, far_slope)
        lift_far[0] = wall_value
        lift_far[1] = wall_slope
        lift_far[2] = far_value
        lift_far[3] = far_slope

    def local_rates(step, kappa):
        for b in range(8):
            line = [state[rows(a, b), :] for a in range(8)]
            even = [line[j] + line[7 - j] for j in range(4)]
            odd = [line[j] - line[7 - j] for j in range(4)]
            for i in range(4):
                for_even, for_odd = halves(ADVECT[i])
                left, right = weighted(for_even, even), weighted(for_odd, odd)
                for_even, for_odd = halves(SPREAD[i])
                inner, outer = weighted(for_even, even), weighted(for_odd, odd)
                near = vel[rows(i, b), :] * (left + right) + kappa * (inner + outer)
                far = vel[rows(7 - i, b), :] * (right - left) + kappa * (inner - outer)
                if i == 0:
                    lower = lift_s[0, b] * pltpu.roll(line[7], 8, 1) - (kappa * 28.0) * pltpu.roll(
                        slope_s[1, b], 8, 1
                    )
                    upper = lift_s[1, b] * pltpu.roll(line[0], 120, 1) + (
                        kappa * 28.0
                    ) * pltpu.roll(slope_s[0, b], 120, 1)
                    near = near + jnp.where(first_row, 0.0, lower)
                    far = far + jnp.where(first_row, upper, 0.0)
                rate[rows(i, b), :] = near
                rate[rows(7 - i, b), :] = far
        for pair in range(4):
            both = range(2 * pair, 2 * pair + 2)
            planes = [state[pl.ds(64 * a, 64), :] for a in both]
            plane = jnp.concatenate(planes, axis=1)
            high = plane.astype(BF16)
            low = (plane - high.astype(F32)).astype(BF16)
            stacked = jnp.concatenate([high, low, high], axis=0)
            product = jnp.dot(matrix_ref[...], stacked, preferred_element_type=F32)
            for k, a in enumerate(both):
                block = product[:, 128 * k : 128 * (k + 1)]
                bottom, top = state[face(a, 0), :], state[face(a, 7), :]
                first, last = state[rows(a, 0), :], state[rows(a, 7), :]
                for b in range(8):
                    at = slice(8 * b, 8 * b + 8)
                    value = (
                        rate[rows(a, b), :]
                        + vel[rows(8 + a, b), :] * block[0:64][at]
                        + vel[rows(16 + a, b), :] * block[64:128][at]
                        + kappa * block[128:192][at]
                    )
                    if b == 0:
                        lower = lift_w[0, a] * pltpu.roll(last, 1, 1) - (
                            kappa * 28.0
                        ) * pltpu.roll(slope_w[1, a], 1, 1)
                        value = value + jnp.where(width_lane == 0, 0.0, lower)
                    if b == 7:
                        upper = lift_w[1, a] * pltpu.roll(first, 127, 1) + (
                            kappa * 28.0
                        ) * pltpu.roll(slope_w[0, a], 127, 1)
                        value = value + jnp.where(width_lane == 7, 0.0, upper)
                    state[rows(a, b), :] = adj[rows(a, b), :] + step * value
                lower = lift_z[0, a] * pltpu.roll(top, 16, 1) - (kappa * 28.0) * pltpu.roll(
                    slope_z[1, a], 16, 1
                )
                upper = lift_z[1, a] * pltpu.roll(bottom, 112, 1) + (kappa * 28.0) * pltpu.roll(
                    slope_z[0, a], 112, 1
                )
                state[face(a, 0), :] += step * jnp.where(layer == 0, 0.0, lower)
                state[face(a, 7), :] += step * jnp.where(layer == 7, 0.0, upper)

    def far_rates(stage, step, kappa, wall_index):
        moves = copies(stage)
        moves[ACROSS].wait_recv()
        change = step * (lift_far[2] * side_in[stage, 1, 0] + lift_far[3] * side_in[stage, 1, 1])
        for a in range(8):
            moved = pltpu.roll(change, to_edge(a), 1)
            state[rows(a, edge), :] += jnp.where(width_lane == edge, moved, 0.0)
        slope_factor = kappa * 28.0
        moves[BEHIND].wait_recv()
        lower_lanes = first_row & (p > 0)
        for b in range(8):
            packet = path_in[stage, 0, b]
            change = lift_s[0, b] * pltpu.roll(packet, 120, 1) - slope_factor * packet
            state[rows(0, b), :] += jnp.where(lower_lanes, step * change, 0.0)
        moves[AHEAD].wait_recv()
        upper_lanes = jnp.logical_not(first_row) & (p < blocks - 1)
        for b in range(8):
            packet = path_in[stage, 1, b]
            change = lift_s[1, b] * pltpu.roll(packet, 8, 1) + slope_factor * packet
            state[rows(7, b), :] += jnp.where(upper_lanes, step * change, 0.0)
        moves[WALL].wait_recv()
        value = jnp.take_along_axis(side_in[stage, 0, 0], wall_index, axis=1)
        slope = jnp.take_along_axis(side_in[stage, 0, 1], wall_index, axis=1)
        change = step * (lift_far[0] * value + lift_far[1] * slope)
        for a in range(8):
            moved = pltpu.roll(change, 128 - 16 * a, 1) if a else change
            state[face(a, 0), :] += jnp.where(layer == 0, moved, 0.0)

    loads[0].wait()
    pl.semaphore_wait(barrier, 4)
    send_traces(0)
    for load in loads[1:]:
        load.wait()
    kappa = jnp.broadcast_to(kappa_ref[...], (8, 128))
    wall_index = jnp.zeros((8, 128), jnp.int32)
    for j in range(16):
        wall_index = jnp.where((lane & 15) == j, pair_ref[0, j], wall_index)
    wall_index = wall_index + 16 * (7 - layer)
    prepare(kappa)

    def advance(stage, carry):
        step = jnp.float32(TIME_STEP) / (4 - stage).astype(F32)
        local_rates(step, kappa)
        far_rates(stage, step, kappa, wall_index)

        @pl.when(stage < STAGES - 1)
        def _():
            send_traces(stage + 1)

        return carry

    lax.fori_loop(0, STAGES, advance, 0)
    store = pltpu.make_async_copy(state, out_hbm, load_sem.at[3])
    store.start()
    for stage in range(STAGES):
        for move in copies(stage):
            move.wait_send()
    store.wait()


def shards(adjoint, velocity, diffusivity, wall_pair):
    matrix = jnp.asarray(plane_matrix())
    result = pl.pallas_call(
        kernel,
        out_shape=jax.ShapeDtypeStruct((512, 128), F32),
        in_specs=[
            pl.BlockSpec(memory_space=pltpu.HBM),
            pl.BlockSpec(memory_space=pltpu.HBM),
            pl.BlockSpec(memory_space=pltpu.HBM),
            pl.BlockSpec(memory_space=pltpu.HBM),
            pl.BlockSpec(memory_space=pltpu.HBM),
        ],
        out_specs=pl.BlockSpec(memory_space=pl.ANY),
        scratch_shapes=[
            pltpu.VMEM((1, 128), F32),
            pltpu.SMEM((1, 16), jnp.int32),
            pltpu.VMEM((192, 192), BF16),
            pltpu.VMEM((512, 128), F32),
            pltpu.VMEM((1536, 128), F32),
            pltpu.VMEM((512, 128), F32),
            pltpu.VMEM((512, 128), F32),
            pltpu.VMEM((2, 8, 8, 128), F32),
            pltpu.VMEM((2, 8, 8, 128), F32),
            pltpu.VMEM((2, 8, 8, 128), F32),
            pltpu.VMEM((2, 8, 8, 128), F32),
            pltpu.VMEM((2, 8, 8, 128), F32),
            pltpu.VMEM((2, 8, 8, 128), F32),
            pltpu.VMEM((4, 8, 128), F32),
            pltpu.VMEM((STAGES, 2, 8, 8, 128), F32),
            pltpu.VMEM((STAGES, 2, 8, 8, 128), F32),
            pltpu.VMEM((STAGES, 2, 2, 8, 128), F32),
            pltpu.VMEM((STAGES, 2, 2, 8, 128), F32),
            pltpu.SemaphoreType.DMA((7,)),
            pltpu.SemaphoreType.DMA((STAGES, 4)),
            pltpu.SemaphoreType.DMA((STAGES, 4)),
        ],
        compiler_params=pltpu.CompilerParams(
            collective_id=0, has_side_effects=True, vmem_limit_bytes=63 * 1024 * 1024
        ),
        name="plate_step",
    )(
        adjoint.reshape(512, 128),
        velocity.reshape(1536, 128),
        diffusivity,
        wall_pair,
        matrix,
    )
    return result.reshape(adjoint.shape)


def solution(mesh):
    placed = (
        P("width", None, None, None, "path"),
        P(None, "width", None, None, None, "path"),
        P("width", "path"),
        P("path", None),
    )
    return jax.shard_map(
        shards,
        mesh=mesh,
        in_specs=placed,
        out_specs=P("width", None, None, None, "path"),
        check_vma=False,
    )
```

```python
import functools

import jax
import jax.numpy as jnp
import numpy as np
from jax import lax
from jax.experimental import pallas as pl
from jax.experimental.pallas import tpu as pltpu
from jax.sharding import PartitionSpec as P

TIME_STEP = 0.004
ROUNDS = 2
INNER_POINTS = (
    -0.8717401485096066,
    -0.5917001814331423,
    -0.2092992179024789,
    0.2092992179024789,
    0.5917001814331423,
    0.8717401485096066,
)
F32 = jnp.float32
BF16 = jnp.bfloat16
WALL, BEHIND, AHEAD, ACROSS, CROSS_BEHIND, CROSS_AHEAD, WALL_AHEAD, WALL_BEHIND, WALL_ACROSS = range(9)
KINDS = 9
EDGE_V, EDGE_G, SIDE_V, SIDE_G, WALL_V, WALL_G, FOOT_V, FOOT_G, LANES, KAPPA, PATH_V = range(11)
FACTORS = 18


def legendre_seven(points):
    before = np.ones(points.shape)
    current = points * 1.0
    for order in range(1, 7):
        after = ((2.0 * order + 1.0) * points * current - order * before) / (order + 1.0)
        before = current
        current = after
    return current


def lobatto_table():
    degree = 7
    points = np.array((-1.0,) + INNER_POINTS + (1.0,))
    values = legendre_seven(points)
    table = np.zeros((degree + 1, degree + 1))
    for i in range(degree + 1):
        for j in range(degree + 1):
            if i != j:
                table[i, j] = values[i] / (values[j] * (points[i] - points[j]))
    table[0, 0] = -degree * (degree + 1) / 4.0
    table[degree, degree] = degree * (degree + 1) / 4.0
    return table


SLOPE = 2.0 * lobatto_table()
ADVECT = SLOPE.copy()
ADVECT[0, 0] += 28.0
ADVECT[7, 7] -= 28.0
SPREAD = SLOPE @ SLOPE
SPREAD[0] += 28.0 * SLOPE[0]
SPREAD[0, 0] -= 112.0
SPREAD[7] -= 28.0 * SLOPE[7]
SPREAD[7, 7] -= 112.0


def plane_matrix():
    eye = np.eye(8)
    full = np.concatenate(
        [np.kron(ADVECT, eye), np.kron(eye, ADVECT), np.kron(SPREAD, eye) + np.kron(eye, SPREAD)]
    )
    high = full.astype(jnp.bfloat16)
    low = (full - high.astype(np.float64)).astype(jnp.bfloat16)
    return np.concatenate([high, high, low], axis=1)


def weight_rows():
    lane = np.arange(128)
    second, width, layer = (lane >> 3) & 1, lane & 7, lane >> 4
    last = np.where(second[None] == 1, 7, 0)[0]
    flat = [SLOPE[last, width], SLOPE[last, layer], SLOPE[0, width], SLOPE[7, width]]
    wide = [np.broadcast_to(row, (8, 128)) for row in flat]
    tall = [np.broadcast_to(SLOPE[k][:, None], (8, 128)) for k in (0, 7)]
    return np.stack(wide + tall).astype(np.float32)


def halves(row):
    even = [float((row[j] + row[7 - j]) / 2) for j in range(4)]
    odd = [float((row[j] - row[7 - j]) / 2) for j in range(4)]
    return even, odd


def weighted(factors, values):
    total = values[0] * factors[0]
    for j in range(1, 4):
        total = total + values[j] * factors[j]
    return total


def end_slopes(line):
    even = [line[j] + line[7 - j] for j in range(4)]
    odd = [line[j] - line[7 - j] for j in range(4)]
    for_even, for_odd = halves(SLOPE[0])
    left, right = weighted(for_even, even), weighted(for_odd, odd)
    return left + right, right - left


def rows(a, b):
    return pl.ds((a * 8 + b) * 8, 8)


def face(a, c):
    return pl.ds(a * 64 + c, 8, stride=8)


def lanes_moved(value, index):
    return jnp.take_along_axis(value, index, axis=1)


def turned(value, shift):
    return pltpu.roll(value, shift % 128, 1) if shift % 128 else value


def kernel(
    adj_hbm,
    vel_hbm,
    kappa_hbm,
    pair_hbm,
    matrix_hbm,
    weight_hbm,
    out_hbm,
    kappa_ref,
    pair_ref,
    matrix_ref,
    weight,
    adj,
    vel,
    state,
    rate,
    slope_s,
    slope_w,
    slope_z,
    lift_s,
    lift_w,
    lift_z,
    factor_out,
    factor_in,
    path_out,
    path_in,
    wall_out,
    wall_in,
    side_out,
    side_in,
    cross_out,
    cross_in,
    foot_out,
    foot_in,
    far_out,
    far_in,
    load_sem,
    send_sem,
    recv_sem,
    factor_send,
    factor_recv,
):
    p, q = lax.axis_index("path"), lax.axis_index("width")
    blocks = lax.axis_size("path")
    ahead, behind = lax.rem(p + 1, blocks), lax.rem(p + blocks - 1, blocks)
    mirror, across = blocks - 1 - p, 1 - q
    mirror_before = lax.rem(2 * blocks - 2 - p, blocks)
    mirror_after = lax.rem(blocks - p, blocks)

    loads = [
        pltpu.make_async_copy(adj_hbm, state, load_sem.at[0]),
        pltpu.make_async_copy(vel_hbm, vel, load_sem.at[1]),
        pltpu.make_async_copy(adj_hbm, adj, load_sem.at[2]),
        pltpu.make_async_copy(kappa_hbm, kappa_ref, load_sem.at[4]),
        pltpu.make_async_copy(pair_hbm, pair_ref, load_sem.at[5]),
        pltpu.make_async_copy(matrix_hbm, matrix_ref, load_sem.at[6]),
        pltpu.make_async_copy(weight_hbm, weight, load_sem.at[7]),
    ]
    for load in loads:
        load.start()

    barrier = pltpu.get_barrier_semaphore()

    def greet(partner):
        pl.semaphore_signal(barrier, inc=1, device_id=partner, device_id_type=pl.DeviceIdType.MESH)

    greet({"path": mirror})
    greet({"path": mirror, "width": across})
    greet({"path": behind})
    greet({"path": ahead})
    greet({"path": behind, "width": across})
    greet({"path": ahead, "width": across})
    greet({"width": across})

    @pl.when(mirror_before != p)
    def _():
        greet({"path": mirror_before})

    @pl.when(mirror_after != p)
    def _():
        greet({"path": mirror_after})

    lane = lax.broadcasted_iota(jnp.int32, (8, 128), 1)
    level = lax.broadcasted_iota(jnp.int32, (8, 128), 0)
    width_lane = lane & 7
    first_row = (lane & 8) == 0
    row_lane = (lane >> 3) & 1
    layer = lane >> 4
    edge = 7 * (1 - q)
    edge_sign = (1 - 2 * q).astype(F32)
    other_edge = 7 * q

    def rolled(value, shift):
        return pltpu.roll(value, lax.rem(shift + 256, 128), 1)

    def remote(turn, kind, src, dst, device):
        return pltpu.make_async_remote_copy(
            src_ref=src,
            dst_ref=dst,
            send_sem=send_sem.at[turn, kind],
            recv_sem=recv_sem.at[turn, kind],
            device_id=device,
            device_id_type=pl.DeviceIdType.MESH,
        )

    def move(turn, kind):
        if kind == WALL:
            return remote(turn, kind, wall_out.at[turn], wall_in.at[turn], {"path": mirror})
        if kind == BEHIND:
            return remote(turn, kind, path_out.at[turn, 0], path_in.at[turn, 0], {"path": ahead})
        if kind == AHEAD:
            return remote(turn, kind, path_out.at[turn, 1], path_in.at[turn, 1], {"path": behind})
        if kind == ACROSS:
            return remote(turn, kind, side_out.at[turn], side_in.at[turn], {"width": across})
        if kind == CROSS_BEHIND:
            device = {"path": ahead, "width": across}
            return remote(turn, kind, cross_out.at[turn, 0], cross_in.at[turn, 0], device)
        if kind == CROSS_AHEAD:
            device = {"path": behind, "width": across}
            return remote(turn, kind, cross_out.at[turn, 1], cross_in.at[turn, 1], device)
        if kind == WALL_AHEAD:
            device = {"path": mirror_before}
            return remote(turn, kind, foot_out.at[turn, 0], foot_in.at[turn, 0], device)
        if kind == WALL_BEHIND:
            device = {"path": mirror_after}
            return remote(turn, kind, foot_out.at[turn, 1], foot_in.at[turn, 1], device)
        device = {"path": mirror, "width": across}
        return remote(turn, kind, far_out.at[turn], far_in.at[turn], device)

    def factor_move(kind):
        first, count, device = {
            WALL: (SIDE_V, LANES + 1 - SIDE_V, {"path": mirror}),
            BEHIND: (SIDE_V, FACTORS - SIDE_V, {"path": ahead}),
            AHEAD: (SIDE_V, FACTORS - SIDE_V, {"path": behind}),
            ACROSS: (EDGE_V, WALL_G + 1, {"width": across}),
        }[kind]
        return pltpu.make_async_remote_copy(
            src_ref=factor_out.at[pl.ds(first, count)],
            dst_ref=factor_in.at[kind, pl.ds(first, count)],
            send_sem=factor_send.at[kind],
            recv_sem=factor_recv.at[kind],
            device_id=device,
            device_id_type=pl.DeviceIdType.MESH,
        )

    def wall_guard(kind):
        return (mirror_before if kind == WALL_AHEAD else mirror_after) != p

    def send(turn):
        for kind in range(KINDS):
            if kind in (WALL_AHEAD, WALL_BEHIND):
                side = kind - WALL_AHEAD

                @pl.when(wall_guard(kind))
                def _():
                    move(turn, kind).start()

                @pl.when(jnp.logical_not(wall_guard(kind)))
                def _():
                    foot_in[turn, side] = foot_out[turn, side]
            else:
                move(turn, kind).start()

    def receive(turn, kind):
        if kind in (WALL_AHEAD, WALL_BEHIND):

            @pl.when(wall_guard(kind))
            def _():
                move(turn, kind).wait_recv()
        else:
            move(turn, kind).wait_recv()

    def traces_z():
        for a in range(8):
            low, high = end_slopes([state[face(a, c), :] for c in range(8)])
            slope_z[0, a] = low
            slope_z[1, a] = high

    def traces_s():
        for b in range(8):
            low, high = end_slopes([state[rows(a, b), :] for a in range(8)])
            slope_s[0, b] = low
            slope_s[1, b] = high

    def traces_w():
        for a in range(8):
            low, high = end_slopes([state[rows(a, b), :] for b in range(8)])
            slope_w[0, a] = low
            slope_w[1, a] = high

    def traces():
        traces_z()
        traces_s()
        traces_w()

    def by_layer(values):
        packed = values[0]
        for i in range(1, 8):
            packed = jnp.where(layer == i, turned(values[i], 16 * i), packed)
        return packed

    def by_width(values):
        packed = rolled(values[0], 0 - edge)
        for i in range(1, 8):
            packed = jnp.where(width_lane == i, rolled(values[i], i - edge), packed)
        return packed

    def pack(turn, second):
        at = 2 * second
        wall_out[turn, at] = by_layer([state[face(a, 0), :] for a in range(8)])
        wall_out[turn, at + 1] = by_layer([slope_z[0, a] for a in range(8)])
        for b in range(8):
            path_out[turn, 0, 8 * second + b] = jnp.where(
                first_row, turned(slope_s[1, b], 120), state[rows(7, b), :]
            )
            path_out[turn, 1, 8 * second + b] = jnp.where(
                first_row, state[rows(0, b), :], turned(slope_s[0, b], 8)
            )
        side_out[turn, at] = by_width([state[rows(a, edge), :] for a in range(8)])
        side_out[turn, at + 1] = by_width([slope_w[1 - q, a] for a in range(8)])

    def pack_corners(turn):
        value, slope = side_out[turn, 0], side_out[turn, 1]
        for side in range(2):
            packets = [path_out[turn, side, b] for b in range(8)]
            cross_out[turn, side, 0] = by_width(packets)
            foot_out[turn, side, 0] = wall_out[turn, 0]
            foot_out[turn, side, 1] = wall_out[turn, 1]
            foot_out[turn, side, 2] = by_layer(packets)
        cross_out[turn, 0, 1] = jnp.where(first_row, turned(slope, 120), value)
        cross_out[turn, 1, 1] = jnp.where(first_row, value, turned(slope, 8))
        far_out[turn, 0] = wall_out[turn, 0]
        far_out[turn, 1] = wall_out[turn, 1]
        far_out[turn, 2] = jnp.where(layer == 0, value, turned(slope, 16))

    def prepare(kappa, wall_index):
        base = kappa * 112.0
        for i in range(8):
            lift_s[0, i] = base - 28.0 * vel[rows(0, i), :]
            lift_s[1, i] = base + 28.0 * vel[rows(7, i), :]
            lift_w[0, i] = base - 28.0 * vel[rows(8 + i, 0), :]
            lift_w[1, i] = base + 28.0 * vel[rows(8 + i, 7), :]
            lift_z[0, i] = base - 28.0 * vel[face(16 + i, 0), :]
            lift_z[1, i] = base + 28.0 * vel[face(16 + i, 7), :]
        slope = kappa * 28.0
        inside = jnp.where(first_row, p, blocks - 1 - p) > 0
        path_g = jnp.where(inside, jnp.where(first_row, 0.0 - slope, slope), 0.0)
        path_v = [
            jnp.where(inside, jnp.where(first_row, lift_s[0, b], lift_s[1, b]), 0.0)
            for b in range(8)
        ]
        factor_out[SIDE_V] = by_width([lift_w[1 - q, a] for a in range(8)])
        factor_out[SIDE_G] = by_width([slope * edge_sign] * 8)
        factor_out[WALL_V] = by_layer([lift_z[0, a] for a in range(8)])
        factor_out[WALL_G] = by_layer([slope] * 8)
        factor_out[EDGE_V] = by_width(path_v)
        factor_out[EDGE_G] = by_width([path_g] * 8)
        factor_out[FOOT_V] = by_layer(path_v)
        factor_out[FOOT_G] = by_layer([path_g] * 8)
        factor_out[LANES] = wall_index.astype(F32)
        factor_out[KAPPA] = path_g
        for b in range(8):
            factor_out[PATH_V + b] = path_v[b]

    def local_rates(step, kappa):
        for b in range(8):
            line = [state[rows(a, b), :] for a in range(8)]
            even = [line[j] + line[7 - j] for j in range(4)]
            odd = [line[j] - line[7 - j] for j in range(4)]
            for i in range(4):
                for_even, for_odd = halves(ADVECT[i])
                left, right = weighted(for_even, even), weighted(for_odd, odd)
                for_even, for_odd = halves(SPREAD[i])
                inner, outer = weighted(for_even, even), weighted(for_odd, odd)
                near = vel[rows(i, b), :] * (left + right) + kappa * (inner + outer)
                far = vel[rows(7 - i, b), :] * (right - left) + kappa * (inner - outer)
                if i == 0:
                    lower = lift_s[0, b] * pltpu.roll(line[7], 8, 1) - (kappa * 28.0) * pltpu.roll(
                        slope_s[1, b], 8, 1
                    )
                    upper = lift_s[1, b] * pltpu.roll(line[0], 120, 1) + (
                        kappa * 28.0
                    ) * pltpu.roll(slope_s[0, b], 120, 1)
                    near = near + jnp.where(first_row, 0.0, lower)
                    far = far + jnp.where(first_row, upper, 0.0)
                rate[rows(i, b), :] = near
                rate[rows(7 - i, b), :] = far
        for pair in range(4):
            both = range(2 * pair, 2 * pair + 2)
            planes = [state[pl.ds(64 * a, 64), :] for a in both]
            plane = jnp.concatenate(planes, axis=1)
            high = plane.astype(BF16)
            low = (plane - high.astype(F32)).astype(BF16)
            stacked = jnp.concatenate([high, low, high], axis=0)
            product = jnp.dot(matrix_ref[...], stacked, preferred_element_type=F32)
            for k, a in enumerate(both):
                block = product[:, 128 * k : 128 * (k + 1)]
                bottom, top = state[face(a, 0), :], state[face(a, 7), :]
                first, last = state[rows(a, 0), :], state[rows(a, 7), :]
                for b in range(8):
                    at = slice(8 * b, 8 * b + 8)
                    value = (
                        rate[rows(a, b), :]
                        + vel[rows(8 + a, b), :] * block[0:64][at]
                        + vel[rows(16 + a, b), :] * block[64:128][at]
                        + kappa * block[128:192][at]
                    )
                    if b == 0:
                        lower = lift_w[0, a] * pltpu.roll(last, 1, 1) - (
                            kappa * 28.0
                        ) * pltpu.roll(slope_w[1, a], 1, 1)
                        value = value + jnp.where(width_lane == 0, 0.0, lower)
                    if b == 7:
                        upper = lift_w[1, a] * pltpu.roll(first, 127, 1) + (
                            kappa * 28.0
                        ) * pltpu.roll(slope_w[0, a], 127, 1)
                        value = value + jnp.where(width_lane == 7, 0.0, upper)
                    state[rows(a, b), :] = adj[rows(a, b), :] + step * value
                lower = lift_z[0, a] * pltpu.roll(top, 16, 1) - (kappa * 28.0) * pltpu.roll(
                    slope_z[1, a], 16, 1
                )
                upper = lift_z[1, a] * pltpu.roll(bottom, 112, 1) + (kappa * 28.0) * pltpu.roll(
                    slope_z[0, a], 112, 1
                )
                state[face(a, 0), :] += step * jnp.where(layer == 0, 0.0, lower)
                state[face(a, 7), :] += step * jnp.where(layer == 7, 0.0, upper)

    def far_rates(turn, second, step, kappa, wall_index):
        at = 2 * second
        change = step * (
            factor_out[SIDE_V] * side_in[turn, at] + factor_out[SIDE_G] * side_in[turn, at + 1]
        )
        for a in range(8):
            moved = rolled(change, edge - a)
            state[rows(a, edge), :] += jnp.where(width_lane == edge, moved, 0.0)
        path_g = factor_out[KAPPA]
        lower_lanes = first_row & (p > 0)
        upper_lanes = jnp.logical_not(first_row) & (p < blocks - 1)
        for b in range(8):
            packet = path_in[turn, 0, 8 * second + b]
            change = factor_out[PATH_V + b] * pltpu.roll(packet, 120, 1) + path_g * packet
            state[rows(0, b), :] += jnp.where(lower_lanes, step * change, 0.0)
            packet = path_in[turn, 1, 8 * second + b]
            change = factor_out[PATH_V + b] * pltpu.roll(packet, 8, 1) + path_g * packet
            state[rows(7, b), :] += jnp.where(upper_lanes, step * change, 0.0)
        value = lanes_moved(wall_in[turn, at], wall_index)
        slope = lanes_moved(wall_in[turn, at + 1], wall_index)
        change = step * (factor_out[WALL_V] * value + factor_out[WALL_G] * slope)
        for a in range(8):
            moved = turned(change, 0 - 16 * a)
            state[face(a, 0), :] += jnp.where(layer == 0, moved, 0.0)

    def lane_sum(value):
        for apart in (1, 2, 4):
            value = value + turned(value, 0 - apart)
        return value

    def layer_sum(value):
        for apart in (16, 32, 64):
            value = value + turned(value, apart)
        return value

    def level_sum(value):
        return jnp.broadcast_to(jnp.sum(value, axis=0, keepdims=True), (8, 128))

    def complete(turn, step, wall_index):
        low, high = float(SLOPE[0, 0]), float(SLOPE[7, 7])
        for b in range(8):
            packet = path_out[turn, 0, b]
            change = factor_in[AHEAD, PATH_V + b] * turned(packet, 120) + factor_in[AHEAD, KAPPA] * packet
            change = step * jnp.where(first_row, change, low * turned(change, 8))
            path_in[turn, 1, 8 + b] += change
            packet = path_out[turn, 1, b]
            change = factor_in[BEHIND, PATH_V + b] * turned(packet, 8) + factor_in[BEHIND, KAPPA] * packet
            change = step * jnp.where(first_row, high * turned(change, 120), change)
            path_in[turn, 0, 8 + b] += change
        packet = cross_in[turn, 1, 1]
        lower = factor_in[AHEAD, SIDE_V] * packet + factor_in[AHEAD, SIDE_G] * turned(packet, 120)
        packet = cross_in[turn, 0, 1]
        upper = factor_in[BEHIND, SIDE_V] * packet + factor_in[BEHIND, SIDE_G] * turned(packet, 8)
        change = step * jnp.where(first_row, lower, upper)
        slope = lane_sum(change * weight[0])
        lower = jnp.where(first_row, rolled(change, edge), rolled(slope, edge + 8))
        upper = jnp.where(first_row, rolled(slope, edge - 8), rolled(change, edge - 7))
        path_in[turn, 1, 8 + edge] += jnp.where(width_lane == edge, lower, 0.0)
        path_in[turn, 0, 8 + edge] += jnp.where(width_lane == edge, upper, 0.0)
        index = factor_in[AHEAD, LANES].astype(jnp.int32)
        lower = factor_in[AHEAD, WALL_V] * lanes_moved(foot_in[turn, 0, 0], index) + factor_in[
            AHEAD, WALL_G
        ] * lanes_moved(foot_in[turn, 0, 1], index)
        index = factor_in[BEHIND, LANES].astype(jnp.int32)
        upper = factor_in[BEHIND, WALL_V] * lanes_moved(foot_in[turn, 1, 0], index) + factor_in[
            BEHIND, WALL_G
        ] * lanes_moved(foot_in[turn, 1, 1], index)
        change = step * jnp.where(first_row, lower, upper)
        slope = layer_sum(change * weight[1])
        lower = jnp.where(first_row, change, turned(slope, 8))
        upper = jnp.where(first_row, turned(slope, 120), turned(change, 16))
        lower = jnp.where(layer == 0, lower, 0.0)
        upper = jnp.where(layer == 0, upper, 0.0)
        for b in range(8):
            path_in[turn, 1, 8 + b, 0:1] += lower[b : b + 1]
            path_in[turn, 0, 8 + b, 0:1] += upper[b : b + 1]
        change = step * (
            factor_in[ACROSS, SIDE_V] * side_out[turn, 0] + factor_in[ACROSS, SIDE_G] * side_out[turn, 1]
        )
        value_side = change
        slope_side = change * (edge_sign * low)
        packet = cross_in[turn, 0, 0]
        lower = factor_in[ACROSS, EDGE_V] * turned(packet, 120) + factor_in[ACROSS, EDGE_G] * packet
        packet = cross_in[turn, 1, 0]
        upper = factor_in[ACROSS, EDGE_V] * turned(packet, 8) + factor_in[ACROSS, EDGE_G] * packet
        change = step * jnp.where(first_row, lower, upper)
        slope = lane_sum(change * weight[2 + q])
        at_first = first_row & (width_lane == 0)
        at_last = jnp.logical_not(first_row) & (width_lane == 7)
        value_side += jnp.where(at_first, rolled(change, 0 - other_edge), 0.0)
        value_side += jnp.where(at_last, rolled(change, 7 - other_edge), 0.0)
        slope_side += jnp.where(at_first, slope, 0.0) + jnp.where(at_last, turned(slope, 7), 0.0)
        change = step * (
            factor_in[ACROSS, WALL_V] * lanes_moved(far_in[turn, 0], wall_index)
            + factor_in[ACROSS, WALL_G] * lanes_moved(far_in[turn, 1], wall_index)
        )
        index = 16 * width_lane + 8 * row_lane + other_edge
        value = lanes_moved(level_sum(jnp.where(level == other_edge, change, 0.0)), index)
        slope = lanes_moved(level_sum(change * weight[4 + q]), index)
        foot = (level == 0) & (layer == 0)
        side_in[turn, 2] += value_side + jnp.where(foot, value, 0.0)
        side_in[turn, 3] += slope_side + jnp.where(foot, slope, 0.0)
        index = factor_in[WALL, LANES].astype(jnp.int32)
        change = step * (
            factor_in[WALL, WALL_V] * lanes_moved(wall_out[turn, 0], index)
            + factor_in[WALL, WALL_G] * lanes_moved(wall_out[turn, 1], index)
        )
        value_wall = change
        slope_wall = change * low
        packet = foot_in[turn, 0, 2]
        lower = factor_in[WALL, FOOT_V] * turned(packet, 120) + factor_in[WALL, FOOT_G] * packet
        packet = foot_in[turn, 1, 2]
        upper = factor_in[WALL, FOOT_V] * turned(packet, 8) + factor_in[WALL, FOOT_G] * packet
        change = step * jnp.where(first_row, lower, upper)
        index = 16 * level + (lane & 15)
        value = lanes_moved(level_sum(jnp.where(level == 0, change, 0.0)), index)
        slope = lanes_moved(level_sum(change * weight[4]), index)
        ends = layer == 7 * row_lane
        value_wall += jnp.where(ends, value, 0.0)
        slope_wall += jnp.where(ends, slope, 0.0)
        packet = far_in[turn, 2]
        change = step * (
            factor_in[WALL, SIDE_V] * packet + factor_in[WALL, SIDE_G] * turned(packet, 112)
        )
        index = 8 * row_lane + layer
        value = lanes_moved(level_sum(jnp.where(level == 0, change, 0.0)), index)
        slope = lanes_moved(level_sum(change * weight[4]), index)
        corner = (level == edge) & (width_lane == edge)
        wall_in[turn, 2] += value_wall + jnp.where(corner, value, 0.0)
        wall_in[turn, 3] += slope_wall + jnp.where(corner, slope, 0.0)

    for load in loads:
        load.wait()
    kappa = jnp.broadcast_to(kappa_ref[...], (8, 128))
    wall_index = jnp.zeros((8, 128), jnp.int32)
    for j in range(16):
        wall_index = jnp.where((lane & 15) == j, pair_ref[0, j], wall_index)
    wall_index = wall_index + 16 * (7 - layer)
    prepare(kappa, wall_index)

    def advance(turn, carry):
        step = jnp.where(turn == 0, TIME_STEP / 4.0, TIME_STEP / 2.0).astype(F32)
        next_step = jnp.where(turn == 0, TIME_STEP / 3.0, TIME_STEP).astype(F32)
        traces()
        pack(turn, 0)
        pack_corners(turn)
        local_rates(step, kappa)
        traces()
        pack(turn, 1)

        @pl.when(turn == 0)
        def _():
            meet = (mirror_before != p).astype(jnp.int32) + (mirror_after != p).astype(jnp.int32)
            pl.semaphore_wait(barrier, 7 + meet)

        send(turn)

        @pl.when(turn == 0)
        def _():
            for kind in (WALL, BEHIND, AHEAD, ACROSS):
                factor_move(kind).start()

        for kind in (ACROSS, BEHIND, AHEAD, WALL):
            receive(turn, kind)
        far_rates(turn, 0, step, kappa, wall_index)
        traces()
        local_rates(next_step, kappa)
        for kind in (CROSS_BEHIND, CROSS_AHEAD, WALL_AHEAD, WALL_BEHIND, WALL_ACROSS):
            receive(turn, kind)

        @pl.when(turn == 0)
        def _():
            for kind in (WALL, BEHIND, AHEAD, ACROSS):
                factor_move(kind).wait_recv()

        complete(turn, step, wall_index)
        far_rates(turn, 1, next_step, kappa, wall_index)
        return carry

    lax.fori_loop(0, ROUNDS, advance, 0)
    store = pltpu.make_async_copy(state, out_hbm, load_sem.at[3])
    store.start()
    for kind in (WALL, BEHIND, AHEAD, ACROSS):
        factor_move(kind).wait_send()
    for turn in range(ROUNDS):
        for kind in range(KINDS):
            if kind in (WALL_AHEAD, WALL_BEHIND):

                @pl.when(wall_guard(kind))
                def _():
                    move(turn, kind).wait_send()
            else:
                move(turn, kind).wait_send()
    store.wait()


def shards(adjoint, velocity, diffusivity, wall_pair):
    tile = (8, 128)
    packets = [
        pltpu.VMEM((FACTORS,) + tile, F32),
        pltpu.VMEM((4, FACTORS) + tile, F32),
    ]
    for shape in ((2, 16), (4,), (4,), (2, 2), (2, 3), (3,)):
        packets += [pltpu.VMEM((ROUNDS,) + shape + tile, F32)] * 2
    result = pl.pallas_call(
        kernel,
        out_shape=jax.ShapeDtypeStruct((512, 128), F32),
        in_specs=[pl.BlockSpec(memory_space=pltpu.HBM)] * 6,
        out_specs=pl.BlockSpec(memory_space=pl.ANY),
        scratch_shapes=[
            pltpu.VMEM((1, 128), F32),
            pltpu.SMEM((1, 16), jnp.int32),
            pltpu.VMEM((192, 192), BF16),
            pltpu.VMEM((6,) + tile, F32),
            pltpu.VMEM((512, 128), F32),
            pltpu.VMEM((1536, 128), F32),
            pltpu.VMEM((512, 128), F32),
            pltpu.VMEM((512, 128), F32),
        ]
        + [pltpu.VMEM((2, 8) + tile, F32)] * 6
        + packets
        + [
            pltpu.SemaphoreType.DMA((8,)),
            pltpu.SemaphoreType.DMA((ROUNDS, KINDS)),
            pltpu.SemaphoreType.DMA((ROUNDS, KINDS)),
            pltpu.SemaphoreType.DMA((4,)),
            pltpu.SemaphoreType.DMA((4,)),
        ],
        compiler_params=pltpu.CompilerParams(
            collective_id=0, has_side_effects=True, vmem_limit_bytes=63 * 1024 * 1024
        ),
        name="plate_step",
    )(
        adjoint.reshape(512, 128),
        velocity.reshape(1536, 128),
        diffusivity,
        wall_pair,
        jnp.asarray(plane_matrix()),
        jnp.asarray(weight_rows()),
    )
    return result.reshape(adjoint.shape)


def solution(mesh):
    placed = (
        P("width", None, None, None, "path"),
        P(None, "width", None, None, None, "path"),
        P("width", "path"),
        P("path", None),
    )
    return jax.shard_map(
        shards,
        mesh=mesh,
        in_specs=placed,
        out_specs=P("width", None, None, None, "path"),
        check_vma=False,
    )
```

```python
import functools

import jax
import jax.numpy as jnp
import numpy as np
from jax import lax
from jax.experimental import pallas as pl
from jax.experimental.pallas import tpu as pltpu
from jax.sharding import PartitionSpec as P

TIME_STEP = 0.004
ROUNDS = 2
INNER_POINTS = (
    -0.8717401485096066,
    -0.5917001814331423,
    -0.2092992179024789,
    0.2092992179024789,
    0.5917001814331423,
    0.8717401485096066,
)
F32 = jnp.float32
BF16 = jnp.bfloat16
WALL, BEHIND, AHEAD, ACROSS, CROSS_BEHIND, CROSS_AHEAD, WALL_AHEAD, WALL_BEHIND, WALL_ACROSS = range(9)
KINDS = 9
SENT = (WALL_ACROSS, WALL, WALL_AHEAD, WALL_BEHIND, BEHIND, AHEAD, CROSS_BEHIND, CROSS_AHEAD, ACROSS)
LOWER_V, PATH_SIDE, PATH_WALL, PATH_ROWS, UPPER_V, EDGE_V, SIDE_V, WALL_V, ROWS, FOOT_V = 0, 4, 5, 6, 7, 11, 12, 13, 14, 15
FACTORS = 16
SIDE_G, WALL_G, PATH_G, AHEAD_SIDE, AHEAD_WALL, BEHIND_SIDE, BEHIND_WALL, ACROSS_SIDE, ACROSS_WALL, ACROSS_EDGE = range(10)
MIRROR_SIDE, MIRROR_WALL, MIRROR_FOOT = range(10, 13)


def legendre_seven(points):
    before = np.ones(points.shape)
    current = points * 1.0
    for order in range(1, 7):
        after = ((2.0 * order + 1.0) * points * current - order * before) / (order + 1.0)
        before = current
        current = after
    return current


def lobatto_table():
    degree = 7
    points = np.array((-1.0,) + INNER_POINTS + (1.0,))
    values = legendre_seven(points)
    table = np.zeros((degree + 1, degree + 1))
    for i in range(degree + 1):
        for j in range(degree + 1):
            if i != j:
                table[i, j] = values[i] / (values[j] * (points[i] - points[j]))
    table[0, 0] = -degree * (degree + 1) / 4.0
    table[degree, degree] = degree * (degree + 1) / 4.0
    return table


SLOPE = 2.0 * lobatto_table()
ADVECT = SLOPE.copy()
ADVECT[0, 0] += 28.0
ADVECT[7, 7] -= 28.0
SPREAD = SLOPE @ SLOPE
SPREAD[0] += 28.0 * SLOPE[0]
SPREAD[0, 0] -= 112.0
SPREAD[7] -= 28.0 * SLOPE[7]
SPREAD[7, 7] -= 112.0


def plane_matrix():
    eye = np.eye(8)
    full = np.concatenate(
        [np.kron(ADVECT, eye), np.kron(eye, ADVECT), np.kron(SPREAD, eye) + np.kron(eye, SPREAD)]
    )
    high = full.astype(jnp.bfloat16)
    low = (full - high.astype(np.float64)).astype(jnp.bfloat16)
    return np.concatenate([high, high, low], axis=1)


def weight_rows():
    lane = np.arange(128)
    second, width, layer = (lane >> 3) & 1, lane & 7, lane >> 4
    last = np.where(second[None] == 1, 7, 0)[0]
    flat = [SLOPE[last, width], SLOPE[last, layer], SLOPE[0, width], SLOPE[7, width]]
    wide = [np.broadcast_to(row, (8, 128)) for row in flat]
    tall = [np.broadcast_to(SLOPE[k][:, None], (8, 128)) for k in (0, 7)]
    return np.stack(wide + tall).astype(np.float32)


def halves(row):
    even = [float((row[j] + row[7 - j]) / 2) for j in range(4)]
    odd = [float((row[j] - row[7 - j]) / 2) for j in range(4)]
    return even, odd


def weighted(factors, values):
    total = values[0] * factors[0]
    for j in range(1, 4):
        total = total + values[j] * factors[j]
    return total


def end_slopes(line):
    even = [line[j] + line[7 - j] for j in range(4)]
    odd = [line[j] - line[7 - j] for j in range(4)]
    for_even, for_odd = halves(SLOPE[0])
    left, right = weighted(for_even, even), weighted(for_odd, odd)
    return left + right, right - left


def rows(a, b):
    return pl.ds((a * 8 + b) * 8, 8)


def face(a, c):
    return pl.ds(a * 64 + c, 8, stride=8)


def lanes_moved(value, index):
    return jnp.take_along_axis(value, index, axis=1)


def turned(value, shift):
    return pltpu.roll(value, shift % 128, 1) if shift % 128 else value


def kernel(
    adj_hbm,
    vel_hbm,
    kappa_hbm,
    pair_hbm,
    matrix_hbm,
    weight_hbm,
    state,
    kappa_ref,
    pair_ref,
    matrix_ref,
    weight,
    adj,
    vel,
    rate,
    slope_s,
    slope_w,
    slope_z,
    lift_s,
    lift_w,
    lift_z,
    path_v,
    slope_factor,
    factor_out,
    factor_in,
    path_out,
    path_in,
    wall_out,
    wall_in,
    side_out,
    side_in,
    cross_out,
    cross_in,
    foot_out,
    foot_in,
    far_out,
    far_in,
    load_sem,
    send_sem,
    recv_sem,
    factor_send,
    factor_recv,
):
    p, q = lax.axis_index("path"), lax.axis_index("width")
    blocks = lax.axis_size("path")
    ahead, behind = lax.rem(p + 1, blocks), lax.rem(p + blocks - 1, blocks)
    mirror, across = blocks - 1 - p, 1 - q
    mirror_before = lax.rem(2 * blocks - 2 - p, blocks)
    mirror_after = lax.rem(blocks - p, blocks)

    barrier = pltpu.get_barrier_semaphore()

    def greet(partner):
        pl.semaphore_signal(barrier, inc=1, device_id=partner, device_id_type=pl.DeviceIdType.MESH)

    greet({"path": mirror})
    greet({"path": mirror, "width": across})
    greet({"path": behind})
    greet({"path": ahead})
    greet({"path": behind, "width": across})
    greet({"path": ahead, "width": across})
    greet({"width": across})

    @pl.when(mirror_before != p)
    def _():
        greet({"path": mirror_before})

    @pl.when(mirror_after != p)
    def _():
        greet({"path": mirror_after})

    loads = [
        pltpu.make_async_copy(adj_hbm, state, load_sem.at[0]),
        pltpu.make_async_copy(vel_hbm, vel, load_sem.at[1]),
        pltpu.make_async_copy(adj_hbm, adj, load_sem.at[2]),
        pltpu.make_async_copy(kappa_hbm, kappa_ref, load_sem.at[4]),
        pltpu.make_async_copy(pair_hbm, pair_ref, load_sem.at[5]),
        pltpu.make_async_copy(matrix_hbm, matrix_ref, load_sem.at[6]),
        pltpu.make_async_copy(weight_hbm, weight, load_sem.at[7]),
    ]
    for load in loads:
        load.start()

    lane = lax.broadcasted_iota(jnp.int32, (8, 128), 1)
    level = lax.broadcasted_iota(jnp.int32, (8, 128), 0)
    width_lane = lane & 7
    first_row = (lane & 8) == 0
    row_lane = (lane >> 3) & 1
    layer = lane >> 4
    edge = 7 * (1 - q)
    edge_sign = (1 - 2 * q).astype(F32)
    other_edge = 7 * q
    side_lanes = lane - width_lane + edge
    other_side_lanes = lane - width_lane + other_edge
    foot_lanes = lane & 15

    def rolled(value, shift):
        return pltpu.roll(value, lax.rem(shift + 256, 128), 1)

    def remote(turn, kind, src, dst, device):
        return pltpu.make_async_remote_copy(
            src_ref=src,
            dst_ref=dst,
            send_sem=send_sem.at[turn, kind],
            recv_sem=recv_sem.at[turn, kind],
            device_id=device,
            device_id_type=pl.DeviceIdType.MESH,
        )

    def move(turn, kind):
        if kind == WALL:
            return remote(turn, kind, wall_out.at[turn], wall_in.at[turn], {"path": mirror})
        if kind == BEHIND:
            return remote(turn, kind, path_out.at[turn, 0], path_in.at[turn, 0], {"path": ahead})
        if kind == AHEAD:
            return remote(turn, kind, path_out.at[turn, 1], path_in.at[turn, 1], {"path": behind})
        if kind == ACROSS:
            return remote(turn, kind, side_out.at[turn], side_in.at[turn], {"width": across})
        if kind == CROSS_BEHIND:
            device = {"path": ahead, "width": across}
            return remote(turn, kind, cross_out.at[turn, 0], cross_in.at[turn, 0], device)
        if kind == CROSS_AHEAD:
            device = {"path": behind, "width": across}
            return remote(turn, kind, cross_out.at[turn, 1], cross_in.at[turn, 1], device)
        if kind == WALL_AHEAD:
            device = {"path": mirror_before}
            return remote(turn, kind, foot_out.at[turn, 0], foot_in.at[turn, 0], device)
        if kind == WALL_BEHIND:
            device = {"path": mirror_after}
            return remote(turn, kind, foot_out.at[turn, 1], foot_in.at[turn, 1], device)
        device = {"path": mirror, "width": across}
        return remote(turn, kind, far_out.at[turn], far_in.at[turn], device)

    def factor_move(kind):
        first, count, device = {
            WALL: (SIDE_V, 4, {"path": mirror}),
            BEHIND: (PATH_SIDE, 7, {"path": ahead}),
            AHEAD: (LOWER_V, 7, {"path": behind}),
            ACROSS: (EDGE_V, 4, {"width": across}),
        }[kind]
        return pltpu.make_async_remote_copy(
            src_ref=factor_out.at[pl.ds(first, count)],
            dst_ref=factor_in.at[kind, pl.ds(first, count)],
            send_sem=factor_send.at[kind],
            recv_sem=factor_recv.at[kind],
            device_id=device,
            device_id_type=pl.DeviceIdType.MESH,
        )

    def wall_guard(kind):
        return (mirror_before if kind == WALL_AHEAD else mirror_after) != p

    def send(turn):
        for kind in SENT:
            if kind in (WALL_AHEAD, WALL_BEHIND):
                side = kind - WALL_AHEAD

                @pl.when(wall_guard(kind))
                def _():
                    move(turn, kind).start()

                @pl.when(jnp.logical_not(wall_guard(kind)))
                def _():
                    foot_in[turn, side] = foot_out[turn, side]
            else:
                move(turn, kind).start()

    def receive(turn, kind):
        if kind in (WALL_AHEAD, WALL_BEHIND):

            @pl.when(wall_guard(kind))
            def _():
                move(turn, kind).wait_recv()
        else:
            move(turn, kind).wait_recv()

    def traces_z():
        for a in range(8):
            low, high = end_slopes([state[face(a, c), :] for c in range(8)])
            slope_z[0, a] = low
            slope_z[1, a] = high

    def traces_s():
        for b in range(8):
            low, high = end_slopes([state[rows(a, b), :] for a in range(8)])
            slope_s[0, b] = low
            slope_s[1, b] = high

    def traces_w():
        for a in range(8):
            low, high = end_slopes([state[rows(a, b), :] for b in range(8)])
            slope_w[0, a] = low
            slope_w[1, a] = high

    def traces():
        traces_z()
        traces_s()
        traces_w()

    def by_layer(values):
        packed = values[0]
        for i in range(1, 8):
            packed = jnp.where(layer == i, turned(values[i], 16 * i), packed)
        return packed

    def by_width(values):
        packed = rolled(values[0], 0 - edge)
        for i in range(1, 8):
            packed = jnp.where(width_lane == i, rolled(values[i], i - edge), packed)
        return packed

    def pack(turn, second):
        at = 2 * second
        wall_out[turn, at] = by_layer([state[face(a, 0), :] for a in range(8)])
        wall_out[turn, at + 1] = by_layer([slope_z[0, a] for a in range(8)])
        for b in range(8):
            path_out[turn, 0, 8 * second + b] = jnp.where(
                first_row, turned(slope_s[1, b], 120), state[rows(7, b), :]
            )
            path_out[turn, 1, 8 * second + b] = jnp.where(
                first_row, state[rows(0, b), :], turned(slope_s[0, b], 8)
            )
        side_out[turn, at] = by_width([state[rows(a, edge), :] for a in range(8)])
        side_out[turn, at + 1] = by_width([slope_w[1 - q, a] for a in range(8)])

    def pack_corners(turn):
        value, slope = side_out[turn, 0], side_out[turn, 1]
        for side in range(2):
            packets = [path_out[turn, side, b] for b in range(8)]
            cross_out[turn, side, 0] = by_width(packets)
            foot_out[turn, side, 0] = wall_out[turn, 0]
            foot_out[turn, side, 1] = wall_out[turn, 1]
            foot_out[turn, side, 2] = by_layer(packets)
        cross_out[turn, 0, 1] = jnp.where(first_row, turned(slope, 120), value)
        cross_out[turn, 1, 1] = jnp.where(first_row, value, turned(slope, 8))
        far_out[turn, 0] = wall_out[turn, 0]
        far_out[turn, 1] = wall_out[turn, 1]
        far_out[turn, 2] = jnp.where(layer == 0, value, turned(slope, 16))

    def prepare(kappa, wall_index):
        base = kappa * 112.0
        for i in range(8):
            lift_s[0, i] = base - 28.0 * vel[rows(0, i), :]
            lift_s[1, i] = base + 28.0 * vel[rows(7, i), :]
            lift_w[0, i] = base - 28.0 * vel[rows(8 + i, 0), :]
            lift_w[1, i] = base + 28.0 * vel[rows(8 + i, 7), :]
            lift_z[0, i] = base - 28.0 * vel[face(16 + i, 0), :]
            lift_z[1, i] = base + 28.0 * vel[face(16 + i, 7), :]
        slope = kappa * 28.0
        inside = jnp.where(first_row, p, blocks - 1 - p) > 0
        path_g = jnp.where(inside, jnp.where(first_row, 0.0 - slope, slope), 0.0)
        for b in range(8):
            lift = jnp.where(first_row, lift_s[0, b], lift_s[1, b])
            path_v[b] = jnp.where(inside, lift, 0.0)
        on_path = [path_v[b] for b in range(8)]
        for k in range(4):
            one, two = on_path[2 * k], on_path[2 * k + 1]
            factor_out[LOWER_V + k] = jnp.where(first_row, one, turned(two, 8))
            factor_out[UPPER_V + k] = jnp.where(first_row, turned(two, 120), one)
        side = by_width([lift_w[1 - q, a] for a in range(8)])
        wall = by_layer([lift_z[0, a] for a in range(8)])
        told = jnp.where(level == 0, wall_index.astype(F32), jnp.where(level == 1, path_g, slope))
        for at in (PATH_SIDE, SIDE_V):
            factor_out[at] = side
            factor_out[at + 1] = wall
            factor_out[at + 2] = told
        factor_out[EDGE_V] = by_width(on_path)
        factor_out[FOOT_V] = by_layer(on_path)
        slope_factor[SIDE_G] = lanes_moved(slope * edge_sign, side_lanes)
        slope_factor[WALL_G] = lanes_moved(slope, foot_lanes)
        slope_factor[PATH_G] = path_g

    def told_row(kind, at, row):
        return jnp.broadcast_to(factor_in[kind, at, row : row + 1], (8, 128))

    def learn():
        for kind, at, side in (
            (AHEAD, PATH_ROWS, AHEAD_SIDE),
            (BEHIND, PATH_ROWS, BEHIND_SIDE),
            (WALL, ROWS, MIRROR_SIDE),
        ):
            slope = told_row(kind, at, 2)
            slope_factor[side] = lanes_moved(slope * edge_sign, side_lanes)
            slope_factor[side + 1] = lanes_moved(slope, foot_lanes)
        slope = told_row(ACROSS, ROWS, 2)
        slope_factor[ACROSS_SIDE] = 0.0 - lanes_moved(slope * edge_sign, other_side_lanes)
        slope_factor[ACROSS_WALL] = lanes_moved(slope, foot_lanes)
        slope_factor[ACROSS_EDGE] = lanes_moved(told_row(ACROSS, ROWS, 1), other_side_lanes)
        slope_factor[MIRROR_FOOT] = lanes_moved(told_row(WALL, ROWS, 1), foot_lanes)

    def local_rates(step, kappa):
        for b in range(8):
            line = [state[rows(a, b), :] for a in range(8)]
            even = [line[j] + line[7 - j] for j in range(4)]
            odd = [line[j] - line[7 - j] for j in range(4)]
            for i in range(4):
                for_even, for_odd = halves(ADVECT[i])
                left, right = weighted(for_even, even), weighted(for_odd, odd)
                for_even, for_odd = halves(SPREAD[i])
                inner, outer = weighted(for_even, even), weighted(for_odd, odd)
                near = vel[rows(i, b), :] * (left + right) + kappa * (inner + outer)
                far = vel[rows(7 - i, b), :] * (right - left) + kappa * (inner - outer)
                if i == 0:
                    lower = lift_s[0, b] * pltpu.roll(line[7], 8, 1) - (kappa * 28.0) * pltpu.roll(
                        slope_s[1, b], 8, 1
                    )
                    upper = lift_s[1, b] * pltpu.roll(line[0], 120, 1) + (
                        kappa * 28.0
                    ) * pltpu.roll(slope_s[0, b], 120, 1)
                    near = near + jnp.where(first_row, 0.0, lower)
                    far = far + jnp.where(first_row, upper, 0.0)
                rate[rows(i, b), :] = near
                rate[rows(7 - i, b), :] = far
        for pair in range(4):
            both = range(2 * pair, 2 * pair + 2)
            planes = [state[pl.ds(64 * a, 64), :] for a in both]
            plane = jnp.concatenate(planes, axis=1)
            high = plane.astype(BF16)
            low = (plane - high.astype(F32)).astype(BF16)
            stacked = jnp.concatenate([high, low, high], axis=0)
            product = jnp.dot(matrix_ref[...], stacked, preferred_element_type=F32)
            for k, a in enumerate(both):
                block = product[:, 128 * k : 128 * (k + 1)]
                bottom, top = state[face(a, 0), :], state[face(a, 7), :]
                first, last = state[rows(a, 0), :], state[rows(a, 7), :]
                for b in range(8):
                    at = slice(8 * b, 8 * b + 8)
                    value = (
                        rate[rows(a, b), :]
                        + vel[rows(8 + a, b), :] * block[0:64][at]
                        + vel[rows(16 + a, b), :] * block[64:128][at]
                        + kappa * block[128:192][at]
                    )
                    if b == 0:
                        lower = lift_w[0, a] * pltpu.roll(last, 1, 1) - (
                            kappa * 28.0
                        ) * pltpu.roll(slope_w[1, a], 1, 1)
                        value = value + jnp.where(width_lane == 0, 0.0, lower)
                    if b == 7:
                        upper = lift_w[1, a] * pltpu.roll(first, 127, 1) + (
                            kappa * 28.0
                        ) * pltpu.roll(slope_w[0, a], 127, 1)
                        value = value + jnp.where(width_lane == 7, 0.0, upper)
                    state[rows(a, b), :] = adj[rows(a, b), :] + step * value
                lower = lift_z[0, a] * pltpu.roll(top, 16, 1) - (kappa * 28.0) * pltpu.roll(
                    slope_z[1, a], 16, 1
                )
                upper = lift_z[1, a] * pltpu.roll(bottom, 112, 1) + (kappa * 28.0) * pltpu.roll(
                    slope_z[0, a], 112, 1
                )
                state[face(a, 0), :] += step * jnp.where(layer == 0, 0.0, lower)
                state[face(a, 7), :] += step * jnp.where(layer == 7, 0.0, upper)

    def far_rates(turn, second, step, kappa, wall_index):
        at = 2 * second
        change = step * (
            factor_out[SIDE_V] * side_in[turn, at] + slope_factor[SIDE_G] * side_in[turn, at + 1]
        )
        for a in range(8):
            moved = rolled(change, edge - a)
            state[rows(a, edge), :] += jnp.where(width_lane == edge, moved, 0.0)
        path_g = slope_factor[PATH_G]
        lower_lanes = first_row & (p > 0)
        upper_lanes = jnp.logical_not(first_row) & (p < blocks - 1)
        for b in range(8):
            packet = path_in[turn, 0, 8 * second + b]
            change = path_v[b] * pltpu.roll(packet, 120, 1) + path_g * packet
            state[rows(0, b), :] += jnp.where(lower_lanes, step * change, 0.0)
            packet = path_in[turn, 1, 8 * second + b]
            change = path_v[b] * pltpu.roll(packet, 8, 1) + path_g * packet
            state[rows(7, b), :] += jnp.where(upper_lanes, step * change, 0.0)
        value = lanes_moved(wall_in[turn, at], wall_index)
        slope = lanes_moved(wall_in[turn, at + 1], wall_index)
        change = step * (factor_out[WALL_V] * value + slope_factor[WALL_G] * slope)
        for a in range(8):
            moved = turned(change, 0 - 16 * a)
            state[face(a, 0), :] += jnp.where(layer == 0, moved, 0.0)

    def lane_sum(value):
        for apart in (1, 2, 4):
            value = value + turned(value, 0 - apart)
        return value

    def layer_sum(value):
        for apart in (16, 32, 64):
            value = value + turned(value, apart)
        return value

    def level_sum(value):
        return jnp.broadcast_to(jnp.sum(value, axis=0, keepdims=True), (8, 128))

    def complete(turn, step, wall_index):
        low, high = float(SLOPE[0, 0]), float(SLOPE[7, 7])
        ahead_g, behind_g = told_row(AHEAD, PATH_ROWS, 1), told_row(BEHIND, PATH_ROWS, 1)
        for b in range(8):
            packet = path_out[turn, 0, b]
            lift = factor_in[AHEAD, LOWER_V + b // 2]
            lift = turned(lift, 120) if b % 2 else lift
            change = lift * turned(packet, 120) + ahead_g * packet
            change = step * jnp.where(first_row, change, low * turned(change, 8))
            path_in[turn, 1, 8 + b] += change
            packet = path_out[turn, 1, b]
            lift = factor_in[BEHIND, UPPER_V + b // 2]
            lift = turned(lift, 8) if b % 2 else lift
            change = lift * turned(packet, 8) + behind_g * packet
            change = step * jnp.where(first_row, high * turned(change, 120), change)
            path_in[turn, 0, 8 + b] += change
        packet = cross_in[turn, 1, 1]
        lower = factor_in[AHEAD, PATH_SIDE] * packet + slope_factor[AHEAD_SIDE] * turned(packet, 120)
        packet = cross_in[turn, 0, 1]
        upper = factor_in[BEHIND, PATH_SIDE] * packet + slope_factor[BEHIND_SIDE] * turned(packet, 8)
        change = step * jnp.where(first_row, lower, upper)
        slope = lane_sum(change * weight[0])
        lower = jnp.where(first_row, rolled(change, edge), rolled(slope, edge + 8))
        upper = jnp.where(first_row, rolled(slope, edge - 8), rolled(change, edge - 7))
        path_in[turn, 1, 8 + edge] += jnp.where(width_lane == edge, lower, 0.0)
        path_in[turn, 0, 8 + edge] += jnp.where(width_lane == edge, upper, 0.0)
        index = told_row(AHEAD, PATH_ROWS, 0).astype(jnp.int32)
        lower = factor_in[AHEAD, PATH_WALL] * lanes_moved(foot_in[turn, 0, 0], index) + slope_factor[
            AHEAD_WALL
        ] * lanes_moved(foot_in[turn, 0, 1], index)
        index = told_row(BEHIND, PATH_ROWS, 0).astype(jnp.int32)
        upper = factor_in[BEHIND, PATH_WALL] * lanes_moved(foot_in[turn, 1, 0], index) + slope_factor[
            BEHIND_WALL
        ] * lanes_moved(foot_in[turn, 1, 1], index)
        change = step * jnp.where(first_row, lower, upper)
        slope = layer_sum(change * weight[1])
        lower = jnp.where(first_row, change, turned(slope, 8))
        upper = jnp.where(first_row, turned(slope, 120), turned(change, 16))
        lower = jnp.where(layer == 0, lower, 0.0)
        upper = jnp.where(layer == 0, upper, 0.0)
        for b in range(8):
            path_in[turn, 1, 8 + b, 0:1] += lower[b : b + 1]
            path_in[turn, 0, 8 + b, 0:1] += upper[b : b + 1]
        change = step * (
            factor_in[ACROSS, SIDE_V] * side_out[turn, 0] + slope_factor[ACROSS_SIDE] * side_out[turn, 1]
        )
        value_side = change
        slope_side = change * (edge_sign * low)
        packet = cross_in[turn, 0, 0]
        lower = factor_in[ACROSS, EDGE_V] * turned(packet, 120) + slope_factor[ACROSS_EDGE] * packet
        packet = cross_in[turn, 1, 0]
        upper = factor_in[ACROSS, EDGE_V] * turned(packet, 8) + slope_factor[ACROSS_EDGE] * packet
        change = step * jnp.where(first_row, lower, upper)
        slope = lane_sum(change * weight[2 + q])
        at_first = first_row & (width_lane == 0)
        at_last = jnp.logical_not(first_row) & (width_lane == 7)
        value_side += jnp.where(at_first, rolled(change, 0 - other_edge), 0.0)
        value_side += jnp.where(at_last, rolled(change, 7 - other_edge), 0.0)
        slope_side += jnp.where(at_first, slope, 0.0) + jnp.where(at_last, turned(slope, 7), 0.0)
        change = step * (
            factor_in[ACROSS, WALL_V] * lanes_moved(far_in[turn, 0], wall_index)
            + slope_factor[ACROSS_WALL] * lanes_moved(far_in[turn, 1], wall_index)
        )
        index = 16 * width_lane + 8 * row_lane + other_edge
        value = lanes_moved(level_sum(jnp.where(level == other_edge, change, 0.0)), index)
        slope = lanes_moved(level_sum(change * weight[4 + q]), index)
        foot = (level == 0) & (layer == 0)
        side_in[turn, 2] += value_side + jnp.where(foot, value, 0.0)
        side_in[turn, 3] += slope_side + jnp.where(foot, slope, 0.0)
        index = told_row(WALL, ROWS, 0).astype(jnp.int32)
        change = step * (
            factor_in[WALL, WALL_V] * lanes_moved(wall_out[turn, 0], index)
            + slope_factor[MIRROR_WALL] * lanes_moved(wall_out[turn, 1], index)
        )
        value_wall = change
        slope_wall = change * low
        packet = foot_in[turn, 0, 2]
        lower = factor_in[WALL, FOOT_V] * turned(packet, 120) + slope_factor[MIRROR_FOOT] * packet
        packet = foot_in[turn, 1, 2]
        upper = factor_in[WALL, FOOT_V] * turned(packet, 8) + slope_factor[MIRROR_FOOT] * packet
        change = step * jnp.where(first_row, lower, upper)
        index = 16 * level + (lane & 15)
        value = lanes_moved(level_sum(jnp.where(level == 0, change, 0.0)), index)
        slope = lanes_moved(level_sum(change * weight[4]), index)
        ends = layer == 7 * row_lane
        value_wall += jnp.where(ends, value, 0.0)
        slope_wall += jnp.where(ends, slope, 0.0)
        packet = far_in[turn, 2]
        change = step * (
            factor_in[WALL, SIDE_V] * packet + slope_factor[MIRROR_SIDE] * turned(packet, 112)
        )
        index = 8 * row_lane + layer
        value = lanes_moved(level_sum(jnp.where(level == 0, change, 0.0)), index)
        slope = lanes_moved(level_sum(change * weight[4]), index)
        corner = (level == edge) & (width_lane == edge)
        wall_in[turn, 2] += value_wall + jnp.where(corner, value, 0.0)
        wall_in[turn, 3] += slope_wall + jnp.where(corner, slope, 0.0)

    for load in loads:
        load.wait()
    kappa = jnp.broadcast_to(kappa_ref[...], (8, 128))
    wall_index = jnp.zeros((8, 128), jnp.int32)
    for j in range(16):
        wall_index = jnp.where((lane & 15) == j, pair_ref[0, j], wall_index)
    wall_index = wall_index + 16 * (7 - layer)
    prepare(kappa, wall_index)

    def advance(turn, carry):
        step = jnp.where(turn == 0, TIME_STEP / 4.0, TIME_STEP / 2.0).astype(F32)
        next_step = jnp.where(turn == 0, TIME_STEP / 3.0, TIME_STEP).astype(F32)
        traces()
        pack(turn, 0)
        pack_corners(turn)
        local_rates(step, kappa)
        traces()
        pack(turn, 1)

        @pl.when(turn == 0)
        def _():
            meet = (mirror_before != p).astype(jnp.int32) + (mirror_after != p).astype(jnp.int32)
            pl.semaphore_wait(barrier, 7 + meet)

        send(turn)

        @pl.when(turn == 0)
        def _():
            for kind in (WALL, BEHIND, AHEAD, ACROSS):
                factor_move(kind).start()

        for kind in (ACROSS, BEHIND, AHEAD, WALL):
            receive(turn, kind)
        far_rates(turn, 0, step, kappa, wall_index)
        traces()
        local_rates(next_step, kappa)
        for kind in (CROSS_BEHIND, CROSS_AHEAD, WALL_AHEAD, WALL_BEHIND, WALL_ACROSS):
            receive(turn, kind)

        @pl.when(turn == 0)
        def _():
            for kind in (WALL, BEHIND, AHEAD, ACROSS):
                factor_move(kind).wait_recv()
            learn()

        complete(turn, step, wall_index)
        far_rates(turn, 1, next_step, kappa, wall_index)
        return carry

    lax.fori_loop(0, ROUNDS, advance, 0)
    for kind in (WALL, BEHIND, AHEAD, ACROSS):
        factor_move(kind).wait_send()
    for turn in range(ROUNDS):
        for kind in range(KINDS):
            if kind in (WALL_AHEAD, WALL_BEHIND):

                @pl.when(wall_guard(kind))
                def _():
                    move(turn, kind).wait_send()
            else:
                move(turn, kind).wait_send()


def shards(adjoint, velocity, diffusivity, wall_pair):
    tile = (8, 128)
    packets = [
        pltpu.VMEM((8,) + tile, F32),
        pltpu.VMEM((13,) + tile, F32),
        pltpu.VMEM((FACTORS,) + tile, F32),
        pltpu.VMEM((4, FACTORS) + tile, F32),
    ]
    for shape in ((2, 16), (4,), (4,), (2, 2), (2, 3), (3,)):
        packets += [pltpu.VMEM((ROUNDS,) + shape + tile, F32)] * 2
    operands = (
        adjoint.reshape(512, 128),
        velocity.reshape(1536, 128),
        diffusivity,
        wall_pair,
        jnp.asarray(plane_matrix()),
        jnp.asarray(weight_rows()),
    )
    result = pl.pallas_call(
        kernel,
        out_shape=jax.ShapeDtypeStruct((512, 128), F32),
        in_specs=[pl.BlockSpec(memory_space=pltpu.HBM)] * 6,
        out_specs=pl.BlockSpec(memory_space=pltpu.VMEM),
        scratch_shapes=[
            pltpu.VMEM((1, 128), F32),
            pltpu.SMEM((1, 16), jnp.int32),
            pltpu.VMEM((192, 192), BF16),
            pltpu.VMEM((6,) + tile, F32),
            pltpu.VMEM((512, 128), F32),
            pltpu.VMEM((1536, 128), F32),
            pltpu.VMEM((512, 128), F32),
        ]
        + [pltpu.VMEM((2, 8) + tile, F32)] * 6
        + packets
        + [
            pltpu.SemaphoreType.DMA((8,)),
            pltpu.SemaphoreType.DMA((ROUNDS, KINDS)),
            pltpu.SemaphoreType.DMA((ROUNDS, KINDS)),
            pltpu.SemaphoreType.DMA((4,)),
            pltpu.SemaphoreType.DMA((4,)),
        ],
        compiler_params=pltpu.CompilerParams(
            collective_id=0, has_side_effects=True, vmem_limit_bytes=32 * 1024 * 1024
        ),
        name="plate_step",
    )(*(pltpu.with_memory_space_constraint(array, pltpu.HBM) for array in operands))
    return result.reshape(adjoint.shape)


def solution(mesh):
    placed = (
        P("width", None, None, None, "path"),
        P(None, "width", None, None, None, "path"),
        P("width", "path"),
        P("path", None),
    )
    return jax.shard_map(
        shards,
        mesh=mesh,
        in_specs=placed,
        out_specs=P("width", None, None, None, "path"),
        check_vma=False,
    )
```

```python
import functools

import jax
import jax.numpy as jnp
import numpy as np
from jax import lax
from jax.experimental import pallas as pl
from jax.experimental.pallas import tpu as pltpu
from jax.sharding import PartitionSpec as P

TIME_STEP = 0.004
ROUNDS = 2
INNER_POINTS = (
    -0.8717401485096066,
    -0.5917001814331423,
    -0.2092992179024789,
    0.2092992179024789,
    0.5917001814331423,
    0.8717401485096066,
)
F32 = jnp.float32
BF16 = jnp.bfloat16
WALL, BEHIND, AHEAD, ACROSS, CROSS_BEHIND, CROSS_AHEAD, WALL_AHEAD, WALL_BEHIND, WALL_ACROSS = range(9)
LATER = 9
KINDS = 13
SENT = (WALL_ACROSS, WALL, WALL_AHEAD, WALL_BEHIND, BEHIND, AHEAD, LATER + WALL) + (
    CROSS_BEHIND,
    CROSS_AHEAD,
    ACROSS,
    LATER + BEHIND,
    LATER + AHEAD,
    LATER + ACROSS,
)
LOWER_V, PATH_SIDE, PATH_WALL, PATH_ROWS, UPPER_V, EDGE_V, SIDE_V, WALL_V, ROWS, FOOT_V = 0, 4, 5, 6, 7, 11, 12, 13, 14, 15
FACTORS = 16
SIDE_G, WALL_G, PATH_G, AHEAD_SIDE, AHEAD_WALL, BEHIND_SIDE, BEHIND_WALL, ACROSS_SIDE, ACROSS_WALL, ACROSS_EDGE = range(10)
MIRROR_SIDE, MIRROR_WALL, MIRROR_FOOT = range(10, 13)


def legendre_seven(points):
    before = np.ones(points.shape)
    current = points * 1.0
    for order in range(1, 7):
        after = ((2.0 * order + 1.0) * points * current - order * before) / (order + 1.0)
        before = current
        current = after
    return current


def lobatto_table():
    degree = 7
    points = np.array((-1.0,) + INNER_POINTS + (1.0,))
    values = legendre_seven(points)
    table = np.zeros((degree + 1, degree + 1))
    for i in range(degree + 1):
        for j in range(degree + 1):
            if i != j:
                table[i, j] = values[i] / (values[j] * (points[i] - points[j]))
    table[0, 0] = -degree * (degree + 1) / 4.0
    table[degree, degree] = degree * (degree + 1) / 4.0
    return table


SLOPE = 2.0 * lobatto_table()
ADVECT = SLOPE.copy()
ADVECT[0, 0] += 28.0
ADVECT[7, 7] -= 28.0
SPREAD = SLOPE @ SLOPE
SPREAD[0] += 28.0 * SLOPE[0]
SPREAD[0, 0] -= 112.0
SPREAD[7] -= 28.0 * SLOPE[7]
SPREAD[7, 7] -= 112.0


def plane_matrix():
    eye = np.eye(8)
    full = np.concatenate(
        [np.kron(ADVECT, eye), np.kron(eye, ADVECT), np.kron(SPREAD, eye) + np.kron(eye, SPREAD)]
    )
    high = full.astype(jnp.bfloat16)
    low = (full - high.astype(np.float64)).astype(jnp.bfloat16)
    return np.concatenate([high, high, low], axis=1)


def weight_rows():
    lane = np.arange(128)
    second, width, layer = (lane >> 3) & 1, lane & 7, lane >> 4
    last = np.where(second[None] == 1, 7, 0)[0]
    flat = [SLOPE[last, width], SLOPE[last, layer], SLOPE[0, width], SLOPE[7, width]]
    wide = [np.broadcast_to(row, (8, 128)) for row in flat]
    tall = [np.broadcast_to(SLOPE[k][:, None], (8, 128)) for k in (0, 7)]
    return np.stack(wide + tall).astype(np.float32)


def halves(row):
    even = [float((row[j] + row[7 - j]) / 2) for j in range(4)]
    odd = [float((row[j] - row[7 - j]) / 2) for j in range(4)]
    return even, odd


def weighted(factors, values):
    total = values[0] * factors[0]
    for j in range(1, 4):
        total = total + values[j] * factors[j]
    return total


def end_slopes(line):
    even = [line[j] + line[7 - j] for j in range(4)]
    odd = [line[j] - line[7 - j] for j in range(4)]
    for_even, for_odd = halves(SLOPE[0])
    left, right = weighted(for_even, even), weighted(for_odd, odd)
    return left + right, right - left


def rows(a, b):
    return pl.ds((a * 8 + b) * 8, 8)


def face(a, c):
    return pl.ds(a * 64 + c, 8, stride=8)


def lanes_moved(value, index):
    return jnp.take_along_axis(value, index, axis=1)


def turned(value, shift):
    return pltpu.roll(value, shift % 128, 1) if shift % 128 else value


def kernel(
    adj_hbm,
    vel_hbm,
    kappa_hbm,
    pair_hbm,
    matrix_hbm,
    weight_hbm,
    state,
    kappa_ref,
    pair_ref,
    matrix_ref,
    weight,
    adj,
    vel,
    rate,
    slope_s,
    slope_w,
    slope_z,
    lift_s,
    lift_w,
    lift_z,
    path_v,
    slope_factor,
    pending,
    factor_out,
    factor_in,
    path_out,
    path_in,
    wall_out,
    wall_in,
    side_out,
    side_in,
    cross_out,
    cross_in,
    foot_out,
    foot_in,
    far_out,
    far_in,
    load_sem,
    send_sem,
    recv_sem,
    factor_send,
    factor_recv,
):
    p, q = lax.axis_index("path"), lax.axis_index("width")
    blocks = lax.axis_size("path")
    ahead, behind = lax.rem(p + 1, blocks), lax.rem(p + blocks - 1, blocks)
    mirror, across = blocks - 1 - p, 1 - q
    mirror_before = lax.rem(2 * blocks - 2 - p, blocks)
    mirror_after = lax.rem(blocks - p, blocks)

    barrier = pltpu.get_barrier_semaphore()

    def greet(partner):
        pl.semaphore_signal(barrier, inc=1, device_id=partner, device_id_type=pl.DeviceIdType.MESH)

    greet({"path": mirror, "width": across})
    greet({"path": mirror})

    @pl.when(mirror_before != p)
    def _():
        greet({"path": mirror_before})

    @pl.when(mirror_after != p)
    def _():
        greet({"path": mirror_after})

    greet({"path": behind})
    greet({"path": ahead})
    greet({"path": behind, "width": across})
    greet({"path": ahead, "width": across})
    greet({"width": across})

    loads = [
        pltpu.make_async_copy(adj_hbm, state, load_sem.at[0]),
        pltpu.make_async_copy(vel_hbm, vel, load_sem.at[1]),
        pltpu.make_async_copy(adj_hbm, adj, load_sem.at[2]),
        pltpu.make_async_copy(kappa_hbm, kappa_ref, load_sem.at[4]),
        pltpu.make_async_copy(pair_hbm, pair_ref, load_sem.at[5]),
        pltpu.make_async_copy(matrix_hbm, matrix_ref, load_sem.at[6]),
        pltpu.make_async_copy(weight_hbm, weight, load_sem.at[7]),
    ]
    for load in loads:
        load.start()

    lane = lax.broadcasted_iota(jnp.int32, (8, 128), 1)
    level = lax.broadcasted_iota(jnp.int32, (8, 128), 0)
    width_lane = lane & 7
    first_row = (lane & 8) == 0
    row_lane = (lane >> 3) & 1
    layer = lane >> 4
    edge = 7 * (1 - q)
    edge_sign = (1 - 2 * q).astype(F32)
    other_edge = 7 * q
    side_lanes = lane - width_lane + edge
    other_side_lanes = lane - width_lane + other_edge
    foot_lanes = lane & 15

    def rolled(value, shift):
        return pltpu.roll(value, lax.rem(shift + 256, 128), 1)

    def remote(turn, kind, src, dst, device):
        return pltpu.make_async_remote_copy(
            src_ref=src,
            dst_ref=dst,
            send_sem=send_sem.at[turn, kind],
            recv_sem=recv_sem.at[turn, kind],
            device_id=device,
            device_id_type=pl.DeviceIdType.MESH,
        )

    def move(turn, kind):
        later = kind >= LATER
        direct = kind - LATER if later else kind
        pair, line = pl.ds(2 * later, 2), pl.ds(8 * later, 8)
        if direct == WALL:
            device = {"path": mirror}
            return remote(turn, kind, wall_out.at[turn, pair], wall_in.at[turn, pair], device)
        if direct == BEHIND:
            device = {"path": ahead}
            return remote(turn, kind, path_out.at[turn, 0, line], path_in.at[turn, 0, line], device)
        if direct == AHEAD:
            device = {"path": behind}
            return remote(turn, kind, path_out.at[turn, 1, line], path_in.at[turn, 1, line], device)
        if direct == ACROSS:
            device = {"width": across}
            return remote(turn, kind, side_out.at[turn, pair], side_in.at[turn, pair], device)
        if kind == CROSS_BEHIND:
            device = {"path": ahead, "width": across}
            return remote(turn, kind, cross_out.at[turn, 0], cross_in.at[turn, 0], device)
        if kind == CROSS_AHEAD:
            device = {"path": behind, "width": across}
            return remote(turn, kind, cross_out.at[turn, 1], cross_in.at[turn, 1], device)
        if kind == WALL_AHEAD:
            device = {"path": mirror_before}
            return remote(turn, kind, foot_out.at[turn, 0], foot_in.at[turn, 0], device)
        if kind == WALL_BEHIND:
            device = {"path": mirror_after}
            return remote(turn, kind, foot_out.at[turn, 1], foot_in.at[turn, 1], device)
        device = {"path": mirror, "width": across}
        return remote(turn, kind, far_out.at[turn], far_in.at[turn], device)

    def factor_move(kind):
        first, count, device = {
            WALL: (SIDE_V, 4, {"path": mirror}),
            BEHIND: (PATH_SIDE, 7, {"path": ahead}),
            AHEAD: (LOWER_V, 7, {"path": behind}),
            ACROSS: (EDGE_V, 4, {"width": across}),
        }[kind]
        return pltpu.make_async_remote_copy(
            src_ref=factor_out.at[pl.ds(first, count)],
            dst_ref=factor_in.at[kind, pl.ds(first, count)],
            send_sem=factor_send.at[kind],
            recv_sem=factor_recv.at[kind],
            device_id=device,
            device_id_type=pl.DeviceIdType.MESH,
        )

    def wall_guard(kind):
        return (mirror_before if kind == WALL_AHEAD else mirror_after) != p

    def send(turn, kinds):
        for kind in kinds:
            if kind in (WALL_AHEAD, WALL_BEHIND):
                side = kind - WALL_AHEAD

                @pl.when(wall_guard(kind))
                def _():
                    move(turn, kind).start()

                @pl.when(jnp.logical_not(wall_guard(kind)))
                def _():
                    foot_in[turn, side] = foot_out[turn, side]
            else:
                move(turn, kind).start()

    def receive(turn, kind):
        if kind in (WALL_AHEAD, WALL_BEHIND):

            @pl.when(wall_guard(kind))
            def _():
                move(turn, kind).wait_recv()
        else:
            move(turn, kind).wait_recv()

    def traces_z():
        for a in range(8):
            low, high = end_slopes([state[face(a, c), :] for c in range(8)])
            slope_z[0, a] = low
            slope_z[1, a] = high

    def traces_s():
        for b in range(8):
            low, high = end_slopes([state[rows(a, b), :] for a in range(8)])
            slope_s[0, b] = low
            slope_s[1, b] = high

    def traces_w():
        for a in range(8):
            low, high = end_slopes([state[rows(a, b), :] for b in range(8)])
            slope_w[0, a] = low
            slope_w[1, a] = high

    def traces():
        traces_z()
        traces_s()
        traces_w()

    def by_layer(values):
        packed = values[0]
        for i in range(1, 8):
            packed = jnp.where(layer == i, turned(values[i], 16 * i), packed)
        return packed

    def by_width(values):
        packed = rolled(values[0], 0 - edge)
        for i in range(1, 8):
            packed = jnp.where(width_lane == i, rolled(values[i], i - edge), packed)
        return packed

    def pack_wall(turn, second):
        wall_out[turn, 2 * second] = by_layer([state[face(a, 0), :] for a in range(8)])
        wall_out[turn, 2 * second + 1] = by_layer([slope_z[0, a] for a in range(8)])

    def pack_side(turn, second):
        side_out[turn, 2 * second] = by_width([state[rows(a, edge), :] for a in range(8)])
        side_out[turn, 2 * second + 1] = by_width([slope_w[1 - q, a] for a in range(8)])

    def pack_path(turn, second):
        for b in range(8):
            path_out[turn, 0, 8 * second + b] = jnp.where(
                first_row, turned(slope_s[1, b], 120), state[rows(7, b), :]
            )
            path_out[turn, 1, 8 * second + b] = jnp.where(
                first_row, state[rows(0, b), :], turned(slope_s[0, b], 8)
            )

    def pack_far(turn):
        far_out[turn, 0] = wall_out[turn, 0]
        far_out[turn, 1] = wall_out[turn, 1]
        far_out[turn, 2] = jnp.where(layer == 0, side_out[turn, 0], turned(side_out[turn, 1], 16))

    def pack_foot(turn):
        for side in range(2):
            foot_out[turn, side, 0] = wall_out[turn, 0]
            foot_out[turn, side, 1] = wall_out[turn, 1]
            foot_out[turn, side, 2] = by_layer([path_out[turn, side, b] for b in range(8)])

    def pack_cross(turn):
        value, slope = side_out[turn, 0], side_out[turn, 1]
        for side in range(2):
            cross_out[turn, side, 0] = by_width([path_out[turn, side, b] for b in range(8)])
        cross_out[turn, 0, 1] = jnp.where(first_row, turned(slope, 120), value)
        cross_out[turn, 1, 1] = jnp.where(first_row, value, turned(slope, 8))

    def prepare(kappa, wall_index):
        base = kappa * 112.0
        for i in range(8):
            lift_s[0, i] = base - 28.0 * vel[rows(0, i), :]
            lift_s[1, i] = base + 28.0 * vel[rows(7, i), :]
            lift_w[0, i] = base - 28.0 * vel[rows(8 + i, 0), :]
            lift_w[1, i] = base + 28.0 * vel[rows(8 + i, 7), :]
            lift_z[0, i] = base - 28.0 * vel[face(16 + i, 0), :]
            lift_z[1, i] = base + 28.0 * vel[face(16 + i, 7), :]
        slope = kappa * 28.0
        inside = jnp.where(first_row, p, blocks - 1 - p) > 0
        path_g = jnp.where(inside, jnp.where(first_row, 0.0 - slope, slope), 0.0)
        for b in range(8):
            lift = jnp.where(first_row, lift_s[0, b], lift_s[1, b])
            path_v[b] = jnp.where(inside, lift, 0.0)
        on_path = [path_v[b] for b in range(8)]
        for k in range(4):
            one, two = on_path[2 * k], on_path[2 * k + 1]
            factor_out[LOWER_V + k] = jnp.where(first_row, one, turned(two, 8))
            factor_out[UPPER_V + k] = jnp.where(first_row, turned(two, 120), one)
        side = by_width([lift_w[1 - q, a] for a in range(8)])
        wall = by_layer([lift_z[0, a] for a in range(8)])
        told = jnp.where(level == 0, wall_index.astype(F32), jnp.where(level == 1, path_g, slope))
        for at in (PATH_SIDE, SIDE_V):
            factor_out[at] = side
            factor_out[at + 1] = wall
            factor_out[at + 2] = told
        factor_out[EDGE_V] = by_width(on_path)
        factor_out[FOOT_V] = by_layer(on_path)
        slope_factor[SIDE_G] = lanes_moved(slope * edge_sign, side_lanes)
        slope_factor[WALL_G] = lanes_moved(slope, foot_lanes)
        slope_factor[PATH_G] = path_g

    def told_row(kind, at, row):
        return jnp.broadcast_to(factor_in[kind, at, row : row + 1], (8, 128))

    def learn():
        for kind, at, side in (
            (AHEAD, PATH_ROWS, AHEAD_SIDE),
            (BEHIND, PATH_ROWS, BEHIND_SIDE),
            (WALL, ROWS, MIRROR_SIDE),
        ):
            slope = told_row(kind, at, 2)
            slope_factor[side] = lanes_moved(slope * edge_sign, side_lanes)
            slope_factor[side + 1] = lanes_moved(slope, foot_lanes)
        slope = told_row(ACROSS, ROWS, 2)
        slope_factor[ACROSS_SIDE] = 0.0 - lanes_moved(slope * edge_sign, other_side_lanes)
        slope_factor[ACROSS_WALL] = lanes_moved(slope, foot_lanes)
        slope_factor[ACROSS_EDGE] = lanes_moved(told_row(ACROSS, ROWS, 1), other_side_lanes)
        slope_factor[MIRROR_FOOT] = lanes_moved(told_row(WALL, ROWS, 1), foot_lanes)

    def local_rates(step, kappa):
        for b in range(8):
            line = [state[rows(a, b), :] for a in range(8)]
            even = [line[j] + line[7 - j] for j in range(4)]
            odd = [line[j] - line[7 - j] for j in range(4)]
            for i in range(4):
                for_even, for_odd = halves(ADVECT[i])
                left, right = weighted(for_even, even), weighted(for_odd, odd)
                for_even, for_odd = halves(SPREAD[i])
                inner, outer = weighted(for_even, even), weighted(for_odd, odd)
                near = vel[rows(i, b), :] * (left + right) + kappa * (inner + outer)
                far = vel[rows(7 - i, b), :] * (right - left) + kappa * (inner - outer)
                if i == 0:
                    lower = lift_s[0, b] * pltpu.roll(line[7], 8, 1) - (kappa * 28.0) * pltpu.roll(
                        slope_s[1, b], 8, 1
                    )
                    upper = lift_s[1, b] * pltpu.roll(line[0], 120, 1) + (
                        kappa * 28.0
                    ) * pltpu.roll(slope_s[0, b], 120, 1)
                    near = near + jnp.where(first_row, 0.0, lower)
                    far = far + jnp.where(first_row, upper, 0.0)
                rate[rows(i, b), :] = near
                rate[rows(7 - i, b), :] = far
        for pair in range(4):
            both = range(2 * pair, 2 * pair + 2)
            planes = [state[pl.ds(64 * a, 64), :] for a in both]
            plane = jnp.concatenate(planes, axis=1)
            high = plane.astype(BF16)
            low = (plane - high.astype(F32)).astype(BF16)
            stacked = jnp.concatenate([high, low, high], axis=0)
            product = jnp.dot(matrix_ref[...], stacked, preferred_element_type=F32)
            for k, a in enumerate(both):
                block = product[:, 128 * k : 128 * (k + 1)]
                bottom, top = state[face(a, 0), :], state[face(a, 7), :]
                first, last = state[rows(a, 0), :], state[rows(a, 7), :]
                for b in range(8):
                    at = slice(8 * b, 8 * b + 8)
                    value = (
                        rate[rows(a, b), :]
                        + vel[rows(8 + a, b), :] * block[0:64][at]
                        + vel[rows(16 + a, b), :] * block[64:128][at]
                        + kappa * block[128:192][at]
                    )
                    if b == 0:
                        lower = lift_w[0, a] * pltpu.roll(last, 1, 1) - (
                            kappa * 28.0
                        ) * pltpu.roll(slope_w[1, a], 1, 1)
                        value = value + jnp.where(width_lane == 0, 0.0, lower)
                    if b == 7:
                        upper = lift_w[1, a] * pltpu.roll(first, 127, 1) + (
                            kappa * 28.0
                        ) * pltpu.roll(slope_w[0, a], 127, 1)
                        value = value + jnp.where(width_lane == 7, 0.0, upper)
                    state[rows(a, b), :] = adj[rows(a, b), :] + step * value
                lower = lift_z[0, a] * pltpu.roll(top, 16, 1) - (kappa * 28.0) * pltpu.roll(
                    slope_z[1, a], 16, 1
                )
                upper = lift_z[1, a] * pltpu.roll(bottom, 112, 1) + (kappa * 28.0) * pltpu.roll(
                    slope_z[0, a], 112, 1
                )
                state[face(a, 0), :] += step * jnp.where(layer == 0, 0.0, lower)
                state[face(a, 7), :] += step * jnp.where(layer == 7, 0.0, upper)

    def far_rates(turn, second, step, kappa, wall_index):
        at = 2 * second
        change = step * (
            factor_out[SIDE_V] * side_in[turn, at] + slope_factor[SIDE_G] * side_in[turn, at + 1]
        )
        for a in range(8):
            moved = rolled(change, edge - a)
            state[rows(a, edge), :] += jnp.where(width_lane == edge, moved, 0.0)
        path_g = slope_factor[PATH_G]
        lower_lanes = first_row & (p > 0)
        upper_lanes = jnp.logical_not(first_row) & (p < blocks - 1)
        for b in range(8):
            packet = path_in[turn, 0, 8 * second + b]
            change = path_v[b] * pltpu.roll(packet, 120, 1) + path_g * packet
            state[rows(0, b), :] += jnp.where(lower_lanes, step * change, 0.0)
            packet = path_in[turn, 1, 8 * second + b]
            change = path_v[b] * pltpu.roll(packet, 8, 1) + path_g * packet
            state[rows(7, b), :] += jnp.where(upper_lanes, step * change, 0.0)
        value = lanes_moved(wall_in[turn, at], wall_index)
        slope = lanes_moved(wall_in[turn, at + 1], wall_index)
        change = step * (factor_out[WALL_V] * value + slope_factor[WALL_G] * slope)
        for a in range(8):
            moved = turned(change, 0 - 16 * a)
            state[face(a, 0), :] += jnp.where(layer == 0, moved, 0.0)

    def lane_sum(value):
        for apart in (1, 2, 4):
            value = value + turned(value, 0 - apart)
        return value

    def layer_sum(value):
        for apart in (16, 32, 64):
            value = value + turned(value, apart)
        return value

    def level_sum(value):
        return jnp.broadcast_to(jnp.sum(value, axis=0, keepdims=True), (8, 128))

    def reflect(turn, step):
        low, high = float(SLOPE[0, 0]), float(SLOPE[7, 7])
        ahead_g, behind_g = told_row(AHEAD, PATH_ROWS, 1), told_row(BEHIND, PATH_ROWS, 1)
        for b in range(8):
            packet = path_out[turn, 0, b]
            lift = factor_in[AHEAD, LOWER_V + b // 2]
            lift = turned(lift, 120) if b % 2 else lift
            change = lift * turned(packet, 120) + ahead_g * packet
            change = step * jnp.where(first_row, change, low * turned(change, 8))
            pending[b] = change
            packet = path_out[turn, 1, b]
            lift = factor_in[BEHIND, UPPER_V + b // 2]
            lift = turned(lift, 8) if b % 2 else lift
            change = lift * turned(packet, 8) + behind_g * packet
            change = step * jnp.where(first_row, high * turned(change, 120), change)
            pending[8 + b] = change
        change = step * (
            factor_in[ACROSS, SIDE_V] * side_out[turn, 0] + slope_factor[ACROSS_SIDE] * side_out[turn, 1]
        )
        pending[16] = change
        pending[17] = change * (edge_sign * low)
        index = told_row(WALL, ROWS, 0).astype(jnp.int32)
        change = step * (
            factor_in[WALL, WALL_V] * lanes_moved(wall_out[turn, 0], index)
            + slope_factor[MIRROR_WALL] * lanes_moved(wall_out[turn, 1], index)
        )
        pending[18] = change
        pending[19] = change * low

    def complete(turn, step, wall_index):
        for b in range(8):
            path_in[turn, 1, 8 + b] += pending[b]
            path_in[turn, 0, 8 + b] += pending[8 + b]
        packet = cross_in[turn, 1, 1]
        lower = factor_in[AHEAD, PATH_SIDE] * packet + slope_factor[AHEAD_SIDE] * turned(packet, 120)
        packet = cross_in[turn, 0, 1]
        upper = factor_in[BEHIND, PATH_SIDE] * packet + slope_factor[BEHIND_SIDE] * turned(packet, 8)
        change = step * jnp.where(first_row, lower, upper)
        slope = lane_sum(change * weight[0])
        lower = jnp.where(first_row, rolled(change, edge), rolled(slope, edge + 8))
        upper = jnp.where(first_row, rolled(slope, edge - 8), rolled(change, edge - 7))
        path_in[turn, 1, 8 + edge] += jnp.where(width_lane == edge, lower, 0.0)
        path_in[turn, 0, 8 + edge] += jnp.where(width_lane == edge, upper, 0.0)
        index = told_row(AHEAD, PATH_ROWS, 0).astype(jnp.int32)
        lower = factor_in[AHEAD, PATH_WALL] * lanes_moved(foot_in[turn, 0, 0], index) + slope_factor[
            AHEAD_WALL
        ] * lanes_moved(foot_in[turn, 0, 1], index)
        index = told_row(BEHIND, PATH_ROWS, 0).astype(jnp.int32)
        upper = factor_in[BEHIND, PATH_WALL] * lanes_moved(foot_in[turn, 1, 0], index) + slope_factor[
            BEHIND_WALL
        ] * lanes_moved(foot_in[turn, 1, 1], index)
        change = step * jnp.where(first_row, lower, upper)
        slope = layer_sum(change * weight[1])
        lower = jnp.where(first_row, change, turned(slope, 8))
        upper = jnp.where(first_row, turned(slope, 120), turned(change, 16))
        lower = jnp.where(layer == 0, lower, 0.0)
        upper = jnp.where(layer == 0, upper, 0.0)
        for b in range(8):
            path_in[turn, 1, 8 + b, 0:1] += lower[b : b + 1]
            path_in[turn, 0, 8 + b, 0:1] += upper[b : b + 1]
        value_side, slope_side = pending[16], pending[17]
        packet = cross_in[turn, 0, 0]
        lower = factor_in[ACROSS, EDGE_V] * turned(packet, 120) + slope_factor[ACROSS_EDGE] * packet
        packet = cross_in[turn, 1, 0]
        upper = factor_in[ACROSS, EDGE_V] * turned(packet, 8) + slope_factor[ACROSS_EDGE] * packet
        change = step * jnp.where(first_row, lower, upper)
        slope = lane_sum(change * weight[2 + q])
        at_first = first_row & (width_lane == 0)
        at_last = jnp.logical_not(first_row) & (width_lane == 7)
        value_side += jnp.where(at_first, rolled(change, 0 - other_edge), 0.0)
        value_side += jnp.where(at_last, rolled(change, 7 - other_edge), 0.0)
        slope_side += jnp.where(at_first, slope, 0.0) + jnp.where(at_last, turned(slope, 7), 0.0)
        change = step * (
            factor_in[ACROSS, WALL_V] * lanes_moved(far_in[turn, 0], wall_index)
            + slope_factor[ACROSS_WALL] * lanes_moved(far_in[turn, 1], wall_index)
        )
        index = 16 * width_lane + 8 * row_lane + other_edge
        value = lanes_moved(level_sum(jnp.where(level == other_edge, change, 0.0)), index)
        slope = lanes_moved(level_sum(change * weight[4 + q]), index)
        foot = (level == 0) & (layer == 0)
        side_in[turn, 2] += value_side + jnp.where(foot, value, 0.0)
        side_in[turn, 3] += slope_side + jnp.where(foot, slope, 0.0)
        value_wall, slope_wall = pending[18], pending[19]
        packet = foot_in[turn, 0, 2]
        lower = factor_in[WALL, FOOT_V] * turned(packet, 120) + slope_factor[MIRROR_FOOT] * packet
        packet = foot_in[turn, 1, 2]
        upper = factor_in[WALL, FOOT_V] * turned(packet, 8) + slope_factor[MIRROR_FOOT] * packet
        change = step * jnp.where(first_row, lower, upper)
        index = 16 * level + (lane & 15)
        value = lanes_moved(level_sum(jnp.where(level == 0, change, 0.0)), index)
        slope = lanes_moved(level_sum(change * weight[4]), index)
        ends = layer == 7 * row_lane
        value_wall += jnp.where(ends, value, 0.0)
        slope_wall += jnp.where(ends, slope, 0.0)
        packet = far_in[turn, 2]
        change = step * (
            factor_in[WALL, SIDE_V] * packet + slope_factor[MIRROR_SIDE] * turned(packet, 112)
        )
        index = 8 * row_lane + layer
        value = lanes_moved(level_sum(jnp.where(level == 0, change, 0.0)), index)
        slope = lanes_moved(level_sum(change * weight[4]), index)
        corner = (level == edge) & (width_lane == edge)
        wall_in[turn, 2] += value_wall + jnp.where(corner, value, 0.0)
        wall_in[turn, 3] += slope_wall + jnp.where(corner, slope, 0.0)

    for load in loads:
        load.wait()
    kappa = jnp.broadcast_to(kappa_ref[...], (8, 128))
    wall_index = jnp.zeros((8, 128), jnp.int32)
    for j in range(16):
        wall_index = jnp.where((lane & 15) == j, pair_ref[0, j], wall_index)
    wall_index = wall_index + 16 * (7 - layer)
    prepare(kappa, wall_index)

    steps = [TIME_STEP / 4.0, TIME_STEP / 3.0, TIME_STEP / 2.0, TIME_STEP]
    for turn in range(ROUNDS):
        step, next_step = steps[2 * turn], steps[2 * turn + 1]

        def begin(*kinds):
            if turn:
                send(turn, kinds)

        traces_z()
        pack_wall(turn, 0)
        traces_w()
        pack_side(turn, 0)
        pack_far(turn)
        begin(WALL_ACROSS, WALL)
        traces_s()
        pack_path(turn, 0)
        begin(BEHIND, AHEAD)
        pack_foot(turn)
        begin(WALL_AHEAD, WALL_BEHIND)
        pack_cross(turn)
        begin(CROSS_BEHIND, CROSS_AHEAD, ACROSS)
        local_rates(step, kappa)
        traces_z()
        pack_wall(turn, 1)
        begin(LATER + WALL)
        traces_s()
        pack_path(turn, 1)
        begin(LATER + BEHIND, LATER + AHEAD)
        traces_w()
        pack_side(turn, 1)
        begin(LATER + ACROSS)
        if turn:
            reflect(turn, step)
        else:
            meet = (mirror_before != p).astype(jnp.int32) + (mirror_after != p).astype(jnp.int32)
            pl.semaphore_wait(barrier, 7 + meet)
            send(turn, SENT)
            for kind in (WALL, BEHIND, AHEAD, ACROSS):
                factor_move(kind).start()
        for kind in (ACROSS, BEHIND, AHEAD, WALL):
            receive(turn, kind)
        far_rates(turn, 0, step, kappa, wall_index)
        traces()
        local_rates(next_step, kappa)
        if turn == 0:
            for kind in (WALL, BEHIND, AHEAD, ACROSS):
                factor_move(kind).wait_recv()
            learn()
            reflect(turn, step)
        for kind in SENT:
            if kind not in (ACROSS, BEHIND, AHEAD, WALL):
                receive(turn, kind)
        complete(turn, step, wall_index)
        far_rates(turn, 1, next_step, kappa, wall_index)
    for kind in (WALL, BEHIND, AHEAD, ACROSS):
        factor_move(kind).wait_send()
    for turn in range(ROUNDS):
        for kind in range(KINDS):
            if kind in (WALL_AHEAD, WALL_BEHIND):

                @pl.when(wall_guard(kind))
                def _():
                    move(turn, kind).wait_send()
            else:
                move(turn, kind).wait_send()


def shards(adjoint, velocity, diffusivity, wall_pair):
    tile = (8, 128)
    packets = [
        pltpu.VMEM((8,) + tile, F32),
        pltpu.VMEM((13,) + tile, F32),
        pltpu.VMEM((20,) + tile, F32),
        pltpu.VMEM((FACTORS,) + tile, F32),
        pltpu.VMEM((4, FACTORS) + tile, F32),
    ]
    for shape in ((2, 16), (4,), (4,), (2, 2), (2, 3), (3,)):
        packets += [pltpu.VMEM((ROUNDS,) + shape + tile, F32)] * 2
    operands = (
        adjoint.reshape(512, 128),
        velocity.reshape(1536, 128),
        diffusivity,
        wall_pair,
        jnp.asarray(plane_matrix()),
        jnp.asarray(weight_rows()),
    )
    result = pl.pallas_call(
        kernel,
        out_shape=jax.ShapeDtypeStruct((512, 128), F32),
        in_specs=[pl.BlockSpec(memory_space=pltpu.HBM)] * 6,
        out_specs=pl.BlockSpec(memory_space=pltpu.VMEM),
        scratch_shapes=[
            pltpu.VMEM((1, 128), F32),
            pltpu.SMEM((1, 16), jnp.int32),
            pltpu.VMEM((192, 192), BF16),
            pltpu.VMEM((6,) + tile, F32),
            pltpu.VMEM((512, 128), F32),
            pltpu.VMEM((1536, 128), F32),
            pltpu.VMEM((512, 128), F32),
        ]
        + [pltpu.VMEM((2, 8) + tile, F32)] * 6
        + packets
        + [
            pltpu.SemaphoreType.DMA((8,)),
            pltpu.SemaphoreType.DMA((ROUNDS, KINDS)),
            pltpu.SemaphoreType.DMA((ROUNDS, KINDS)),
            pltpu.SemaphoreType.DMA((4,)),
            pltpu.SemaphoreType.DMA((4,)),
        ],
        compiler_params=pltpu.CompilerParams(
            collective_id=0, has_side_effects=True, vmem_limit_bytes=32 * 1024 * 1024
        ),
        name="plate_step",
    )(*(pltpu.with_memory_space_constraint(array, pltpu.HBM) for array in operands))
    return result.reshape(adjoint.shape)


def solution(mesh):
    placed = (
        P("width", None, None, None, "path"),
        P(None, "width", None, None, None, "path"),
        P("width", "path"),
        P("path", None),
    )
    return jax.shard_map(
        shards,
        mesh=mesh,
        in_specs=placed,
        out_specs=P("width", None, None, None, "path"),
        check_vma=False,
    )
```

```python
import functools

import jax
import jax.numpy as jnp
import numpy as np
from jax import lax
from jax.experimental import pallas as pl
from jax.experimental.pallas import tpu as pltpu
from jax.sharding import PartitionSpec as P

TIME_STEP = 0.004
ROUNDS = 2
INNER_POINTS = (
    -0.8717401485096066,
    -0.5917001814331423,
    -0.2092992179024789,
    0.2092992179024789,
    0.5917001814331423,
    0.8717401485096066,
)
F32 = jnp.float32
BF16 = jnp.bfloat16
WALL, BEHIND, AHEAD, ACROSS, CROSS_BEHIND, CROSS_AHEAD, WALL_AHEAD, WALL_BEHIND, WALL_ACROSS = range(9)
LATER = 9
KINDS = 13
SENT = (WALL_ACROSS, WALL, WALL_AHEAD, WALL_BEHIND, BEHIND, AHEAD, LATER + WALL) + (
    CROSS_BEHIND,
    CROSS_AHEAD,
    ACROSS,
    LATER + BEHIND,
    LATER + AHEAD,
    LATER + ACROSS,
)
LOWER_V, LOWER_ENDS, PATH_ROWS, UPPER_ENDS, UPPER_V, EDGE_V, SIDE_V, WALL_V, ROWS, FOOT_V = 0, 4, 5, 6, 7, 11, 12, 13, 14, 15
FACTORS = 16
SIDE_G, WALL_G, PATH_G, AHEAD_SIDE, AHEAD_WALL, BEHIND_SIDE, BEHIND_WALL, ACROSS_SIDE, ACROSS_WALL, ACROSS_EDGE = range(10)
MIRROR_SIDE, MIRROR_WALL, MIRROR_FOOT = range(10, 13)


def legendre_seven(points):
    before = np.ones(points.shape)
    current = points * 1.0
    for order in range(1, 7):
        after = ((2.0 * order + 1.0) * points * current - order * before) / (order + 1.0)
        before = current
        current = after
    return current


def lobatto_table():
    degree = 7
    points = np.array((-1.0,) + INNER_POINTS + (1.0,))
    values = legendre_seven(points)
    table = np.zeros((degree + 1, degree + 1))
    for i in range(degree + 1):
        for j in range(degree + 1):
            if i != j:
                table[i, j] = values[i] / (values[j] * (points[i] - points[j]))
    table[0, 0] = -degree * (degree + 1) / 4.0
    table[degree, degree] = degree * (degree + 1) / 4.0
    return table


SLOPE = 2.0 * lobatto_table()
ADVECT = SLOPE.copy()
ADVECT[0, 0] += 28.0
ADVECT[7, 7] -= 28.0
SPREAD = SLOPE @ SLOPE
SPREAD[0] += 28.0 * SLOPE[0]
SPREAD[0, 0] -= 112.0
SPREAD[7] -= 28.0 * SLOPE[7]
SPREAD[7, 7] -= 112.0


def plane_matrix():
    eye = np.eye(8)
    full = np.concatenate(
        [np.kron(ADVECT, eye), np.kron(eye, ADVECT), np.kron(SPREAD, eye) + np.kron(eye, SPREAD)]
    )
    high = full.astype(jnp.bfloat16)
    low = (full - high.astype(np.float64)).astype(jnp.bfloat16)
    return np.concatenate([high, high, low], axis=1)


def weight_rows():
    lane = np.arange(128)
    second, width, layer = (lane >> 3) & 1, lane & 7, lane >> 4
    last = np.where(second[None] == 1, 7, 0)[0]
    flat = [SLOPE[last, width], SLOPE[last, layer], SLOPE[0, width], SLOPE[7, width]]
    wide = [np.broadcast_to(row, (8, 128)) for row in flat]
    tall = [np.broadcast_to(SLOPE[k][:, None], (8, 128)) for k in (0, 7)]
    return np.stack(wide + tall).astype(np.float32)


def halves(row):
    even = [float((row[j] + row[7 - j]) / 2) for j in range(4)]
    odd = [float((row[j] - row[7 - j]) / 2) for j in range(4)]
    return even, odd


def weighted(factors, values):
    total = values[0] * factors[0]
    for j in range(1, 4):
        total = total + values[j] * factors[j]
    return total


def end_slopes(line):
    even = [line[j] + line[7 - j] for j in range(4)]
    odd = [line[j] - line[7 - j] for j in range(4)]
    for_even, for_odd = halves(SLOPE[0])
    left, right = weighted(for_even, even), weighted(for_odd, odd)
    return left + right, right - left


def rows(a, b):
    return pl.ds((a * 8 + b) * 8, 8)


def face(a, c):
    return pl.ds(a * 64 + c, 8, stride=8)


def lanes_moved(value, index):
    return jnp.take_along_axis(value, index, axis=1)


def turned(value, shift):
    return pltpu.roll(value, shift % 128, 1) if shift % 128 else value


def kernel(
    adj_hbm,
    vel_hbm,
    kappa_hbm,
    pair_hbm,
    matrix_hbm,
    weight_hbm,
    state,
    kappa_ref,
    pair_ref,
    matrix_ref,
    weight,
    adj,
    vel,
    rate,
    slope_s,
    slope_w,
    slope_z,
    lift_s,
    lift_w,
    lift_z,
    path_v,
    slope_factor,
    pending,
    factor_out,
    factor_in,
    path_out,
    path_in,
    wall_out,
    wall_in,
    side_out,
    side_in,
    cross_out,
    cross_in,
    foot_out,
    foot_in,
    far_out,
    far_in,
    load_sem,
    send_sem,
    recv_sem,
    factor_send,
    factor_recv,
):
    p, q = lax.axis_index("path"), lax.axis_index("width")
    blocks = lax.axis_size("path")
    ahead, behind = lax.rem(p + 1, blocks), lax.rem(p + blocks - 1, blocks)
    mirror, across = blocks - 1 - p, 1 - q
    mirror_before = lax.rem(2 * blocks - 2 - p, blocks)
    mirror_after = lax.rem(blocks - p, blocks)

    barrier = pltpu.get_barrier_semaphore()

    def greet(partner):
        pl.semaphore_signal(barrier, inc=1, device_id=partner, device_id_type=pl.DeviceIdType.MESH)

    greet({"path": mirror, "width": across})
    greet({"path": mirror})

    @pl.when(mirror_before != p)
    def _():
        greet({"path": mirror_before})

    @pl.when(mirror_after != p)
    def _():
        greet({"path": mirror_after})

    greet({"path": behind})
    greet({"path": ahead})
    greet({"path": behind, "width": across})
    greet({"path": ahead, "width": across})
    greet({"width": across})

    loads = [
        pltpu.make_async_copy(adj_hbm, state, load_sem.at[0]),
        pltpu.make_async_copy(vel_hbm, vel, load_sem.at[1]),
        pltpu.make_async_copy(adj_hbm, adj, load_sem.at[2]),
        pltpu.make_async_copy(kappa_hbm, kappa_ref, load_sem.at[4]),
        pltpu.make_async_copy(pair_hbm, pair_ref, load_sem.at[5]),
        pltpu.make_async_copy(matrix_hbm, matrix_ref, load_sem.at[6]),
        pltpu.make_async_copy(weight_hbm, weight, load_sem.at[7]),
    ]
    for load in loads:
        load.start()

    lane = lax.broadcasted_iota(jnp.int32, (8, 128), 1)
    level = lax.broadcasted_iota(jnp.int32, (8, 128), 0)
    width_lane = lane & 7
    first_row = (lane & 8) == 0
    row_lane = (lane >> 3) & 1
    layer = lane >> 4
    edge = 7 * (1 - q)
    edge_sign = (1 - 2 * q).astype(F32)
    other_edge = 7 * q
    side_lanes = lane - width_lane + edge
    other_side_lanes = lane - width_lane + other_edge
    foot_lanes = lane & 15

    def rolled(value, shift):
        return pltpu.roll(value, lax.rem(shift + 256, 128), 1)

    def remote(turn, kind, src, dst, device):
        return pltpu.make_async_remote_copy(
            src_ref=src,
            dst_ref=dst,
            send_sem=send_sem.at[turn, kind],
            recv_sem=recv_sem.at[turn, kind],
            device_id=device,
            device_id_type=pl.DeviceIdType.MESH,
        )

    def move(turn, kind):
        later = kind >= LATER
        direct = kind - LATER if later else kind
        pair, line = pl.ds(2 * later, 2), pl.ds(8 * later, 8)
        if direct == WALL:
            device = {"path": mirror}
            return remote(turn, kind, wall_out.at[turn, pair], wall_in.at[turn, pair], device)
        if direct == BEHIND:
            device = {"path": ahead}
            return remote(turn, kind, path_out.at[turn, 0, line], path_in.at[turn, 0, line], device)
        if direct == AHEAD:
            device = {"path": behind}
            return remote(turn, kind, path_out.at[turn, 1, line], path_in.at[turn, 1, line], device)
        if direct == ACROSS:
            device = {"width": across}
            return remote(turn, kind, side_out.at[turn, pair], side_in.at[turn, pair], device)
        if kind == CROSS_BEHIND:
            device = {"path": ahead, "width": across}
            return remote(turn, kind, cross_out.at[turn, 0], cross_in.at[turn, 0], device)
        if kind == CROSS_AHEAD:
            device = {"path": behind, "width": across}
            return remote(turn, kind, cross_out.at[turn, 1], cross_in.at[turn, 1], device)
        if kind == WALL_AHEAD:
            device = {"path": mirror_before}
            return remote(turn, kind, foot_out.at[turn, 0], foot_in.at[turn, 0], device)
        if kind == WALL_BEHIND:
            device = {"path": mirror_after}
            return remote(turn, kind, foot_out.at[turn, 1], foot_in.at[turn, 1], device)
        device = {"path": mirror, "width": across}
        return remote(turn, kind, far_out.at[turn], far_in.at[turn], device)

    def factor_move(kind):
        first, count, device = {
            WALL: (SIDE_V, 4, {"path": mirror}),
            BEHIND: (PATH_ROWS, 6, {"path": ahead}),
            AHEAD: (LOWER_V, 6, {"path": behind}),
            ACROSS: (EDGE_V, 4, {"width": across}),
        }[kind]
        return pltpu.make_async_remote_copy(
            src_ref=factor_out.at[pl.ds(first, count)],
            dst_ref=factor_in.at[kind, pl.ds(first, count)],
            send_sem=factor_send.at[kind],
            recv_sem=factor_recv.at[kind],
            device_id=device,
            device_id_type=pl.DeviceIdType.MESH,
        )

    def wall_guard(kind):
        return (mirror_before if kind == WALL_AHEAD else mirror_after) != p

    def send(turn, kinds):
        for kind in kinds:
            if kind in (WALL_AHEAD, WALL_BEHIND):
                side = kind - WALL_AHEAD

                @pl.when(wall_guard(kind))
                def _():
                    move(turn, kind).start()

                @pl.when(jnp.logical_not(wall_guard(kind)))
                def _():
                    foot_in[turn, side] = foot_out[turn, side]
            else:
                move(turn, kind).start()

    def receive(turn, kind):
        if kind in (WALL_AHEAD, WALL_BEHIND):

            @pl.when(wall_guard(kind))
            def _():
                move(turn, kind).wait_recv()
        else:
            move(turn, kind).wait_recv()

    def traces_z():
        for a in range(8):
            low, high = end_slopes([state[face(a, c), :] for c in range(8)])
            slope_z[0, a] = low
            slope_z[1, a] = high

    def traces_s():
        for b in range(8):
            low, high = end_slopes([state[rows(a, b), :] for a in range(8)])
            slope_s[0, b] = low
            slope_s[1, b] = high

    def traces_w():
        for a in range(8):
            low, high = end_slopes([state[rows(a, b), :] for b in range(8)])
            slope_w[0, a] = low
            slope_w[1, a] = high

    def traces():
        traces_z()
        traces_s()
        traces_w()

    def by_layer(values):
        packed = values[0]
        for i in range(1, 8):
            packed = jnp.where(layer == i, turned(values[i], 16 * i), packed)
        return packed

    def by_width(values):
        packed = rolled(values[0], 0 - edge)
        for i in range(1, 8):
            packed = jnp.where(width_lane == i, rolled(values[i], i - edge), packed)
        return packed

    def pack_wall(turn, second):
        wall_out[turn, 2 * second] = by_layer([state[face(a, 0), :] for a in range(8)])
        wall_out[turn, 2 * second + 1] = by_layer([slope_z[0, a] for a in range(8)])

    def pack_side(turn, second):
        side_out[turn, 2 * second] = by_width([state[rows(a, edge), :] for a in range(8)])
        side_out[turn, 2 * second + 1] = by_width([slope_w[1 - q, a] for a in range(8)])

    def pack_path(turn, second):
        for b in range(8):
            path_out[turn, 0, 8 * second + b] = jnp.where(
                first_row, turned(slope_s[1, b], 120), state[rows(7, b), :]
            )
            path_out[turn, 1, 8 * second + b] = jnp.where(
                first_row, state[rows(0, b), :], turned(slope_s[0, b], 8)
            )

    def pack_far(turn):
        far_out[turn, 0] = wall_out[turn, 0]
        far_out[turn, 1] = wall_out[turn, 1]
        far_out[turn, 2] = jnp.where(layer == 0, side_out[turn, 0], turned(side_out[turn, 1], 16))

    def pack_foot(turn):
        for side in range(2):
            foot_out[turn, side, 0] = wall_out[turn, 0]
            foot_out[turn, side, 1] = wall_out[turn, 1]
            foot_out[turn, side, 2] = by_layer([path_out[turn, side, b] for b in range(8)])

    def pack_cross(turn):
        value, slope = side_out[turn, 0], side_out[turn, 1]
        for side in range(2):
            cross_out[turn, side, 0] = by_width([path_out[turn, side, b] for b in range(8)])
        cross_out[turn, 0, 1] = jnp.where(first_row, turned(slope, 120), value)
        cross_out[turn, 1, 1] = jnp.where(first_row, value, turned(slope, 8))

    def prepare(kappa, wall_index):
        base = kappa * 112.0
        for i in range(8):
            lift_s[0, i] = base - 28.0 * vel[rows(0, i), :]
            lift_s[1, i] = base + 28.0 * vel[rows(7, i), :]
            lift_w[0, i] = base - 28.0 * vel[rows(8 + i, 0), :]
            lift_w[1, i] = base + 28.0 * vel[rows(8 + i, 7), :]
            lift_z[0, i] = base - 28.0 * vel[face(16 + i, 0), :]
            lift_z[1, i] = base + 28.0 * vel[face(16 + i, 7), :]
        slope = kappa * 28.0
        inside = jnp.where(first_row, p, blocks - 1 - p) > 0
        path_g = jnp.where(inside, jnp.where(first_row, 0.0 - slope, slope), 0.0)
        for b in range(8):
            lift = jnp.where(first_row, lift_s[0, b], lift_s[1, b])
            path_v[b] = jnp.where(inside, lift, 0.0)
        on_path = [path_v[b] for b in range(8)]
        for k in range(4):
            one, two = on_path[2 * k], on_path[2 * k + 1]
            factor_out[LOWER_V + k] = jnp.where(first_row, one, turned(two, 8))
            factor_out[UPPER_V + k] = jnp.where(first_row, turned(two, 120), one)
        side = by_width([lift_w[1 - q, a] for a in range(8)])
        wall = by_layer([lift_z[0, a] for a in range(8)])
        told = jnp.where(level == 0, wall_index.astype(F32), jnp.where(level == 1, path_g, slope))
        factor_out[LOWER_ENDS] = jnp.where(first_row, side, turned(wall, 8))
        factor_out[UPPER_ENDS] = jnp.where(first_row, turned(wall, 120), side)
        factor_out[PATH_ROWS] = told
        factor_out[SIDE_V] = side
        factor_out[WALL_V] = wall
        factor_out[ROWS] = told
        factor_out[EDGE_V] = by_width(on_path)
        factor_out[FOOT_V] = by_layer(on_path)
        slope_factor[SIDE_G] = lanes_moved(slope * edge_sign, side_lanes)
        slope_factor[WALL_G] = lanes_moved(slope, foot_lanes)
        slope_factor[PATH_G] = path_g

    def told_row(kind, at, row):
        return jnp.broadcast_to(factor_in[kind, at, row : row + 1], (8, 128))

    def learn():
        for kind, at, side in (
            (AHEAD, PATH_ROWS, AHEAD_SIDE),
            (BEHIND, PATH_ROWS, BEHIND_SIDE),
            (WALL, ROWS, MIRROR_SIDE),
        ):
            slope = told_row(kind, at, 2)
            slope_factor[side] = lanes_moved(slope * edge_sign, side_lanes)
            slope_factor[side + 1] = lanes_moved(slope, foot_lanes)
        slope = told_row(ACROSS, ROWS, 2)
        slope_factor[ACROSS_SIDE] = 0.0 - lanes_moved(slope * edge_sign, other_side_lanes)
        slope_factor[ACROSS_WALL] = lanes_moved(slope, foot_lanes)
        slope_factor[ACROSS_EDGE] = lanes_moved(told_row(ACROSS, ROWS, 1), other_side_lanes)
        slope_factor[MIRROR_FOOT] = lanes_moved(told_row(WALL, ROWS, 1), foot_lanes)

    def local_rates(step, kappa):
        for b in range(8):
            line = [state[rows(a, b), :] for a in range(8)]
            even = [line[j] + line[7 - j] for j in range(4)]
            odd = [line[j] - line[7 - j] for j in range(4)]
            for i in range(4):
                for_even, for_odd = halves(ADVECT[i])
                left, right = weighted(for_even, even), weighted(for_odd, odd)
                for_even, for_odd = halves(SPREAD[i])
                inner, outer = weighted(for_even, even), weighted(for_odd, odd)
                near = vel[rows(i, b), :] * (left + right) + kappa * (inner + outer)
                far = vel[rows(7 - i, b), :] * (right - left) + kappa * (inner - outer)
                if i == 0:
                    lower = lift_s[0, b] * pltpu.roll(line[7], 8, 1) - (kappa * 28.0) * pltpu.roll(
                        slope_s[1, b], 8, 1
                    )
                    upper = lift_s[1, b] * pltpu.roll(line[0], 120, 1) + (
                        kappa * 28.0
                    ) * pltpu.roll(slope_s[0, b], 120, 1)
                    near = near + jnp.where(first_row, 0.0, lower)
                    far = far + jnp.where(first_row, upper, 0.0)
                rate[rows(i, b), :] = near
                rate[rows(7 - i, b), :] = far
        for pair in range(4):
            both = range(2 * pair, 2 * pair + 2)
            planes = [state[pl.ds(64 * a, 64), :] for a in both]
            plane = jnp.concatenate(planes, axis=1)
            high = plane.astype(BF16)
            low = (plane - high.astype(F32)).astype(BF16)
            stacked = jnp.concatenate([high, low, high], axis=0)
            product = jnp.dot(matrix_ref[...], stacked, preferred_element_type=F32)
            for k, a in enumerate(both):
                block = product[:, 128 * k : 128 * (k + 1)]
                bottom, top = state[face(a, 0), :], state[face(a, 7), :]
                first, last = state[rows(a, 0), :], state[rows(a, 7), :]
                for b in range(8):
                    at = slice(8 * b, 8 * b + 8)
                    value = (
                        rate[rows(a, b), :]
                        + vel[rows(8 + a, b), :] * block[0:64][at]
                        + vel[rows(16 + a, b), :] * block[64:128][at]
                        + kappa * block[128:192][at]
                    )
                    if b == 0:
                        lower = lift_w[0, a] * pltpu.roll(last, 1, 1) - (
                            kappa * 28.0
                        ) * pltpu.roll(slope_w[1, a], 1, 1)
                        value = value + jnp.where(width_lane == 0, 0.0, lower)
                    if b == 7:
                        upper = lift_w[1, a] * pltpu.roll(first, 127, 1) + (
                            kappa * 28.0
                        ) * pltpu.roll(slope_w[0, a], 127, 1)
                        value = value + jnp.where(width_lane == 7, 0.0, upper)
                    state[rows(a, b), :] = adj[rows(a, b), :] + step * value
                lower = lift_z[0, a] * pltpu.roll(top, 16, 1) - (kappa * 28.0) * pltpu.roll(
                    slope_z[1, a], 16, 1
                )
                upper = lift_z[1, a] * pltpu.roll(bottom, 112, 1) + (kappa * 28.0) * pltpu.roll(
                    slope_z[0, a], 112, 1
                )
                state[face(a, 0), :] += step * jnp.where(layer == 0, 0.0, lower)
                state[face(a, 7), :] += step * jnp.where(layer == 7, 0.0, upper)

    def far_rates(turn, second, step, kappa, wall_index):
        at = 2 * second
        change = step * (
            factor_out[SIDE_V] * side_in[turn, at] + slope_factor[SIDE_G] * side_in[turn, at + 1]
        )
        for a in range(8):
            moved = rolled(change, edge - a)
            state[rows(a, edge), :] += jnp.where(width_lane == edge, moved, 0.0)
        path_g = slope_factor[PATH_G]
        lower_lanes = first_row & (p > 0)
        upper_lanes = jnp.logical_not(first_row) & (p < blocks - 1)
        for b in range(8):
            packet = path_in[turn, 0, 8 * second + b]
            change = path_v[b] * pltpu.roll(packet, 120, 1) + path_g * packet
            state[rows(0, b), :] += jnp.where(lower_lanes, step * change, 0.0)
            packet = path_in[turn, 1, 8 * second + b]
            change = path_v[b] * pltpu.roll(packet, 8, 1) + path_g * packet
            state[rows(7, b), :] += jnp.where(upper_lanes, step * change, 0.0)
        value = lanes_moved(wall_in[turn, at], wall_index)
        slope = lanes_moved(wall_in[turn, at + 1], wall_index)
        change = step * (factor_out[WALL_V] * value + slope_factor[WALL_G] * slope)
        for a in range(8):
            moved = turned(change, 0 - 16 * a)
            state[face(a, 0), :] += jnp.where(layer == 0, moved, 0.0)

    def lane_sum(value):
        for apart in (1, 2, 4):
            value = value + turned(value, 0 - apart)
        return value

    def layer_sum(value):
        for apart in (16, 32, 64):
            value = value + turned(value, apart)
        return value

    def level_sum(value):
        return jnp.broadcast_to(jnp.sum(value, axis=0, keepdims=True), (8, 128))

    def reflect(turn, step):
        low, high = float(SLOPE[0, 0]), float(SLOPE[7, 7])
        ahead_g, behind_g = told_row(AHEAD, PATH_ROWS, 1), told_row(BEHIND, PATH_ROWS, 1)
        for b in range(8):
            packet = path_out[turn, 0, b]
            lift = factor_in[AHEAD, LOWER_V + b // 2]
            lift = turned(lift, 120) if b % 2 else lift
            change = lift * turned(packet, 120) + ahead_g * packet
            change = step * jnp.where(first_row, change, low * turned(change, 8))
            pending[b] = change
            packet = path_out[turn, 1, b]
            lift = factor_in[BEHIND, UPPER_V + b // 2]
            lift = turned(lift, 8) if b % 2 else lift
            change = lift * turned(packet, 8) + behind_g * packet
            change = step * jnp.where(first_row, high * turned(change, 120), change)
            pending[8 + b] = change
        change = step * (
            factor_in[ACROSS, SIDE_V] * side_out[turn, 0] + slope_factor[ACROSS_SIDE] * side_out[turn, 1]
        )
        pending[16] = change
        pending[17] = change * (edge_sign * low)
        index = told_row(WALL, ROWS, 0).astype(jnp.int32)
        change = step * (
            factor_in[WALL, WALL_V] * lanes_moved(wall_out[turn, 0], index)
            + slope_factor[MIRROR_WALL] * lanes_moved(wall_out[turn, 1], index)
        )
        pending[18] = change
        pending[19] = change * low

    def complete(turn, step, wall_index):
        for b in range(8):
            path_in[turn, 1, 8 + b] += pending[b]
            path_in[turn, 0, 8 + b] += pending[8 + b]
        packet = cross_in[turn, 1, 1]
        lower = factor_in[AHEAD, LOWER_ENDS] * packet + slope_factor[AHEAD_SIDE] * turned(packet, 120)
        packet = cross_in[turn, 0, 1]
        upper = factor_in[BEHIND, UPPER_ENDS] * packet + slope_factor[BEHIND_SIDE] * turned(packet, 8)
        change = step * jnp.where(first_row, lower, upper)
        slope = lane_sum(change * weight[0])
        lower = jnp.where(first_row, rolled(change, edge), rolled(slope, edge + 8))
        upper = jnp.where(first_row, rolled(slope, edge - 8), rolled(change, edge - 7))
        path_in[turn, 1, 8 + edge] += jnp.where(width_lane == edge, lower, 0.0)
        path_in[turn, 0, 8 + edge] += jnp.where(width_lane == edge, upper, 0.0)
        index = told_row(AHEAD, PATH_ROWS, 0).astype(jnp.int32)
        lower = turned(factor_in[AHEAD, LOWER_ENDS], 120) * lanes_moved(foot_in[turn, 0, 0], index) + slope_factor[
            AHEAD_WALL
        ] * lanes_moved(foot_in[turn, 0, 1], index)
        index = told_row(BEHIND, PATH_ROWS, 0).astype(jnp.int32)
        upper = turned(factor_in[BEHIND, UPPER_ENDS], 8) * lanes_moved(foot_in[turn, 1, 0], index) + slope_factor[
            BEHIND_WALL
        ] * lanes_moved(foot_in[turn, 1, 1], index)
        change = step * jnp.where(first_row, lower, upper)
        slope = layer_sum(change * weight[1])
        lower = jnp.where(first_row, change, turned(slope, 8))
        upper = jnp.where(first_row, turned(slope, 120), turned(change, 16))
        lower = jnp.where(layer == 0, lower, 0.0)
        upper = jnp.where(layer == 0, upper, 0.0)
        for b in range(8):
            path_in[turn, 1, 8 + b, 0:1] += lower[b : b + 1]
            path_in[turn, 0, 8 + b, 0:1] += upper[b : b + 1]
        value_side, slope_side = pending[16], pending[17]
        packet = cross_in[turn, 0, 0]
        lower = factor_in[ACROSS, EDGE_V] * turned(packet, 120) + slope_factor[ACROSS_EDGE] * packet
        packet = cross_in[turn, 1, 0]
        upper = factor_in[ACROSS, EDGE_V] * turned(packet, 8) + slope_factor[ACROSS_EDGE] * packet
        change = step * jnp.where(first_row, lower, upper)
        slope = lane_sum(change * weight[2 + q])
        at_first = first_row & (width_lane == 0)
        at_last = jnp.logical_not(first_row) & (width_lane == 7)
        value_side += jnp.where(at_first, rolled(change, 0 - other_edge), 0.0)
        value_side += jnp.where(at_last, rolled(change, 7 - other_edge), 0.0)
        slope_side += jnp.where(at_first, slope, 0.0) + jnp.where(at_last, turned(slope, 7), 0.0)
        change = step * (
            factor_in[ACROSS, WALL_V] * lanes_moved(far_in[turn, 0], wall_index)
            + slope_factor[ACROSS_WALL] * lanes_moved(far_in[turn, 1], wall_index)
        )
        index = 16 * width_lane + 8 * row_lane + other_edge
        value = lanes_moved(level_sum(jnp.where(level == other_edge, change, 0.0)), index)
        slope = lanes_moved(level_sum(change * weight[4 + q]), index)
        foot = (level == 0) & (layer == 0)
        side_in[turn, 2] += value_side + jnp.where(foot, value, 0.0)
        side_in[turn, 3] += slope_side + jnp.where(foot, slope, 0.0)
        value_wall, slope_wall = pending[18], pending[19]
        packet = foot_in[turn, 0, 2]
        lower = factor_in[WALL, FOOT_V] * turned(packet, 120) + slope_factor[MIRROR_FOOT] * packet
        packet = foot_in[turn, 1, 2]
        upper = factor_in[WALL, FOOT_V] * turned(packet, 8) + slope_factor[MIRROR_FOOT] * packet
        change = step * jnp.where(first_row, lower, upper)
        index = 16 * level + (lane & 15)
        value = lanes_moved(level_sum(jnp.where(level == 0, change, 0.0)), index)
        slope = lanes_moved(level_sum(change * weight[4]), index)
        ends = layer == 7 * row_lane
        value_wall += jnp.where(ends, value, 0.0)
        slope_wall += jnp.where(ends, slope, 0.0)
        packet = far_in[turn, 2]
        change = step * (
            factor_in[WALL, SIDE_V] * packet + slope_factor[MIRROR_SIDE] * turned(packet, 112)
        )
        index = 8 * row_lane + layer
        value = lanes_moved(level_sum(jnp.where(level == 0, change, 0.0)), index)
        slope = lanes_moved(level_sum(change * weight[4]), index)
        corner = (level == edge) & (width_lane == edge)
        wall_in[turn, 2] += value_wall + jnp.where(corner, value, 0.0)
        wall_in[turn, 3] += slope_wall + jnp.where(corner, slope, 0.0)

    for load in loads:
        load.wait()
    kappa = jnp.broadcast_to(kappa_ref[...], (8, 128))
    wall_index = jnp.zeros((8, 128), jnp.int32)
    for j in range(16):
        wall_index = jnp.where((lane & 15) == j, pair_ref[0, j], wall_index)
    wall_index = wall_index + 16 * (7 - layer)
    prepare(kappa, wall_index)

    steps = [TIME_STEP / 4.0, TIME_STEP / 3.0, TIME_STEP / 2.0, TIME_STEP]
    for turn in range(ROUNDS):
        step, next_step = steps[2 * turn], steps[2 * turn + 1]

        def begin(*kinds):
            if turn:
                send(turn, kinds)

        traces_z()
        pack_wall(turn, 0)
        traces_w()
        pack_side(turn, 0)
        pack_far(turn)
        begin(WALL_ACROSS, WALL)
        traces_s()
        pack_path(turn, 0)
        begin(BEHIND, AHEAD)
        pack_foot(turn)
        begin(WALL_AHEAD, WALL_BEHIND)
        pack_cross(turn)
        begin(CROSS_BEHIND, CROSS_AHEAD, ACROSS)
        local_rates(step, kappa)
        traces_z()
        pack_wall(turn, 1)
        begin(LATER + WALL)
        traces_s()
        pack_path(turn, 1)
        begin(LATER + BEHIND, LATER + AHEAD)
        traces_w()
        pack_side(turn, 1)
        begin(LATER + ACROSS)
        if turn:
            reflect(turn, step)
        else:
            meet = (mirror_before != p).astype(jnp.int32) + (mirror_after != p).astype(jnp.int32)
            pl.semaphore_wait(barrier, 7 + meet)
            send(turn, SENT)
            for kind in (WALL, BEHIND, AHEAD, ACROSS):
                factor_move(kind).start()
        for kind in (ACROSS, BEHIND, AHEAD, WALL):
            receive(turn, kind)
        far_rates(turn, 0, step, kappa, wall_index)
        traces()
        local_rates(next_step, kappa)
        if turn == 0:
            for kind in (WALL, BEHIND, AHEAD, ACROSS):
                factor_move(kind).wait_recv()
            learn()
            reflect(turn, step)
        for kind in SENT:
            if kind not in (ACROSS, BEHIND, AHEAD, WALL):
                receive(turn, kind)
        complete(turn, step, wall_index)
        far_rates(turn, 1, next_step, kappa, wall_index)
    for kind in (WALL, BEHIND, AHEAD, ACROSS):
        factor_move(kind).wait_send()
    for turn in range(ROUNDS):
        for kind in range(KINDS):
            if kind in (WALL_AHEAD, WALL_BEHIND):

                @pl.when(wall_guard(kind))
                def _():
                    move(turn, kind).wait_send()
            else:
                move(turn, kind).wait_send()


def shards(adjoint, velocity, diffusivity, wall_pair):
    tile = (8, 128)
    packets = [
        pltpu.VMEM((8,) + tile, F32),
        pltpu.VMEM((13,) + tile, F32),
        pltpu.VMEM((20,) + tile, F32),
        pltpu.VMEM((FACTORS,) + tile, F32),
        pltpu.VMEM((4, FACTORS) + tile, F32),
    ]
    for shape in ((2, 16), (4,), (4,), (2, 2), (2, 3), (3,)):
        packets += [pltpu.VMEM((ROUNDS,) + shape + tile, F32)] * 2
    operands = (
        adjoint.reshape(512, 128),
        velocity.reshape(1536, 128),
        diffusivity,
        wall_pair,
        jnp.asarray(plane_matrix()),
        jnp.asarray(weight_rows()),
    )
    result = pl.pallas_call(
        kernel,
        out_shape=jax.ShapeDtypeStruct((512, 128), F32),
        in_specs=[pl.BlockSpec(memory_space=pltpu.HBM)] * 6,
        out_specs=pl.BlockSpec(memory_space=pltpu.VMEM),
        scratch_shapes=[
            pltpu.VMEM((1, 128), F32),
            pltpu.SMEM((1, 16), jnp.int32),
            pltpu.VMEM((192, 192), BF16),
            pltpu.VMEM((6,) + tile, F32),
            pltpu.VMEM((512, 128), F32),
            pltpu.VMEM((1536, 128), F32),
            pltpu.VMEM((512, 128), F32),
        ]
        + [pltpu.VMEM((2, 8) + tile, F32)] * 6
        + packets
        + [
            pltpu.SemaphoreType.DMA((8,)),
            pltpu.SemaphoreType.DMA((ROUNDS, KINDS)),
            pltpu.SemaphoreType.DMA((ROUNDS, KINDS)),
            pltpu.SemaphoreType.DMA((4,)),
            pltpu.SemaphoreType.DMA((4,)),
        ],
        compiler_params=pltpu.CompilerParams(
            collective_id=0, has_side_effects=True, vmem_limit_bytes=32 * 1024 * 1024
        ),
        name="plate_step",
    )(*(pltpu.with_memory_space_constraint(array, pltpu.HBM) for array in operands))
    return result.reshape(adjoint.shape)


def solution(mesh):
    placed = (
        P("width", None, None, None, "path"),
        P(None, "width", None, None, None, "path"),
        P("width", "path"),
        P("path", None),
    )
    return jax.shard_map(
        shards,
        mesh=mesh,
        in_specs=placed,
        out_specs=P("width", None, None, None, "path"),
        check_vma=False,
    )
```

```python
import functools

import jax
import jax.numpy as jnp
import numpy as np
from jax import lax
from jax.experimental import pallas as pl
from jax.experimental.pallas import tpu as pltpu
from jax.sharding import PartitionSpec as P

TIME_STEP = 0.004
ROUNDS = 2
INNER_POINTS = (
    -0.8717401485096066,
    -0.5917001814331423,
    -0.2092992179024789,
    0.2092992179024789,
    0.5917001814331423,
    0.8717401485096066,
)
F32 = jnp.float32
BF16 = jnp.bfloat16
WALL, BEHIND, AHEAD, ACROSS, CROSS_BEHIND, CROSS_AHEAD, WALL_AHEAD, WALL_BEHIND, WALL_ACROSS = range(9)
LATER = 9
KINDS = 13
SENT = (WALL_ACROSS, WALL, WALL_AHEAD, WALL_BEHIND, BEHIND, AHEAD, LATER + WALL) + (
    CROSS_BEHIND,
    CROSS_AHEAD,
    ACROSS,
    LATER + BEHIND,
    LATER + AHEAD,
    LATER + ACROSS,
)
LOWER_V, LOWER_ENDS, PATH_ROWS, UPPER_ENDS, UPPER_V, EDGE_V, SIDE_V, WALL_V, ROWS, FOOT_V = 0, 4, 5, 6, 7, 11, 12, 13, 14, 15
FACTORS = 16
SIDE_G, WALL_G, PATH_G, AHEAD_SIDE, AHEAD_WALL, BEHIND_SIDE, BEHIND_WALL, ACROSS_SIDE, ACROSS_WALL, ACROSS_EDGE = range(10)
MIRROR_SIDE, MIRROR_WALL, MIRROR_FOOT = range(10, 13)


def legendre_seven(points):
    before = np.ones(points.shape)
    current = points * 1.0
    for order in range(1, 7):
        after = ((2.0 * order + 1.0) * points * current - order * before) / (order + 1.0)
        before = current
        current = after
    return current


def lobatto_table():
    degree = 7
    points = np.array((-1.0,) + INNER_POINTS + (1.0,))
    values = legendre_seven(points)
    table = np.zeros((degree + 1, degree + 1))
    for i in range(degree + 1):
        for j in range(degree + 1):
            if i != j:
                table[i, j] = values[i] / (values[j] * (points[i] - points[j]))
    table[0, 0] = -degree * (degree + 1) / 4.0
    table[degree, degree] = degree * (degree + 1) / 4.0
    return table


SLOPE = 2.0 * lobatto_table()
ADVECT = SLOPE.copy()
ADVECT[0, 0] += 28.0
ADVECT[7, 7] -= 28.0
SPREAD = SLOPE @ SLOPE
SPREAD[0] += 28.0 * SLOPE[0]
SPREAD[0, 0] -= 112.0
SPREAD[7] -= 28.0 * SLOPE[7]
SPREAD[7, 7] -= 112.0


def plane_matrix():
    eye = np.eye(8)
    full = np.concatenate(
        [np.kron(ADVECT, eye), np.kron(eye, ADVECT), np.kron(SPREAD, eye) + np.kron(eye, SPREAD)]
    )
    high = full.astype(jnp.bfloat16)
    low = (full - high.astype(np.float64)).astype(jnp.bfloat16)
    return np.concatenate([high, high, low], axis=1)


def weight_rows():
    lane = np.arange(128)
    second, width, layer = (lane >> 3) & 1, lane & 7, lane >> 4
    last = np.where(second[None] == 1, 7, 0)[0]
    flat = [SLOPE[last, width], SLOPE[last, layer], SLOPE[0, width], SLOPE[7, width]]
    wide = [np.broadcast_to(row, (8, 128)) for row in flat]
    tall = [np.broadcast_to(SLOPE[k][:, None], (8, 128)) for k in (0, 7)]
    return np.stack(wide + tall).astype(np.float32)


def halves(row):
    even = [float((row[j] + row[7 - j]) / 2) for j in range(4)]
    odd = [float((row[j] - row[7 - j]) / 2) for j in range(4)]
    return even, odd


def weighted(factors, values):
    total = values[0] * factors[0]
    for j in range(1, 4):
        total = total + values[j] * factors[j]
    return total


def end_slopes(line):
    even = [line[j] + line[7 - j] for j in range(4)]
    odd = [line[j] - line[7 - j] for j in range(4)]
    for_even, for_odd = halves(SLOPE[0])
    left, right = weighted(for_even, even), weighted(for_odd, odd)
    return left + right, right - left


def rows(a, b):
    return pl.ds((a * 8 + b) * 8, 8)


def face(a, c):
    return pl.ds(a * 64 + c, 8, stride=8)


def lanes_moved(value, index):
    return jnp.take_along_axis(value, index, axis=1)


def turned(value, shift):
    return pltpu.roll(value, shift % 128, 1) if shift % 128 else value


def kernel(
    adj_hbm,
    vel_hbm,
    kappa_hbm,
    pair_hbm,
    matrix_hbm,
    weight_hbm,
    state,
    kappa_ref,
    pair_ref,
    matrix_ref,
    weight,
    adj,
    vel,
    rate,
    slope_s,
    slope_w,
    slope_z,
    lift_s,
    lift_w,
    lift_z,
    path_v,
    slope_factor,
    pending,
    factor_out,
    factor_in,
    path_out,
    path_in,
    wall_out,
    wall_in,
    side_out,
    side_in,
    cross_out,
    cross_in,
    foot_out,
    foot_in,
    far_out,
    far_in,
    load_sem,
    send_sem,
    recv_sem,
    factor_send,
    factor_recv,
):
    p, q = lax.axis_index("path"), lax.axis_index("width")
    blocks = lax.axis_size("path")
    ahead, behind = lax.rem(p + 1, blocks), lax.rem(p + blocks - 1, blocks)
    mirror, across = blocks - 1 - p, 1 - q
    mirror_before = lax.rem(2 * blocks - 2 - p, blocks)
    mirror_after = lax.rem(blocks - p, blocks)

    barrier = pltpu.get_barrier_semaphore()

    def greet(partner):
        pl.semaphore_signal(barrier, inc=1, device_id=partner, device_id_type=pl.DeviceIdType.MESH)

    greet({"path": mirror, "width": across})
    greet({"path": mirror})

    @pl.when(mirror_before != p)
    def _():
        greet({"path": mirror_before})

    @pl.when(mirror_after != p)
    def _():
        greet({"path": mirror_after})

    greet({"path": behind})
    greet({"path": ahead})
    greet({"path": behind, "width": across})
    greet({"path": ahead, "width": across})
    greet({"width": across})

    loads = [
        pltpu.make_async_copy(adj_hbm, state, load_sem.at[0]),
        pltpu.make_async_copy(vel_hbm, vel, load_sem.at[1]),
        pltpu.make_async_copy(adj_hbm, adj, load_sem.at[2]),
        pltpu.make_async_copy(kappa_hbm, kappa_ref, load_sem.at[4]),
        pltpu.make_async_copy(pair_hbm, pair_ref, load_sem.at[5]),
        pltpu.make_async_copy(matrix_hbm, matrix_ref, load_sem.at[6]),
        pltpu.make_async_copy(weight_hbm, weight, load_sem.at[7]),
    ]
    for load in loads:
        load.start()

    lane = lax.broadcasted_iota(jnp.int32, (8, 128), 1)
    level = lax.broadcasted_iota(jnp.int32, (8, 128), 0)
    width_lane = lane & 7
    first_row = (lane & 8) == 0
    row_lane = (lane >> 3) & 1
    layer = lane >> 4
    edge = 7 * (1 - q)
    edge_sign = (1 - 2 * q).astype(F32)
    other_edge = 7 * q
    side_lanes = lane - width_lane + edge
    other_side_lanes = lane - width_lane + other_edge
    foot_lanes = lane & 15

    def rolled(value, shift):
        return pltpu.roll(value, lax.rem(shift + 256, 128), 1)

    def remote(turn, kind, src, dst, device):
        return pltpu.make_async_remote_copy(
            src_ref=src,
            dst_ref=dst,
            send_sem=send_sem.at[turn, kind],
            recv_sem=recv_sem.at[turn, kind],
            device_id=device,
            device_id_type=pl.DeviceIdType.MESH,
        )

    def move(turn, kind):
        later = kind >= LATER
        direct = kind - LATER if later else kind
        pair, line = pl.ds(2 * later, 2), pl.ds(8 * later, 8)
        if direct == WALL:
            device = {"path": mirror}
            return remote(turn, kind, wall_out.at[turn, pair], wall_in.at[turn, pair], device)
        if direct == BEHIND:
            device = {"path": ahead}
            return remote(turn, kind, path_out.at[turn, 0, line], path_in.at[turn, 0, line], device)
        if direct == AHEAD:
            device = {"path": behind}
            return remote(turn, kind, path_out.at[turn, 1, line], path_in.at[turn, 1, line], device)
        if direct == ACROSS:
            device = {"width": across}
            return remote(turn, kind, side_out.at[turn, pair], side_in.at[turn, pair], device)
        if kind == CROSS_BEHIND:
            device = {"path": ahead, "width": across}
            return remote(turn, kind, cross_out.at[turn, 0], cross_in.at[turn, 0], device)
        if kind == CROSS_AHEAD:
            device = {"path": behind, "width": across}
            return remote(turn, kind, cross_out.at[turn, 1], cross_in.at[turn, 1], device)
        if kind == WALL_AHEAD:
            device = {"path": mirror_before}
            return remote(turn, kind, foot_out.at[turn, 0], foot_in.at[turn, 0], device)
        if kind == WALL_BEHIND:
            device = {"path": mirror_after}
            return remote(turn, kind, foot_out.at[turn, 1], foot_in.at[turn, 1], device)
        device = {"path": mirror, "width": across}
        return remote(turn, kind, far_out.at[turn], far_in.at[turn], device)

    def factor_move(kind):
        first, count, device = {
            WALL: (SIDE_V, 4, {"path": mirror}),
            BEHIND: (PATH_ROWS, 6, {"path": ahead}),
            AHEAD: (LOWER_V, 6, {"path": behind}),
            ACROSS: (EDGE_V, 4, {"width": across}),
        }[kind]
        return pltpu.make_async_remote_copy(
            src_ref=factor_out.at[pl.ds(first, count)],
            dst_ref=factor_in.at[kind, pl.ds(first, count)],
            send_sem=factor_send.at[kind],
            recv_sem=factor_recv.at[kind],
            device_id=device,
            device_id_type=pl.DeviceIdType.MESH,
        )

    def wall_guard(kind):
        return (mirror_before if kind == WALL_AHEAD else mirror_after) != p

    def send(turn, kinds):
        for kind in kinds:
            if kind in (WALL_AHEAD, WALL_BEHIND):
                side = kind - WALL_AHEAD

                @pl.when(wall_guard(kind))
                def _():
                    move(turn, kind).start()

                @pl.when(jnp.logical_not(wall_guard(kind)))
                def _():
                    foot_in[turn, side] = foot_out[turn, side]
            else:
                move(turn, kind).start()

    def receive(turn, kind):
        if kind in (WALL_AHEAD, WALL_BEHIND):

            @pl.when(wall_guard(kind))
            def _():
                move(turn, kind).wait_recv()
        else:
            move(turn, kind).wait_recv()

    def traces_z():
        for a in range(8):
            low, high = end_slopes([state[face(a, c), :] for c in range(8)])
            slope_z[0, a] = low
            slope_z[1, a] = high

    def traces_s():
        for b in range(8):
            low, high = end_slopes([state[rows(a, b), :] for a in range(8)])
            slope_s[0, b] = low
            slope_s[1, b] = high

    def traces_w():
        for a in range(8):
            low, high = end_slopes([state[rows(a, b), :] for b in range(8)])
            slope_w[0, a] = low
            slope_w[1, a] = high

    def traces():
        traces_z()
        traces_s()
        traces_w()

    def by_layer(values):
        packed = values[0]
        for i in range(1, 8):
            packed = jnp.where(layer == i, turned(values[i], 16 * i), packed)
        return packed

    def by_width(values):
        packed = rolled(values[0], 0 - edge)
        for i in range(1, 8):
            packed = jnp.where(width_lane == i, rolled(values[i], i - edge), packed)
        return packed

    def pack_wall(turn, second):
        wall_out[turn, 2 * second] = by_layer([state[face(a, 0), :] for a in range(8)])
        wall_out[turn, 2 * second + 1] = by_layer([slope_z[0, a] for a in range(8)])

    def pack_side(turn, second):
        side_out[turn, 2 * second] = by_width([state[rows(a, edge), :] for a in range(8)])
        side_out[turn, 2 * second + 1] = by_width([slope_w[1 - q, a] for a in range(8)])

    def pack_path(turn, second):
        for b in range(8):
            path_out[turn, 0, 8 * second + b] = jnp.where(
                first_row, turned(slope_s[1, b], 120), state[rows(7, b), :]
            )
            path_out[turn, 1, 8 * second + b] = jnp.where(
                first_row, state[rows(0, b), :], turned(slope_s[0, b], 8)
            )

    def pack_far(turn):
        far_out[turn, 0] = wall_out[turn, 0]
        far_out[turn, 1] = wall_out[turn, 1]
        far_out[turn, 2] = jnp.where(layer == 0, side_out[turn, 0], turned(side_out[turn, 1], 16))

    def pack_foot(turn):
        for side in range(2):
            foot_out[turn, side, 0] = wall_out[turn, 0]
            foot_out[turn, side, 1] = wall_out[turn, 1]
            foot_out[turn, side, 2] = by_layer([path_out[turn, side, b] for b in range(8)])

    def pack_cross(turn):
        value, slope = side_out[turn, 0], side_out[turn, 1]
        for side in range(2):
            cross_out[turn, side, 0] = by_width([path_out[turn, side, b] for b in range(8)])
        cross_out[turn, 0, 1] = jnp.where(first_row, turned(slope, 120), value)
        cross_out[turn, 1, 1] = jnp.where(first_row, value, turned(slope, 8))

    def prepare(kappa, wall_index):
        base = kappa * 112.0
        for i in range(8):
            lift_s[0, i] = base - 28.0 * vel[rows(0, i), :]
            lift_s[1, i] = base + 28.0 * vel[rows(7, i), :]
            lift_w[0, i] = base - 28.0 * vel[rows(8 + i, 0), :]
            lift_w[1, i] = base + 28.0 * vel[rows(8 + i, 7), :]
            lift_z[0, i] = base - 28.0 * vel[face(16 + i, 0), :]
            lift_z[1, i] = base + 28.0 * vel[face(16 + i, 7), :]
        slope = kappa * 28.0
        inside = jnp.where(first_row, p, blocks - 1 - p) > 0
        path_g = jnp.where(inside, jnp.where(first_row, 0.0 - slope, slope), 0.0)
        for b in range(8):
            lift = jnp.where(first_row, lift_s[0, b], lift_s[1, b])
            path_v[b] = jnp.where(inside, lift, 0.0)
        on_path = [path_v[b] for b in range(8)]
        for k in range(4):
            one, two = on_path[2 * k], on_path[2 * k + 1]
            factor_out[LOWER_V + k] = jnp.where(first_row, one, turned(two, 8))
            factor_out[UPPER_V + k] = jnp.where(first_row, turned(two, 120), one)
        side = by_width([lift_w[1 - q, a] for a in range(8)])
        wall = by_layer([lift_z[0, a] for a in range(8)])
        told = jnp.where(level == 0, wall_index.astype(F32), jnp.where(level == 1, path_g, slope))
        factor_out[LOWER_ENDS] = jnp.where(first_row, side, turned(wall, 8))
        factor_out[UPPER_ENDS] = jnp.where(first_row, turned(wall, 120), side)
        factor_out[PATH_ROWS] = told
        factor_out[SIDE_V] = side
        factor_out[WALL_V] = wall
        factor_out[ROWS] = told
        factor_out[EDGE_V] = by_width(on_path)
        factor_out[FOOT_V] = by_layer(on_path)
        slope_factor[SIDE_G] = lanes_moved(slope * edge_sign, side_lanes)
        slope_factor[WALL_G] = lanes_moved(slope, foot_lanes)
        slope_factor[PATH_G] = path_g

    def told_row(kind, at, row):
        return jnp.broadcast_to(factor_in[kind, at, row : row + 1], (8, 128))

    def learn():
        for kind, at, side in (
            (AHEAD, PATH_ROWS, AHEAD_SIDE),
            (BEHIND, PATH_ROWS, BEHIND_SIDE),
            (WALL, ROWS, MIRROR_SIDE),
        ):
            slope = told_row(kind, at, 2)
            slope_factor[side] = lanes_moved(slope * edge_sign, side_lanes)
            slope_factor[side + 1] = lanes_moved(slope, foot_lanes)
        slope = told_row(ACROSS, ROWS, 2)
        slope_factor[ACROSS_SIDE] = 0.0 - lanes_moved(slope * edge_sign, other_side_lanes)
        slope_factor[ACROSS_WALL] = lanes_moved(slope, foot_lanes)
        slope_factor[ACROSS_EDGE] = lanes_moved(told_row(ACROSS, ROWS, 1), other_side_lanes)
        slope_factor[MIRROR_FOOT] = lanes_moved(told_row(WALL, ROWS, 1), foot_lanes)

    def local_rates(step, kappa):
        for b in range(8):
            line = [state[rows(a, b), :] for a in range(8)]
            even = [line[j] + line[7 - j] for j in range(4)]
            odd = [line[j] - line[7 - j] for j in range(4)]
            for i in range(4):
                for_even, for_odd = halves(ADVECT[i])
                left, right = weighted(for_even, even), weighted(for_odd, odd)
                for_even, for_odd = halves(SPREAD[i])
                inner, outer = weighted(for_even, even), weighted(for_odd, odd)
                near = vel[rows(i, b), :] * (left + right) + kappa * (inner + outer)
                far = vel[rows(7 - i, b), :] * (right - left) + kappa * (inner - outer)
                if i == 0:
                    lower = lift_s[0, b] * pltpu.roll(line[7], 8, 1) - (kappa * 28.0) * pltpu.roll(
                        slope_s[1, b], 8, 1
                    )
                    upper = lift_s[1, b] * pltpu.roll(line[0], 120, 1) + (
                        kappa * 28.0
                    ) * pltpu.roll(slope_s[0, b], 120, 1)
                    near = near + jnp.where(first_row, 0.0, lower)
                    far = far + jnp.where(first_row, upper, 0.0)
                rate[rows(i, b), :] = near
                rate[rows(7 - i, b), :] = far
        for pair in range(4):
            both = range(2 * pair, 2 * pair + 2)
            planes = [state[pl.ds(64 * a, 64), :] for a in both]
            plane = jnp.concatenate(planes, axis=1)
            high = plane.astype(BF16)
            low = (plane - high.astype(F32)).astype(BF16)
            stacked = jnp.concatenate([high, low, high], axis=0)
            product = jnp.dot(matrix_ref[...], stacked, preferred_element_type=F32)
            for k, a in enumerate(both):
                block = product[:, 128 * k : 128 * (k + 1)]
                bottom, top = state[face(a, 0), :], state[face(a, 7), :]
                first, last = state[rows(a, 0), :], state[rows(a, 7), :]
                for b in range(8):
                    at = slice(8 * b, 8 * b + 8)
                    value = (
                        rate[rows(a, b), :]
                        + vel[rows(8 + a, b), :] * block[0:64][at]
                        + vel[rows(16 + a, b), :] * block[64:128][at]
                        + kappa * block[128:192][at]
                    )
                    if b == 0:
                        lower = lift_w[0, a] * pltpu.roll(last, 1, 1) - (
                            kappa * 28.0
                        ) * pltpu.roll(slope_w[1, a], 1, 1)
                        value = value + jnp.where(width_lane == 0, 0.0, lower)
                    if b == 7:
                        upper = lift_w[1, a] * pltpu.roll(first, 127, 1) + (
                            kappa * 28.0
                        ) * pltpu.roll(slope_w[0, a], 127, 1)
                        value = value + jnp.where(width_lane == 7, 0.0, upper)
                    state[rows(a, b), :] = adj[rows(a, b), :] + step * value
                lower = lift_z[0, a] * pltpu.roll(top, 16, 1) - (kappa * 28.0) * pltpu.roll(
                    slope_z[1, a], 16, 1
                )
                upper = lift_z[1, a] * pltpu.roll(bottom, 112, 1) + (kappa * 28.0) * pltpu.roll(
                    slope_z[0, a], 112, 1
                )
                state[face(a, 0), :] += step * jnp.where(layer == 0, 0.0, lower)
                state[face(a, 7), :] += step * jnp.where(layer == 7, 0.0, upper)

    def far_rates(turn, second, step, kappa, wall_index):
        at = 2 * second
        change = step * (
            factor_out[SIDE_V] * side_in[turn, at] + slope_factor[SIDE_G] * side_in[turn, at + 1]
        )
        for a in range(8):
            moved = rolled(change, edge - a)
            state[rows(a, edge), :] += jnp.where(width_lane == edge, moved, 0.0)
        path_g = slope_factor[PATH_G]
        lower_lanes = first_row & (p > 0)
        upper_lanes = jnp.logical_not(first_row) & (p < blocks - 1)
        for b in range(8):
            packet = path_in[turn, 0, 8 * second + b]
            change = path_v[b] * pltpu.roll(packet, 120, 1) + path_g * packet
            state[rows(0, b), :] += jnp.where(lower_lanes, step * change, 0.0)
            packet = path_in[turn, 1, 8 * second + b]
            change = path_v[b] * pltpu.roll(packet, 8, 1) + path_g * packet
            state[rows(7, b), :] += jnp.where(upper_lanes, step * change, 0.0)
        value = lanes_moved(wall_in[turn, at], wall_index)
        slope = lanes_moved(wall_in[turn, at + 1], wall_index)
        change = step * (factor_out[WALL_V] * value + slope_factor[WALL_G] * slope)
        for a in range(8):
            moved = turned(change, 0 - 16 * a)
            state[face(a, 0), :] += jnp.where(layer == 0, moved, 0.0)

    def lane_sum(value):
        for apart in (1, 2, 4):
            value = value + turned(value, 0 - apart)
        return value

    def layer_sum(value):
        for apart in (16, 32, 64):
            value = value + turned(value, apart)
        return value

    def level_sum(value):
        return jnp.broadcast_to(jnp.sum(value, axis=0, keepdims=True), (8, 128))

    def reflect(turn, step):
        low, high = float(SLOPE[0, 0]), float(SLOPE[7, 7])
        ahead_g, behind_g = told_row(AHEAD, PATH_ROWS, 1), told_row(BEHIND, PATH_ROWS, 1)
        for b in range(8):
            packet = path_out[turn, 0, b]
            lift = factor_in[AHEAD, LOWER_V + b // 2]
            lift = turned(lift, 120) if b % 2 else lift
            change = lift * turned(packet, 120) + ahead_g * packet
            change = step * jnp.where(first_row, change, low * turned(change, 8))
            pending[b] = change
            packet = path_out[turn, 1, b]
            lift = factor_in[BEHIND, UPPER_V + b // 2]
            lift = turned(lift, 8) if b % 2 else lift
            change = lift * turned(packet, 8) + behind_g * packet
            change = step * jnp.where(first_row, high * turned(change, 120), change)
            pending[8 + b] = change
        change = step * (
            factor_in[ACROSS, SIDE_V] * side_out[turn, 0] + slope_factor[ACROSS_SIDE] * side_out[turn, 1]
        )
        pending[16] = change
        pending[17] = change * (edge_sign * low)
        index = told_row(WALL, ROWS, 0).astype(jnp.int32)
        change = step * (
            factor_in[WALL, WALL_V] * lanes_moved(wall_out[turn, 0], index)
            + slope_factor[MIRROR_WALL] * lanes_moved(wall_out[turn, 1], index)
        )
        pending[18] = change
        pending[19] = change * low

    def complete(turn, step, wall_index):
        for b in range(8):
            path_in[turn, 1, 8 + b] += pending[b]
            path_in[turn, 0, 8 + b] += pending[8 + b]
        packet = cross_in[turn, 1, 1]
        lower = factor_in[AHEAD, LOWER_ENDS] * packet + slope_factor[AHEAD_SIDE] * turned(packet, 120)
        packet = cross_in[turn, 0, 1]
        upper = factor_in[BEHIND, UPPER_ENDS] * packet + slope_factor[BEHIND_SIDE] * turned(packet, 8)
        change = step * jnp.where(first_row, lower, upper)
        slope = lane_sum(change * weight[0])
        lower = jnp.where(first_row, rolled(change, edge), rolled(slope, edge + 8))
        upper = jnp.where(first_row, rolled(slope, edge - 8), rolled(change, edge - 7))
        path_in[turn, 1, 8 + edge] += jnp.where(width_lane == edge, lower, 0.0)
        path_in[turn, 0, 8 + edge] += jnp.where(width_lane == edge, upper, 0.0)
        index = told_row(AHEAD, PATH_ROWS, 0).astype(jnp.int32)
        lower = turned(factor_in[AHEAD, LOWER_ENDS], 120) * lanes_moved(foot_in[turn, 0, 0], index) + slope_factor[
            AHEAD_WALL
        ] * lanes_moved(foot_in[turn, 0, 1], index)
        index = told_row(BEHIND, PATH_ROWS, 0).astype(jnp.int32)
        upper = turned(factor_in[BEHIND, UPPER_ENDS], 8) * lanes_moved(foot_in[turn, 1, 0], index) + slope_factor[
            BEHIND_WALL
        ] * lanes_moved(foot_in[turn, 1, 1], index)
        change = step * jnp.where(first_row, lower, upper)
        slope = layer_sum(change * weight[1])
        lower = jnp.where(first_row, change, turned(slope, 8))
        upper = jnp.where(first_row, turned(slope, 120), turned(change, 16))
        lower = jnp.where(layer == 0, lower, 0.0)
        upper = jnp.where(layer == 0, upper, 0.0)
        for b in range(8):
            path_in[turn, 1, 8 + b, 0:1] += lower[b : b + 1]
            path_in[turn, 0, 8 + b, 0:1] += upper[b : b + 1]
        value_side, slope_side = pending[16], pending[17]
        packet = cross_in[turn, 0, 0]
        lower = factor_in[ACROSS, EDGE_V] * turned(packet, 120) + slope_factor[ACROSS_EDGE] * packet
        packet = cross_in[turn, 1, 0]
        upper = factor_in[ACROSS, EDGE_V] * turned(packet, 8) + slope_factor[ACROSS_EDGE] * packet
        change = step * jnp.where(first_row, lower, upper)
        slope = lane_sum(change * weight[2 + q])
        at_first = first_row & (width_lane == 0)
        at_last = jnp.logical_not(first_row) & (width_lane == 7)
        value_side += jnp.where(at_first, rolled(change, 0 - other_edge), 0.0)
        value_side += jnp.where(at_last, rolled(change, 7 - other_edge), 0.0)
        slope_side += jnp.where(at_first, slope, 0.0) + jnp.where(at_last, turned(slope, 7), 0.0)
        change = step * (
            factor_in[ACROSS, WALL_V] * lanes_moved(far_in[turn, 0], wall_index)
            + slope_factor[ACROSS_WALL] * lanes_moved(far_in[turn, 1], wall_index)
        )
        index = 16 * width_lane + 8 * row_lane + other_edge
        value = lanes_moved(level_sum(jnp.where(level == other_edge, change, 0.0)), index)
        slope = lanes_moved(level_sum(change * weight[4 + q]), index)
        foot = (level == 0) & (layer == 0)
        side_in[turn, 2] += value_side + jnp.where(foot, value, 0.0)
        side_in[turn, 3] += slope_side + jnp.where(foot, slope, 0.0)
        value_wall, slope_wall = pending[18], pending[19]
        packet = foot_in[turn, 0, 2]
        lower = factor_in[WALL, FOOT_V] * turned(packet, 120) + slope_factor[MIRROR_FOOT] * packet
        packet = foot_in[turn, 1, 2]
        upper = factor_in[WALL, FOOT_V] * turned(packet, 8) + slope_factor[MIRROR_FOOT] * packet
        change = step * jnp.where(first_row, lower, upper)
        index = 16 * level + (lane & 15)
        value = lanes_moved(level_sum(jnp.where(level == 0, change, 0.0)), index)
        slope = lanes_moved(level_sum(change * weight[4]), index)
        ends = layer == 7 * row_lane
        value_wall += jnp.where(ends, value, 0.0)
        slope_wall += jnp.where(ends, slope, 0.0)
        packet = far_in[turn, 2]
        change = step * (
            factor_in[WALL, SIDE_V] * packet + slope_factor[MIRROR_SIDE] * turned(packet, 112)
        )
        index = 8 * row_lane + layer
        value = lanes_moved(level_sum(jnp.where(level == 0, change, 0.0)), index)
        slope = lanes_moved(level_sum(change * weight[4]), index)
        corner = (level == edge) & (width_lane == edge)
        wall_in[turn, 2] += value_wall + jnp.where(corner, value, 0.0)
        wall_in[turn, 3] += slope_wall + jnp.where(corner, slope, 0.0)

    for load in loads:
        load.wait()
    kappa = jnp.broadcast_to(kappa_ref[...], (8, 128))
    wall_index = jnp.zeros((8, 128), jnp.int32)
    for j in range(16):
        wall_index = jnp.where((lane & 15) == j, pair_ref[0, j], wall_index)
    wall_index = wall_index + 16 * (7 - layer)
    prepare(kappa, wall_index)

    steps = [TIME_STEP / 4.0, TIME_STEP / 3.0, TIME_STEP / 2.0, TIME_STEP]
    for turn in range(ROUNDS):
        step, next_step = steps[2 * turn], steps[2 * turn + 1]

        def begin(*kinds):
            if turn:
                send(turn, kinds)

        traces_z()
        pack_wall(turn, 0)
        traces_w()
        pack_side(turn, 0)
        pack_far(turn)
        begin(WALL_ACROSS, WALL)
        traces_s()
        pack_path(turn, 0)
        pack_foot(turn)
        begin(WALL_AHEAD, WALL_BEHIND, BEHIND, AHEAD)
        pack_cross(turn)
        begin(CROSS_BEHIND, CROSS_AHEAD, ACROSS)
        local_rates(step, kappa)
        traces_z()
        pack_wall(turn, 1)
        begin(LATER + WALL)
        traces_s()
        pack_path(turn, 1)
        begin(LATER + BEHIND, LATER + AHEAD)
        traces_w()
        pack_side(turn, 1)
        begin(LATER + ACROSS)
        if turn:
            reflect(turn, step)
        else:
            meet = (mirror_before != p).astype(jnp.int32) + (mirror_after != p).astype(jnp.int32)
            pl.semaphore_wait(barrier, 7 + meet)
            send(turn, SENT)
            for kind in (WALL, BEHIND, AHEAD, ACROSS):
                factor_move(kind).start()
        for kind in (ACROSS, BEHIND, AHEAD, WALL):
            receive(turn, kind)
        far_rates(turn, 0, step, kappa, wall_index)
        traces()
        local_rates(next_step, kappa)
        if turn == 0:
            for kind in (WALL, BEHIND, AHEAD, ACROSS):
                factor_move(kind).wait_recv()
            learn()
            reflect(turn, step)
        for kind in SENT:
            if kind not in (ACROSS, BEHIND, AHEAD, WALL):
                receive(turn, kind)
        complete(turn, step, wall_index)
        far_rates(turn, 1, next_step, kappa, wall_index)
    for kind in (WALL, BEHIND, AHEAD, ACROSS):
        factor_move(kind).wait_send()
    for turn in range(ROUNDS):
        for kind in range(KINDS):
            if kind in (WALL_AHEAD, WALL_BEHIND):

                @pl.when(wall_guard(kind))
                def _():
                    move(turn, kind).wait_send()
            else:
                move(turn, kind).wait_send()


def shards(adjoint, velocity, diffusivity, wall_pair):
    tile = (8, 128)
    packets = [
        pltpu.VMEM((8,) + tile, F32),
        pltpu.VMEM((13,) + tile, F32),
        pltpu.VMEM((20,) + tile, F32),
        pltpu.VMEM((FACTORS,) + tile, F32),
        pltpu.VMEM((4, FACTORS) + tile, F32),
    ]
    for shape in ((2, 16), (4,), (4,), (2, 2), (2, 3), (3,)):
        packets += [pltpu.VMEM((ROUNDS,) + shape + tile, F32)] * 2
    operands = (
        adjoint.reshape(512, 128),
        velocity.reshape(1536, 128),
        diffusivity,
        wall_pair,
        jnp.asarray(plane_matrix()),
        jnp.asarray(weight_rows()),
    )
    result = pl.pallas_call(
        kernel,
        out_shape=jax.ShapeDtypeStruct((512, 128), F32),
        in_specs=[pl.BlockSpec(memory_space=pltpu.HBM)] * 6,
        out_specs=pl.BlockSpec(memory_space=pltpu.VMEM),
        scratch_shapes=[
            pltpu.VMEM((1, 128), F32),
            pltpu.SMEM((1, 16), jnp.int32),
            pltpu.VMEM((192, 192), BF16),
            pltpu.VMEM((6,) + tile, F32),
            pltpu.VMEM((512, 128), F32),
            pltpu.VMEM((1536, 128), F32),
            pltpu.VMEM((512, 128), F32),
        ]
        + [pltpu.VMEM((2, 8) + tile, F32)] * 6
        + packets
        + [
            pltpu.SemaphoreType.DMA((8,)),
            pltpu.SemaphoreType.DMA((ROUNDS, KINDS)),
            pltpu.SemaphoreType.DMA((ROUNDS, KINDS)),
            pltpu.SemaphoreType.DMA((4,)),
            pltpu.SemaphoreType.DMA((4,)),
        ],
        compiler_params=pltpu.CompilerParams(
            collective_id=0, has_side_effects=True, vmem_limit_bytes=32 * 1024 * 1024
        ),
        name="plate_step",
    )(*(pltpu.with_memory_space_constraint(array, pltpu.HBM) for array in operands))
    return result.reshape(adjoint.shape)


def solution(mesh):
    placed = (
        P("width", None, None, None, "path"),
        P(None, "width", None, None, None, "path"),
        P("width", "path"),
        P("path", None),
    )
    return jax.shard_map(
        shards,
        mesh=mesh,
        in_specs=placed,
        out_specs=P("width", None, None, None, "path"),
        check_vma=False,
    )
```
